32 devices in a mesh: wave: 8 (over z, x), hemi: 2 (over y), fld: 2 (over core).
Axes of the slice: x: 2, y: 2, z: 4, core: 2. Of those that a mesh axis runs over, the one named last changes fastest.
Arguments:
- grid: float32 [2, 4, 32, 5248], P(None, None, ('wave', 'hemi', 'fld')), may hold values from -6 to 6
- lon_count: int32 [32], P(('wave', 'hemi', 'fld')), may hold values from 20 to 5136, as said below
- wave_order: int32 [768], replicated, may hold values from 0 to 767, as said below
- legendre: bfloat16 [768, 2, 2, 8, 384], P(('wave', 'fld'), 'hemi'), may hold values from -1.5 to 1.5
- stiffness: float32 [2], replicated, may hold values from 0.5 to 4
Outputs:
- smooth: float32 [2, 4, 32, 5248], P(None, None, ('wave', 'hemi', 'fld'))
- bracket: float32 [4, 32, 5248], P(None, ('wave', 'hemi', 'fld'))
The draws below stay inside these ranges and needn't reach their ends.
Inputs may be any that keep to these rules, and one draw needn't show every extreme that they name: `lon_count`: cycle r has 20 + 4 t longitudes, t its cycle number counted from the pole; cycles 2 i and 2 i + 1 are mirror partners with equal counts, and different pairs have different cycle numbers. `wave_order`: each wavenumber appears once.
All inputs are finite; a program needn't handle non-finite values.
Results may differ from the reference program's by a relative error of at most 0.0052.
Values may be sent and summed in bfloat16 or wider, within the bound.
A program may use at most 64 MiB of HBM per device.

```python
import math
import jax
import jax.numpy as jnp
from jax import lax

M = 768
CYCLE_MAX = 1280
FIELDS = 2
LEVELS = 4
K = 384
LONP = 5248
BANDS = 8
BAND_PAIRS = 2
PAIRS = 16
CYCLES = 32
SLOT_DEV = 48


def draw_lon_count(key, part):
    middle = jax.random.permutation(key, CYCLE_MAX - 2) + 1
    chosen = jnp.concatenate([jnp.array([0, CYCLE_MAX - 1], dtype=jnp.int32), middle[:PAIRS - 2].astype(jnp.int32)])
    numbers = jax.random.permutation(jax.random.fold_in(key, 7), chosen)
    paired = jnp.stack([numbers, numbers], axis=1).reshape(CYCLES)
    return (20 + 4 * paired).astype(jnp.int32)


def draw_wave_order(key, part):
    groups = M // SLOT_DEV
    blocks = jax.random.permutation(key, groups).astype(jnp.int32)
    inner_order = jax.random.permutation(jax.random.fold_in(key, 3), SLOT_DEV).astype(jnp.int32)
    return (blocks[:, None] * SLOT_DEV + inner_order[None, :]).reshape(M).astype(jnp.int32)


def block_levels(own_key, shape, shards, least, largest):
    loudness = 1.0
    for axis_at, shards_of in shards:
        steps = jax.random.uniform(jax.random.fold_in(jax.random.fold_in(own_key, 6), axis_at), (shards_of,), jnp.float32, least / len(shards), largest / len(shards))
        loudness = loudness * jnp.repeat(jnp.exp(steps), shape[axis_at] // shards_of).reshape((-1,) + (1,) * (len(shape) - 1 - axis_at))
    return loudness


def scatter_about(rng, shape, spread, bound, cuts=(), kind=jnp.bfloat16):
    level = block_levels(rng, shape, cuts, -0.22, 0.18) if cuts else 1.0
    entries = jax.random.normal(rng, shape, jnp.float32) * spread * level
    return jnp.minimum(jnp.maximum(entries, -bound), bound).astype(kind)


def setup_inputs(seed: int = 0) -> dict:
    arg_keys = jax.random.split(jax.random.key(seed), 6)
    return {
        "grid": scatter_about(arg_keys[0], (FIELDS, LEVELS, CYCLES, LONP), 1.0, 6.0, ((2, 32),), jnp.float32),
        "lon_count": draw_lon_count(jax.random.fold_in(arg_keys[5], 71), 0),
        "wave_order": draw_wave_order(jax.random.fold_in(arg_keys[5], 71), 0),
        "legendre": scatter_about(arg_keys[3], (M, BAND_PAIRS, 2, BANDS, K), PAIRS ** -0.5, 1.5, ((0, 16), (1, 2))),
        "stiffness": jnp.clip(jnp.exp(jax.random.uniform(arg_keys[4], (FIELDS,), jnp.float32, math.log(0.5), math.log(4.0))), 0.5, 4.0),
    }


exact_mode = lax.Precision.HIGHEST

def cycle_tables(cycle_length):
    wavenumbers = jnp.arange(M, dtype=jnp.int32)
    longitudes = jnp.arange(LONP, dtype=jnp.int32)
    phases = wavenumbers[:, None] * longitudes[None, :] % cycle_length
    angles = 2.0 * jnp.pi / cycle_length.astype(jnp.float32) * phases.astype(jnp.float32)
    cycle_scale = 1.0 / jnp.sqrt(cycle_length.astype(jnp.float32))
    return (jnp.cos(angles), jnp.sin(angles), cycle_scale)

def reference(grid, lon_count, wave_order, legendre, stiffness):
    rows_per = FIELDS * LEVELS
    wavenumbers = jnp.arange(M, dtype=jnp.int32)
    longitudes = jnp.arange(LONP, dtype=jnp.int32)
    cycle_rows = jnp.transpose(grid, (2, 0, 1, 3)).reshape(CYCLES, rows_per, LONP)

    def forward(packed):
        rows_here, cycle_length = packed
        cosine, sine_table, cycle_scale = cycle_tables(cycle_length)
        rows_here = jnp.where(longitudes[None, :] < cycle_length, rows_here, 0.0)
        real_part = jnp.dot(rows_here, cosine.T, precision=exact_mode) * cycle_scale
        imag_part = -jnp.dot(rows_here, sine_table.T, precision=exact_mode) * cycle_scale
        both_parts = jnp.concatenate([real_part, imag_part], axis=0)
        return jnp.where((2 * wavenumbers < cycle_length)[None, :], both_parts, 0.0)
    fourier = lax.map(forward, (cycle_rows, lon_count))
    slotted = fourier[:, :, wave_order]
    north_cycles = slotted[0::2]
    south_cycles = slotted[1::2]
    even_part = (north_cycles + south_cycles).astype(jnp.bfloat16)
    odd_part = (north_cycles - south_cycles).astype(jnp.bfloat16)
    parities = jnp.moveaxis(jnp.stack([even_part, odd_part], axis=1), 3, 0)
    chan_stiff = jnp.tile(jnp.repeat(stiffness, LEVELS), 2)
    degree_steps = 2 * jnp.arange(K, dtype=jnp.int32)

    def legendre_slot(packed):
        weights, columns, slot_wave = packed
        matrices = jnp.transpose(weights, (1, 3, 2, 0)).reshape(2, K, PAIRS)
        results = []
        for parity in range(2):
            spectral = jnp.dot(matrices[parity], columns[:, parity], preferred_element_type=jnp.float32)
            degrees = slot_wave + degree_steps + parity
            spectral = jnp.where((degrees < M)[:, None], spectral, 0.0)
            degree_float = degrees.astype(jnp.float32)
            degree_ratio = degree_float * (degree_float + 1.0) / (M * (M - 1))
            damped = (spectral / (1.0 + chan_stiff[None, :] * degree_ratio[:, None])).astype(jnp.bfloat16)
            results.append(jnp.dot(matrices[parity].T, damped, preferred_element_type=jnp.float32))
        return jnp.stack(results)
    returned = lax.map(legendre_slot, (legendre, parities, wave_order))
    north_vals = returned[:, 0] + returned[:, 1]
    south_vals = returned[:, 0] - returned[:, 1]
    cycle_slots = jnp.stack([north_vals, south_vals], axis=2).reshape(M, CYCLES, 2 * rows_per)
    spectra = jnp.zeros((CYCLES, 2 * rows_per, M), jnp.float32).at[:, :, wave_order].set(jnp.transpose(cycle_slots, (1, 2, 0)))

    def inverse(packed):
        coefs, cycle_length = packed
        cosine, sine_table, cycle_scale = cycle_tables(cycle_length)
        weight_wave = jnp.where(wavenumbers == 0, 1.0, 2.0) * jnp.where(2 * wavenumbers < cycle_length, cycle_scale, 0.0)
        real_part = coefs[:rows_per] * weight_wave
        imag_part = coefs[rows_per:] * weight_wave
        wave_ratio = wavenumbers.astype(jnp.float32) / M
        values = jnp.dot(real_part, cosine, precision=exact_mode) - jnp.dot(imag_part, sine_table, precision=exact_mode)
        slopes = -jnp.dot(imag_part * wave_ratio, cosine, precision=exact_mode) - jnp.dot(real_part * wave_ratio, sine_table, precision=exact_mode)
        live_points = (longitudes < cycle_length)[None, :]
        return (jnp.where(live_points, values, 0.0), jnp.where(live_points, slopes, 0.0))
    smooth_cycles, slope_cycles = lax.map(inverse, (spectra, lon_count))
    smooth = jnp.transpose(smooth_cycles.reshape(CYCLES, FIELDS, LEVELS, LONP), (1, 2, 0, 3))
    slope = jnp.transpose(slope_cycles.reshape(CYCLES, FIELDS, LEVELS, LONP), (1, 2, 0, 3))
    bracket = smooth[0] * slope[1] - smooth[1] * slope[0]
    return (smooth, bracket)
```

```python
import functools
import math

import jax
import jax.numpy as jnp
from jax import lax
from jax.experimental import pallas as pl
from jax.experimental.pallas import tpu as pltpu
from jax.sharding import PartitionSpec as P

LANES = 128
SUB = 32
F32 = jnp.float32
BF16 = jnp.bfloat16
NN = (((1,), (0,)), ((), ()))
NT = (((1,), (1,)), ((), ()))
MESH = pl.DeviceIdType.MESH


def round_up(value, step):
    return -(-value // step) * step


def mxu(a, b, dims=NN):
    return lax.dot_general(a, b, dims, preferred_element_type=F32)


def split(x):
    high = x.astype(BF16)
    return high, (x - high.astype(F32)).astype(BF16)


def iota(shape, axis):
    return lax.broadcasted_iota(jnp.int32, shape, axis)


def sine_turn(x):
    y = x * x
    total = jnp.full_like(y, 0.0)
    for power in (13, 11, 9, 7, 5, 3, 1):
        sign = 1.0 if power % 4 == 1 else -1.0
        total = total * y + sign * (2.0 * math.pi) ** power / math.factorial(power)
    return total * x


def turn_tables(steps, period):
    inverse = 1.0 / period
    rest = steps - jnp.floor(steps * inverse) * period
    turn = rest * inverse
    turn = turn - jnp.floor(turn + 0.5)
    shifted = turn - 0.25
    shifted = jnp.where(shifted < -0.5, shifted + 1.0, shifted)
    return sine_turn(0.25 - jnp.abs(turn)), sine_turn(0.25 - jnp.abs(shifted))


def length_of(lon_ref):
    count = lon_ref[0]
    return count, lax.shift_right_logical(count, 2), jnp.full((1, 1), count.astype(F32), F32)


def fold_tables(n_float, quarter):
    steps = iota((8, quarter), 0) * iota((8, quarter), 1)
    return turn_tables(steps.astype(F32), n_float)


def roll_lanes(x, amount):
    amount = amount % x.shape[1]
    return x if amount == 0 else pltpu.roll(x, amount, 1)


def pack_message(block0, block1, place):
    lane = iota(block0.shape, 1)
    rows = jnp.where(
        lane % (2 * SUB) < SUB, roll_lanes(block0, -SUB * place), roll_lanes(block1, SUB - SUB * place)
    )
    return jnp.where(lane[0:4] < 2 * SUB, rows[0:4], roll_lanes(rows[4:8], 2 * SUB))


def unpack_message(message):
    return jnp.concatenate([message, roll_lanes(message, 2 * SUB)], axis=0)


def spaced_slots(row, owners):
    slots = row.shape[1] // owners
    per = LANES // SUB
    lane = iota((1, LANES), 1)
    blocks = []
    for v in range(owners // per):
        block = jnp.full((1, LANES), -1, jnp.int32)
        for place in range(per):
            start = (v * per + place) * slots
            low, high = start // LANES, (start + slots - 1) // LANES
            for source in range(low, high + 1):
                piece = roll_lanes(
                    row[:, source * LANES : (source + 1) * LANES],
                    place * SUB - (start - source * LANES),
                )
                at = lane - place * SUB
                from_lane = at + start - source * LANES
                block = jnp.where(
                    (at >= 0) & (at < slots) & (from_lane >= 0) & (from_lane < LANES), piece, block
                )
        blocks.append(block)
    return jnp.concatenate(blocks, axis=1)


def shift_left(x, amount, most):
    width = x.shape[1]
    amounts = jnp.full(x.shape, amount, jnp.int32)
    for bit in reversed(range(most.bit_length())):
        step = 1 << bit
        if step % LANES == 0:
            moved = jnp.concatenate([x[:, step:], x[:, :step]], axis=1)
        else:
            moved = pltpu.roll(x, width - step, 1)
        x = jnp.where((amounts & step) != 0, moved, x)
    return x


def lane_gather(tile, index):
    return jnp.take_along_axis(tile, index, axis=1, mode="promise_in_bounds")


def window_at(tiles, start, most, count):
    whole = lax.shift_right_logical(start, 7)
    bits = (most // LANES).bit_length()
    for bit in reversed(range(bits)):
        step = 1 << bit
        keep = count + step
        hit = jnp.full(tiles[0].shape, whole, jnp.int32) & step != 0
        tiles = [
            jnp.where(hit, tiles[i + step], tiles[i]) if i + step < len(tiles) else tiles[i]
            for i in range(min(keep, len(tiles)))
        ]
    lane = iota(tiles[0].shape, 1) + jnp.full(tiles[0].shape, start & (LANES - 1), jnp.int32)
    index = lane & (LANES - 1)
    turned = [lane_gather(tile, index) for tile in tiles[: count + 1]]
    inside = lane < LANES
    return jnp.concatenate(
        [jnp.where(inside, turned[i], turned[i + 1]) for i in range(count)], axis=1
    )


def build_tables(lon_ref, grid_ref, wave_ref, table_ref, order_ref, rows, pieces, low_table):
    fields, levels, _, lon_slots = grid_ref.shape
    quarter = table_ref.shape[1]
    waves4 = table_ref.shape[0] // 2
    _, fourth, _ = length_of(lon_ref)
    fourth_float = jnp.full((1, 1), fourth.astype(F32), F32)
    pieces[0] = rows[:, :quarter]
    tiles = [rows[:, i * LANES : (i + 1) * LANES] for i in range(rows.shape[1] // LANES)]
    for a in range(1, 4):
        pieces[a] = window_at(tiles, fourth * a, a * (lon_slots // 4), quarter // LANES)
    c_steps = iota((waves4, LANES), 0)
    lane_steps = iota((waves4, LANES), 1)
    near_cos, near_sin = turn_tables((c_steps * lane_steps).astype(F32), fourth_float)
    far_cos, far_sin = turn_tables((c_steps * lane_steps * LANES).astype(F32), fourth_float)
    for block in range(quarter // LANES):
        fc, fs = far_cos[:, block : block + 1], far_sin[:, block : block + 1]
        cols = pl.ds(block * LANES, LANES)
        for part, value in enumerate(
            (near_cos * fc - near_sin * fs, near_cos * fs + near_sin * fc)
        ):
            high, low = split(value)
            table_ref[pl.ds(part * waves4, waves4), cols] = high
            low_table[pl.ds(part * waves4, waves4), cols] = low
    wave_row = spaced_slots(wave_ref[...].reshape(1, -1), order_ref.shape[1] // SUB)
    for r in range(4):
        m = 4 * iota((waves4, wave_row.shape[1]), 0) + r
        order_ref[pl.ds(r * waves4, waves4), :] = jnp.where(wave_row == m, 1.0, 0.0).astype(BF16)


def forward_stage(lon_ref, send_ref, table_ref, order_ref, pieces, low_table):
    quarter = table_ref.shape[1]
    waves4 = table_ref.shape[0] // 2
    owners = send_ref.shape[0]
    count, fourth, n_float = length_of(lon_ref)
    live = iota((8, quarter), 1) < fourth
    parts = [jnp.where(live, pieces[a], 0.0) for a in range(4)]
    x0, x1, x2, x3 = parts
    fold_cos, fold_sin = fold_tables(n_float, quarter)
    c1, s1, c2, s2 = fold_cos[1:2], fold_sin[1:2], fold_cos[2:3], fold_sin[2:3]
    c3, s3 = fold_cos[3:4], fold_sin[3:4]
    a02, d02, a13, d13 = x0 + x2, x0 - x2, x1 + x3, x1 - x3
    even = a02 - a13
    z = jnp.concatenate(
        [
            a02 + a13,
            d02 * c1 - d13 * s1,
            even * c2,
            d02 * c3 + d13 * s3,
            jnp.zeros_like(x0),
            -d13 * c1 - d02 * s1,
            -even * s2,
            d13 * c3 - d02 * s3,
        ],
        axis=0,
    )
    z_high, z_low = split(z)
    both = mxu(jnp.concatenate([z_high, z_low], axis=0), table_ref[...], NT)
    total = both[:64] + both[64:] + mxu(z_high, low_table[...], NT)
    real = total[:32, :waves4] + total[32:, waves4:]
    imag = total[32:, :waves4] - total[:32, waves4:]
    scale = 1.0 / jnp.sqrt(n_float)
    m = 4 * iota((32, waves4), 1) + iota((32, waves4), 0) // 8
    keep = 2 * m < count
    real = jnp.where(keep, real * scale, 0.0)
    imag = jnp.where(keep, imag * scale, 0.0)
    fourier = jnp.concatenate(
        [
            jnp.concatenate([part[8 * r : 8 * r + 8] for r in range(4)], axis=1)
            for part in (real, imag)
        ],
        axis=0,
    )
    sorted2 = mxu(jnp.concatenate(split(fourier), axis=0), order_ref[...])
    slots = sorted2[:16] + sorted2[16:]
    per = LANES // SUB
    for o in range(owners):
        cols = slice(o // per * LANES, o // per * LANES + LANES)
        send_ref[o] = pack_message(slots[0:8, cols], slots[8:16, cols], o % per)


def middle_kernel(
    axes, wave_count, lon_ref, stiff_hbm, wave_hbm, grid_ref, legendre_ref,
    spectra_ref, table_ref,
    stiff_ref, wave_ref, wave_row_ref, order_ref, rows, pieces, low_table, send_ref, own_ref, other_ref,
    recv, back_send, back_recv, spread, gather, lhs, damped,
    send_sem, recv_sem, back_send_sem, back_recv_sem, own_sem, swap_sem, in_sem,
):
    bands, hemis, sides = axes
    devices = bands * hemis * sides
    w, h, f = lax.axis_index("wave"), lax.axis_index("hemi"), lax.axis_index("fld")
    my_owner = (w * sides + f) * hemis + h
    slot_count = own_ref.shape[0] // (2 * bands)
    pairs2 = 2 * slot_count
    k_count = own_ref.shape[1]

    group = bands * sides

    def partner(i):
        iw, ih, side = i // (hemis * sides), i // sides % hemis, i % sides
        pw = lax.rem(w + iw, bands) if iw else w
        return pw, (1 - h if ih else h), (1 - f if side else f), ih

    barrier = pltpu.get_barrier_semaphore()

    for i in range(1, devices):
        pl.semaphore_signal(barrier, inc=1, device_id=partner(i)[:3], device_id_type=MESH)

    def slot_of(pw, pf, ih):
        return ih * group + pw * sides + pf

    own_half = pltpu.make_async_copy(legendre_ref.at[h], own_ref, own_sem.at[2])
    stiff_in = pltpu.make_async_copy(stiff_hbm, stiff_ref, in_sem.at[1])
    wave_in = pltpu.make_async_copy(wave_hbm, wave_ref, in_sem.at[2])
    wave_row_in = pltpu.make_async_copy(wave_hbm, wave_row_ref, in_sem.at[3])
    wave_row_in.start()
    grid_in = [
        pltpu.make_async_copy(
            grid_ref.at[r // grid_ref.shape[1], r % grid_ref.shape[1]],
            rows.at[pl.ds(r, 1), pl.ds(0, grid_ref.shape[3])],
            in_sem.at[4 + r],
        )
        for r in range(8)
    ]
    for copy in grid_in:
        copy.start()
    wave_in.start()
    stiff_in.start()
    own_half.start()
    rows[:, pl.ds(grid_ref.shape[3], rows.shape[1] - grid_ref.shape[3])] = jnp.zeros(
        (8, rows.shape[1] - grid_ref.shape[3]), F32
    )
    wave_row_in.wait()
    for copy in grid_in:
        copy.wait()
    build_tables(lon_ref, grid_ref, wave_row_ref, table_ref, order_ref, rows, pieces, low_table)
    pl.semaphore_wait(barrier, devices - 1)
    swap = pltpu.make_async_remote_copy(
        src_ref=legendre_ref.at[1 - h],
        dst_ref=other_ref,
        send_sem=swap_sem.at[0],
        recv_sem=swap_sem.at[1],
        device_id=(w, 1 - h, f),
        device_id_type=MESH,
    )
    swap.start()
    forward_stage(lon_ref, send_ref, table_ref, order_ref, pieces, low_table)

    own_copy = pltpu.make_async_copy(
        send_ref.at[my_owner], recv.at[w * sides + f], own_sem.at[0]
    )
    own_copy.start()

    def out_copy(i):
        pw, ph, pf, ih = partner(i)
        return pltpu.make_async_remote_copy(
            src_ref=send_ref.at[(pw * sides + pf) * hemis + ph],
            dst_ref=recv.at[slot_of(w, f, ih)],
            send_sem=send_sem.at[i],
            recv_sem=recv_sem.at[slot_of(w, f, ih)],
            device_id=(pw, ph, pf),
            device_id_type=MESH,
        )

    def in_copy(i):
        pw, ph, pf, ih = partner(i)
        there = slot_of(pw, pf, ih)
        return pltpu.make_async_remote_copy(
            src_ref=send_ref.at[0],
            dst_ref=recv.at[there],
            send_sem=send_sem.at[i],
            recv_sem=recv_sem.at[there],
            device_id=(pw, ph, pf),
            device_id_type=MESH,
        )

    def loop(act):
        for i in range(1, devices):
            act(i)

    loop(lambda i: out_copy(i).start())

    wave_in.wait()
    stiff_in.wait()
    shape = spread.shape
    row, col = iota(shape, 0), iota(shape, 1)
    s_row = row % SUB
    spread[...] = jnp.where(
        (s_row < slot_count)
        & (col == s_row * (2 * bands) + row // (SUB * bands) * bands + row // SUB % bands),
        1.0,
        0.0,
    ).astype(BF16)
    shape = gather.shape
    row, col = iota(shape, 0), iota(shape, 1)
    hit = (
        (col % SUB == row // (2 * bands))
        & (col // (SUB * sides) == row % bands)
    )
    odd = (row // bands % 2) * (col // SUB % sides)
    gather[...] = jnp.where(hit, jnp.where(odd == 1, -1.0, 1.0), 0.0).astype(BF16)
    diagonal = iota((pairs2, own_ref.shape[0]), 1) // bands == iota((pairs2, own_ref.shape[0]), 0)
    degree_row = iota((pairs2, k_count), 0)
    degrees = degree_row % 2 + 2 * iota((pairs2, k_count), 1)
    first = my_owner * slot_count
    for s in range(slot_count):
        degrees = degrees + jnp.where(degree_row // 2 == s, wave_ref[first + s], 0)
    degree_float = degrees.astype(F32)
    ratio = degree_float * (degree_float + 1.0) / (wave_count * (wave_count - 1))
    damping = [
        jnp.where(degrees < wave_count, 1.0 / (1.0 + stiff_ref[field] * ratio), 0.0)
        for field in range(2)
    ]

    own_half.wait()
    own_copy.wait()
    loop(lambda i: in_copy(i).wait_recv())
    swap.wait_recv()

    per = LANES // SUB
    lane_block = iota((8, LANES), 1) // SUB
    spectral = None
    for rel in range(hemis):
        packed = []
        unpacked = {}
        for b in range(bands):
            north = recv[rel * group + b * sides]
            south = recv[rel * group + b * sides + 1]
            unpacked[b, 0] = unpack_message(north + south)
            unpacked[b, 1] = unpack_message(north - south)
        for part in range(2):
            blocks = [jnp.zeros((8, LANES), F32) for _ in range(2 * bands // per)]
            for b in range(bands):
                for q in range(2):
                    at = (q * bands + b) // per
                    moved = roll_lanes(unpacked[b, q], SUB * (b % per) - SUB * part)
                    blocks[at] = jnp.where(lane_block == b % per, moved, blocks[at])
            packed.append(jnp.concatenate(blocks, axis=1))
        parities = jnp.concatenate(packed, axis=0).astype(BF16)
        values = mxu(parities, spread[...])
        for ch in range(16):
            lhs[pl.ds(ch * pairs2, pairs2), :] = jnp.where(
                diagonal, values[ch : ch + 1, :], 0.0
            ).astype(BF16)
        weights = own_ref if rel == 0 else other_ref
        term = mxu(lhs[...], weights[...])
        spectral = term if spectral is None else spectral + term
    for ch in range(16):
        rows = slice(ch * pairs2, (ch + 1) * pairs2)
        damped[rows, :] = (spectral[rows] * damping[ch // 4 % 2]).astype(BF16)

    for rel in range(hemis):
        weights = own_ref if rel == 0 else other_ref
        full = mxu(damped[...], weights[...], NT)
        sums = jnp.concatenate(
            [
                jnp.sum(
                    jnp.where(diagonal, full[ch * pairs2 : (ch + 1) * pairs2], 0.0),
                    axis=0,
                    keepdims=True,
                )
                for ch in range(16)
            ],
            axis=0,
        )
        both = mxu(jnp.concatenate(split(sums), axis=0), gather[...])
        cycles = both[:16] + both[16:]
        for t in range(group):
            cols = slice(t // per * LANES, t // per * LANES + LANES)
            back_send[rel * group + t] = pack_message(cycles[0:8, cols], cycles[8:16, cols], t % per)

    own_back = pltpu.make_async_copy(
        back_send.at[w * sides + f], back_recv.at[my_owner], own_sem.at[1]
    )
    own_back.start()

    def home_copy(i):
        pw, ph, pf, ih = partner(i)
        return pltpu.make_async_remote_copy(
            src_ref=back_send.at[slot_of(pw, pf, ih)],
            dst_ref=back_recv.at[my_owner],
            send_sem=back_send_sem.at[i],
            recv_sem=back_recv_sem.at[my_owner],
            device_id=(pw, ph, pf),
            device_id_type=MESH,
        )

    def home_in(i):
        pw, ph, pf, ih = partner(i)
        there = (pw * sides + pf) * hemis + ph
        return pltpu.make_async_remote_copy(
            src_ref=back_send.at[0],
            dst_ref=back_recv.at[there],
            send_sem=back_send_sem.at[i],
            recv_sem=back_recv_sem.at[there],
            device_id=(pw, ph, pf),
            device_id_type=MESH,
        )

    loop(lambda i: home_copy(i).start())
    own_back.wait()
    loop(lambda i: home_in(i).wait_recv())
    packed = []
    for part in range(2):
        blocks = []
        for v in range(devices // per):
            block = jnp.zeros((8, LANES), F32)
            for at in range(per):
                moved = roll_lanes(unpack_message(back_recv[v * per + at]), SUB * at - SUB * part)
                block = jnp.where(lane_block == at, moved, block)
            blocks.append(block)
        packed.append(jnp.concatenate(blocks, axis=1))
    slots = jnp.concatenate(packed, axis=0)
    both = mxu(jnp.concatenate(split(slots), axis=0), order_ref[...], NT)
    spectra_ref[...] = both[:16] + both[16:]
    swap.wait_send()
    loop(lambda i: out_copy(i).wait_send())
    loop(lambda i: home_copy(i).wait_send())


def inverse_kernel(
    wave_count, lon_ref, spectra_ref, table_ref, smooth_ref, bracket_ref, acc
):
    fields, levels, _, lon_slots = smooth_ref.shape
    quarter = table_ref.shape[1]
    waves4 = table_ref.shape[0] // 2
    acc[...] = jnp.zeros_like(acc)
    count, fourth, n_float = length_of(lon_ref)
    fold_cos, fold_sin = fold_tables(n_float, quarter)
    spectra = spectra_ref[...]
    lines = []
    imag_lines = []
    for r in range(4):
        m = 4 * iota((8, waves4), 1) + r
        weight = jnp.where(2 * m < count, jnp.where(m == 0, 1.0, 2.0), 0.0)
        cols = slice(r * waves4, (r + 1) * waves4)
        real, imag = spectra[0:8, cols] * weight, spectra[8:16, cols] * weight
        steep = m.astype(F32) / wave_count
        cre = jnp.concatenate([real, -imag * steep], axis=0)
        cim = jnp.concatenate([imag, real * steep], axis=0)
        lines.append(jnp.concatenate([cre, -cim], axis=1))
        if r:
            imag_lines.append(jnp.concatenate([cim, cre], axis=1))
    left = jnp.concatenate(lines + imag_lines, axis=0).astype(BF16)
    sums = mxu(left, table_ref[...])
    re = [sums[16 * r : 16 * r + 16] for r in range(4)]
    im = [None] + [sums[48 + 16 * r : 64 + 16 * r] for r in range(1, 4)]
    cos = [fold_cos[r : r + 1] for r in range(4)]
    sin = [fold_sin[r : r + 1] for r in range(4)]
    h0 = re[0]
    h1r, h1i = re[1] * cos[1] - im[1] * sin[1], re[1] * sin[1] + im[1] * cos[1]
    h2 = re[2] * cos[2] - im[2] * sin[2]
    h3r, h3i = re[3] * cos[3] - im[3] * sin[3], re[3] * sin[3] + im[3] * cos[3]
    even, odd, cross, turn = h0 + h2, h0 - h2, h1r + h3r, h3i - h1i
    live = iota((16, quarter), 1) < fourth
    scale = 1.0 / jnp.sqrt(n_float)
    width = quarter + LANES
    for a, value in enumerate((even + cross, odd + turn, even - cross, odd - turn)):
        value = jnp.where(live, value * scale, 0.0)
        smooth, slope = value[0:8], value[8:16]
        flipped = jnp.concatenate([slope[4:8], slope[0:4]], axis=0)
        product = smooth * flipped
        bracket = product - jnp.concatenate([product[4:8], product[0:4]], axis=0)
        segment = jnp.concatenate([smooth, bracket], axis=0)
        segment = jnp.concatenate([segment, jnp.zeros((16, LANES), F32)], axis=1)
        start = fourth * a
        segment = pltpu.roll(segment, lax.rem(start, LANES), 1)
        aligned = pl.multiple_of((start // LANES) * LANES, LANES)
        acc[:, pl.ds(aligned, width)] += segment
    for f in range(fields):
        for l in range(levels):
            smooth_ref[f, l] = acc[pl.ds(f * levels + l, 1), pl.ds(0, lon_slots)]
    for l in range(levels):
        bracket_ref[l] = acc[pl.ds(8 + l, 1), pl.ds(0, lon_slots)]


def in_hbm(x):
    return pltpu.with_memory_space_constraint(x, pltpu.HBM)


def fast_device(axes, grid, lon_count, wave_order, legendre, stiffness):
    bands, hemis, sides = axes
    owners = bands * hemis * sides
    wave_count = wave_order.shape[0]
    fields, levels, _, lon_slots = grid.shape
    slots = wave_count // owners
    k_count = legendre.shape[4]
    quarter = round_up(lon_slots // 4, LANES)
    waves4 = round_up(wave_count // 4, LANES)
    long_rows = lon_slots + 2 * LANES
    smem = pl.BlockSpec(memory_space=pltpu.SMEM)
    vmem = pl.BlockSpec(memory_space=pltpu.VMEM)
    hbm = pl.BlockSpec(memory_space=pltpu.HBM)
    weights = legendre.reshape(hemis, slots * 2 * bands, k_count)
    group = bands * sides
    lines = 16 * 2 * slots
    spectra, table = pl.pallas_call(
        functools.partial(middle_kernel, axes, wave_count),
        out_shape=(
            pltpu.VMEM((16, 4 * waves4), F32),
            pltpu.VMEM((2 * waves4, quarter), BF16),
        ),
        in_specs=[smem, hbm, hbm, hbm, hbm],
        out_specs=(vmem, vmem),
        scratch_shapes=[
            pltpu.SMEM(stiffness.shape, F32),
            pltpu.SMEM(wave_order.shape, jnp.int32),
            pltpu.VMEM(wave_order.shape, jnp.int32),
            pltpu.VMEM((4 * waves4, owners * SUB), BF16),
            pltpu.VMEM((8, long_rows), F32),
            pltpu.VMEM((4, 8, quarter), F32),
            pltpu.VMEM((2 * waves4, quarter), BF16),
            pltpu.VMEM((owners, 4, LANES), F32),
            pltpu.VMEM((slots * 2 * bands, k_count), BF16),
            pltpu.VMEM((slots * 2 * bands, k_count), BF16),
            pltpu.VMEM((owners, 4, LANES), F32),
            pltpu.VMEM((owners, 4, LANES), F32),
            pltpu.VMEM((owners, 4, LANES), F32),
            pltpu.VMEM((2 * bands * SUB, slots * 2 * bands), BF16),
            pltpu.VMEM((slots * 2 * bands, group * SUB), BF16),
            pltpu.VMEM((lines, slots * 2 * bands), BF16),
            pltpu.VMEM((lines, k_count), BF16),
            pltpu.SemaphoreType.DMA((owners,)),
            pltpu.SemaphoreType.DMA((owners,)),
            pltpu.SemaphoreType.DMA((owners,)),
            pltpu.SemaphoreType.DMA((owners,)),
            pltpu.SemaphoreType.DMA((3,)),
            pltpu.SemaphoreType.DMA((2,)),
            pltpu.SemaphoreType.DMA((12,)),
        ],
        compiler_params=pltpu.CompilerParams(collective_id=0, has_side_effects=True, vmem_limit_bytes=24 << 20),
        name="middle",
    )(lon_count, *[in_hbm(x) for x in (stiffness, wave_order, grid, weights)])
    return pl.pallas_call(
        functools.partial(inverse_kernel, wave_count),
        out_shape=(
            jax.ShapeDtypeStruct(grid.shape, F32),
            jax.ShapeDtypeStruct((levels, 1, lon_slots), F32),
        ),
        in_specs=[smem, vmem, vmem],
        out_specs=(vmem, vmem),
        scratch_shapes=[
            pltpu.VMEM((16, long_rows), F32),
        ],
        compiler_params=pltpu.CompilerParams(vmem_limit_bytes=24 << 20),
        name="inverse",
    )(lon_count, spectra, table)


M = 768
FIELDS = 2
LEVELS = 4
K = 384


exact_mode = lax.Precision.HIGHEST


def general_device(grid, lon_count, wave_order, legendre, stiffness):
    lon_slots = grid.shape[3]
    rows_per = FIELDS * LEVELS
    channels = 2 * rows_per
    inner_width = 64
    wave_blocks = M // inner_width
    band_count = lax.axis_size("wave")
    slot_dev = M // (2 * band_count)
    cycle_length = lon_count[0]
    longitudes = jnp.arange(lon_slots, dtype=jnp.int32)
    wavenumbers = jnp.arange(M, dtype=jnp.int32)
    angle_step = 2.0 * jnp.pi / cycle_length.astype(jnp.float32)
    block_starts = jnp.arange(wave_blocks, dtype=jnp.int32) * inner_width
    inner_waves = jnp.arange(inner_width, dtype=jnp.int32)
    outer_angle = angle_step * (block_starts[:, None] * longitudes[None, :] % cycle_length).astype(
        jnp.float32
    )
    outer_cos = jnp.cos(outer_angle)
    outer_sin = jnp.sin(outer_angle)
    inner_angle = angle_step * (longitudes[:, None] * inner_waves[None, :] % cycle_length).astype(
        jnp.float32
    )
    inner_table = jnp.concatenate([jnp.cos(inner_angle), jnp.sin(inner_angle)], axis=1)
    cycle_scale = 1.0 / jnp.sqrt(cycle_length.astype(jnp.float32))
    live_points = longitudes < cycle_length
    wave_live = 2 * wavenumbers < cycle_length
    cycle_rows = jnp.where(live_points[None, :], grid[:, :, 0, :].reshape(rows_per, lon_slots), 0.0)
    modulated = jnp.stack(
        [cycle_rows[:, None, :] * outer_cos[None], -(cycle_rows[:, None, :] * outer_sin[None])]
    )
    product = jnp.dot(
        modulated.reshape(2 * rows_per * wave_blocks, lon_slots), inner_table, precision=exact_mode
    )
    product = product.reshape(2, rows_per, wave_blocks, 2 * inner_width)
    real_part = product[0, :, :, :inner_width] + product[1, :, :, inner_width:]
    imag_part = product[1, :, :, :inner_width] - product[0, :, :, inner_width:]
    fourier = jnp.stack([real_part, imag_part]).reshape(channels, M) * cycle_scale
    fourier = jnp.where(wave_live[None, :], fourier, 0.0)
    slotted = fourier[:, wave_order].reshape(channels, band_count, 2, slot_dev)
    side_index = lax.axis_index("fld")
    arrived = lax.all_to_all(
        lax.all_to_all(slotted[None, :, None], "wave", split_axis=3, concat_axis=2, tiled=True),
        "fld",
        split_axis=4,
        concat_axis=0,
        tiled=True,
    )
    stacked = arrived.reshape(2, channels, band_count, slot_dev)
    even_part = (stacked[0] + stacked[1]).astype(jnp.bfloat16)
    odd_part = (stacked[0] - stacked[1]).astype(jnp.bfloat16)
    parities = jnp.stack([even_part, odd_part])
    weights = legendre[:, 0]
    owner_index = lax.axis_index("wave") * 2 + side_index
    my_waves = lax.dynamic_slice_in_dim(wave_order, owner_index * slot_dev, slot_dev)
    degrees = (
        my_waves[:, None, None]
        + 2 * jnp.arange(K, dtype=jnp.int32)[None, None, :]
        + jnp.arange(2, dtype=jnp.int32)[None, :, None]
    )
    valid_degree = degrees < M
    spectral = jnp.einsum("aqwk,qcwa->aqck", weights, parities, preferred_element_type=jnp.float32)
    spectral = jnp.where(valid_degree[:, :, None, :], spectral, 0.0)
    chan_stiff = jnp.tile(jnp.repeat(stiffness, LEVELS), 2)
    degree_float = degrees.astype(jnp.float32)
    degree_ratio = degree_float * (degree_float + 1.0) / (M * (M - 1))
    summed = lax.psum(spectral, "hemi")
    damped = (
        summed / (1.0 + chan_stiff[None, None, :, None] * degree_ratio[:, :, None, :])
    ).astype(jnp.bfloat16)
    returned = jnp.einsum("aqwk,aqck->qcwa", weights, damped, preferred_element_type=jnp.float32)
    north_vals = returned[0] + returned[1]
    south_vals = returned[0] - returned[1]
    homebound = lax.all_to_all(
        lax.all_to_all(
            jnp.stack([north_vals, south_vals])[:, None, None],
            "wave",
            split_axis=4,
            concat_axis=2,
            tiled=True,
        ),
        "fld",
        split_axis=0,
        concat_axis=1,
        tiled=True,
    )
    homebound = homebound.reshape(2, band_count, channels, slot_dev)
    slot_values = jnp.transpose(homebound, (2, 1, 0, 3)).reshape(channels, M)
    spectra = jnp.zeros((channels, M), jnp.float32).at[:, wave_order].set(slot_values)
    weight_wave = jnp.where(wavenumbers == 0, 1.0, 2.0) * jnp.where(wave_live, cycle_scale, 0.0)
    real_coef = spectra[:rows_per] * weight_wave
    imag_coef = spectra[rows_per:] * weight_wave
    wave_ratio = wavenumbers.astype(jnp.float32) / M
    cos_coef = jnp.stack([real_coef, -(imag_coef * wave_ratio)]).reshape(
        2 * rows_per, wave_blocks, inner_width
    )
    sin_coef = jnp.stack([imag_coef, real_coef * wave_ratio]).reshape(
        2 * rows_per, wave_blocks, inner_width
    )
    left_rows = jnp.stack(
        [
            jnp.concatenate([cos_coef, -sin_coef], axis=2),
            jnp.concatenate([sin_coef, cos_coef], axis=2),
        ]
    )
    cycle_sums = lax.dot_general(
        left_rows.reshape(4 * rows_per * wave_blocks, 2 * inner_width),
        inner_table,
        (((1,), (1,)), ((), ())),
        precision=exact_mode,
    )
    cycle_sums = cycle_sums.reshape(2, 2 * rows_per, wave_blocks, lon_slots)
    values = jnp.sum(cycle_sums[0] * outer_cos[None] - cycle_sums[1] * outer_sin[None], axis=1)
    values = jnp.where(live_points[None, :], values, 0.0)
    smooth_rows = values[:rows_per].reshape(FIELDS, LEVELS, lon_slots)
    slope_rows = values[rows_per:].reshape(FIELDS, LEVELS, lon_slots)
    bracket = smooth_rows[0] * slope_rows[1] - smooth_rows[1] * slope_rows[0]
    return (smooth_rows[:, :, None, :], bracket[:, None, :])


def solution(mesh):
    axes = (mesh.shape["wave"], mesh.shape["hemi"], mesh.shape["fld"])
    bands, hemis, sides = axes
    placed = (
        P(None, None, ("wave", "hemi", "fld"), None),
        P(("wave", "hemi", "fld")),
        P(),
        P(("wave", "fld"), "hemi", None, None, None),
        P(),
    )
    fits = bands == 8 and hemis == 2 and sides == 2 and M % (bands * hemis * sides) == 0
    step = functools.partial(fast_device, axes) if fits else general_device
    return jax.shard_map(
        step,
        mesh=mesh,
        in_specs=placed,
        out_specs=(
            P(None, None, ("wave", "hemi", "fld"), None),
            P(None, ("wave", "hemi", "fld"), None),
        ),
        check_vma=False,
    )
```

```python
import functools
import math

import jax
import jax.numpy as jnp
from jax import lax
from jax.experimental import pallas as pl
from jax.experimental.pallas import tpu as pltpu
from jax.sharding import PartitionSpec as P

LANES = 128
SUB = 8
HALF = LANES // 2
F32 = jnp.float32
BF16 = jnp.bfloat16
NN = (((1,), (0,)), ((), ()))
NT = (((1,), (1,)), ((), ()))
TN = (((0,), (0,)), ((), ()))
MESH = pl.DeviceIdType.MESH


def round_up(value, step):
    return -(-value // step) * step


def mxu(a, b, dims=NN):
    return lax.dot_general(a, b, dims, preferred_element_type=F32)


def split(x):
    high = x.astype(BF16)
    return high, (x - high.astype(F32)).astype(BF16)


def iota(shape, axis):
    return lax.broadcasted_iota(jnp.int32, shape, axis)


def sine_turn(x):
    y = x * x
    total = jnp.full_like(y, 0.0)
    for power in (13, 11, 9, 7, 5, 3, 1):
        sign = 1.0 if power % 4 == 1 else -1.0
        total = total * y + sign * (2.0 * math.pi) ** power / math.factorial(power)
    return total * x


def turn_tables(steps, period):
    inverse = 1.0 / period
    rest = steps - jnp.floor(steps * inverse) * period
    turn = rest * inverse
    turn = turn - jnp.floor(turn + 0.5)
    shifted = turn - 0.25
    shifted = jnp.where(shifted < -0.5, shifted + 1.0, shifted)
    return sine_turn(0.25 - jnp.abs(turn)), sine_turn(0.25 - jnp.abs(shifted))


def length_of(lon_ref):
    count = lon_ref[0]
    return count, lax.shift_right_logical(count, 2), jnp.full((1, 1), count.astype(F32), F32)


def fold_tables(n_float, quarter):
    steps = iota((8, quarter), 0) * iota((8, quarter), 1)
    return turn_tables(steps.astype(F32), n_float)


def roll_lanes(x, amount):
    amount = amount % x.shape[1]
    return x if amount == 0 else pltpu.roll(x, amount, 1)


def lane_gather(tile, index):
    return jnp.take_along_axis(tile, index, axis=1, mode="promise_in_bounds")


def window_at(tiles, start, most, count):
    whole = lax.shift_right_logical(start, 7)
    bits = (most // LANES).bit_length()
    for bit in reversed(range(bits)):
        step = 1 << bit
        keep = count + step
        hit = jnp.full(tiles[0].shape, whole, jnp.int32) & step != 0
        tiles = [
            jnp.where(hit, tiles[i + step], tiles[i]) if i + step < len(tiles) else tiles[i]
            for i in range(min(keep, len(tiles)))
        ]
    lane = iota(tiles[0].shape, 1) + jnp.full(tiles[0].shape, start & (LANES - 1), jnp.int32)
    index = lane & (LANES - 1)
    turned = [lane_gather(tile, index) for tile in tiles[: count + 1]]
    inside = lane < LANES
    return jnp.concatenate(
        [jnp.where(inside, turned[i], turned[i + 1]) for i in range(count)], axis=1
    )


def half_low(shape):
    return iota(shape, 1) < HALF


def wave_of(tile, shape):
    lane = iota(shape, 1)
    if tile < 4:
        return 4 * lane + tile
    step = jnp.where(lane < HALF, lane, lane - HALF)
    return 4 * (LANES + step) + 2 * (tile - 4) + jnp.where(lane < HALF, 0, 1)


def pick(tiles, tile_id, lane_id):
    out = None
    for i, tile in enumerate(tiles):
        moved = lane_gather(tile, lane_id)
        out = moved if out is None else jnp.where(tile_id == i, moved, out)
    return out


def slot_waves(wave_row, owners):
    row = jnp.broadcast_to(wave_row.astype(F32), (SUB, wave_row.shape[1]))
    tiles = [row[:, i * LANES : (i + 1) * LANES] for i in range(row.shape[1] // LANES)]
    slots = row.shape[1] // owners
    lane = iota((SUB, LANES), 1)
    out = []
    for group in range(slots // SUB):
        for part in range(owners // 16):
            slot = (part * 16 + lane // SUB) * slots + group * SUB + lane % SUB
            first = part * 16 * slots // LANES
            last = ((part * 16 + 15) * slots + group * SUB + SUB - 1) // LANES
            out.append(pick(tiles[first : last + 1], slot // LANES - first, slot % LANES))
    return out


def build_tables(lon_ref, rows, table_ref, low_table, pieces, lon_slots):
    quarter = table_ref.shape[1]
    waves4 = table_ref.shape[0] // 2
    _, fourth, _ = length_of(lon_ref)
    fourth_float = jnp.full((1, 1), fourth.astype(F32), F32)
    c_steps = iota((waves4, LANES), 0)
    lane_steps = iota((waves4, LANES), 1)
    near_cos, near_sin = turn_tables((c_steps * lane_steps).astype(F32), fourth_float)
    far_cos, far_sin = turn_tables((c_steps * lane_steps * LANES).astype(F32), fourth_float)
    rest = waves4 - LANES
    for block in range(quarter // LANES):
        fc, fs = far_cos[:, block : block + 1], far_sin[:, block : block + 1]
        cols = pl.ds(block * LANES, LANES)
        for part, value in enumerate(
            (near_cos * fc - near_sin * fs, near_cos * fs + near_sin * fc)
        ):
            high, low = split(value)
            for ref, half in ((table_ref, high), (low_table, low)):
                ref[pl.ds(part * LANES, LANES), cols] = half[:LANES]
                ref[pl.ds(2 * LANES + part * rest, rest), cols] = half[LANES:]


def forward_stage(lon_ref, rows, table_ref, low_table, waves, flip, send_ref, lon_slots):
    quarter = table_ref.shape[1]
    count, fourth, n_float = length_of(lon_ref)
    live = iota((8, quarter), 1) < fourth
    tiles = [rows[:, i * LANES : (i + 1) * LANES] for i in range(rows.shape[1] // LANES)]
    parts = [rows[:, :quarter]]
    for a in range(1, 4):
        parts.append(window_at(tiles, fourth * a, a * (lon_slots // 4), quarter // LANES))
    x0, x1, x2, x3 = [jnp.where(live, part, 0.0) for part in parts]
    fold_cos, fold_sin = fold_tables(n_float, quarter)
    c1, s1, c2, s2 = fold_cos[1:2], fold_sin[1:2], fold_cos[2:3], fold_sin[2:3]
    c3, s3 = fold_cos[3:4], fold_sin[3:4]
    a02, d02, a13, d13 = x0 + x2, x0 - x2, x1 + x3, x1 - x3
    even = a02 - a13
    z = jnp.concatenate(
        [
            a02 + a13,
            d02 * c1 - d13 * s1,
            even * c2,
            d02 * c3 + d13 * s3,
            jnp.zeros_like(x0),
            -d13 * c1 - d02 * s1,
            -even * s2,
            d13 * c3 - d02 * s3,
        ],
        axis=0,
    )
    z_high, z_low = split(z)
    both = mxu(jnp.concatenate([z_high, z_low], axis=0), table_ref[...], NT)
    total = both[:64] + both[64:] + mxu(z_high, low_table[...], NT)
    t0, t1, t2 = (total[:, i * LANES : (i + 1) * LANES] for i in range(3))
    near = [t0[:32] + t1[32:], t0[32:] - t1[:32]]
    turned = roll_lanes(t2, HALF)
    low = half_low((32, LANES))
    far = [
        jnp.where(low, t2[:32], turned[:32]) + jnp.where(low, turned[32:], t2[32:]),
        jnp.where(low, t2[32:], turned[32:]) - jnp.where(low, turned[:32], t2[:32]),
    ]
    scale = 1.0 / jnp.sqrt(n_float)
    low = half_low((8, LANES))
    sources = []
    for tile in range(6):
        if tile < 4:
            halves = [part[8 * tile : 8 * tile + 8] for part in near]
        else:
            r = 2 * (tile - 4)
            halves = [
                jnp.where(low, part[8 * r : 8 * r + 8], part[8 * r + 8 : 8 * r + 16])
                for part in far
            ]
        keep = 2 * wave_of(tile, (8, LANES)) < count
        sources.append([jnp.where(keep, half * scale, 0.0) for half in halves])
    moved = []
    for wave in waves:
        m = wave.astype(jnp.int32)
        r, c = m % 4, m // 4
        tile_id = jnp.where(c < LANES, r, 4 + r // 2)
        lane_id = jnp.where(c < LANES, c, c - LANES + HALF * (r % 2))
        for part in range(2):
            moved.append(pick([source[part] for source in sources], tile_id, lane_id))
    moved.append(jnp.zeros((LANES - 8 * len(moved), LANES), F32))
    flip[...] = jnp.concatenate(moved, axis=0).T
    lane_block = iota((16, LANES), 1) // 16
    lines = [flip[pl.ds(s, 16, stride=SUB), :] for s in range(SUB)]
    for t in range(len(waves)):
        out = None
        for s in range(SUB):
            line = roll_lanes(lines[s], 16 * (s - t))
            out = line if out is None else jnp.where(lane_block == s, line, out)
        send_ref[pl.ds(16 * SUB * (t % 2) + t // 2, 16, stride=SUB), :] = out


def home_lines(back_recv, flip, tile_count):
    lane_block = iota((16, LANES), 1) // 16
    lines = [
        back_recv[pl.ds(16 * SUB * (t % 2) + t // 2, 16, stride=SUB), :] for t in range(tile_count)
    ]
    for s in range(SUB):
        out = jnp.zeros((16, LANES), F32)
        for t in range(tile_count):
            out = jnp.where(lane_block == t, roll_lanes(lines[t], 16 * (t - s)), out)
        flip[pl.ds(s, 16, stride=SUB), :] = out
    turned = flip[...].T
    return [
        [turned[16 * t + 8 * part : 16 * t + 8 * part + 8] for t in range(tile_count)]
        for part in range(2)
    ]


def find_places(waves, places):
    stacked = jnp.concatenate(
        [wave[0:1] for wave in waves] + [jnp.zeros((LANES - len(waves), LANES), F32)], axis=0
    ).T
    place = iota((LANES, LANES), 0).astype(F32)
    for tile in range(6):
        want = wave_of(tile, (LANES, LANES)).astype(F32)
        total = jnp.zeros((LANES, LANES), F32)
        for t in range(len(waves)):
            total = jnp.where(stacked[:, t : t + 1] == want, place + float(LANES * t), total)
        places[pl.ds(tile * SUB, SUB), :] = jnp.broadcast_to(
            jnp.sum(total, axis=0, keepdims=True), (SUB, LANES)
        ).astype(jnp.int32)


def damping_table(wave_count, stiff_ref, wave_ref, first, damp):
    groups, k_count, width = damp.shape
    lane = iota((SUB, width), 1)
    field = lane // 4 % 2
    stiff = jnp.where(field == 0, stiff_ref[0], stiff_ref[1])
    for g in range(groups):
        wave = lane // LANES
        for s in range(SUB):
            wave = wave + jnp.where(lane // 16 % SUB == s, wave_ref[first + g * SUB + s], 0)
        degrees = wave[0:1] + 2 * iota((k_count, width), 0)
        degree_float = degrees.astype(F32)
        ratio = degree_float * (degree_float + 1.0) / (wave_count * (wave_count - 1))
        damp[g] = jnp.where(degrees < wave_count, 1.0 / (1.0 + stiff[0:1] * ratio), 0.0)


def left_lines(count, wave_count, sources, places, left_ref):
    low = half_low((16, LANES))
    near_re, near_im, far_re, far_im = [], [], [], []
    for tile in range(6):
        code = places[pl.ds(tile * SUB, SUB), :]
        tile_id, lane_id = code // LANES, code % LANES
        m = wave_of(tile, (8, LANES))
        weight = jnp.where(2 * m < count, jnp.where(m == 0, 1.0, 2.0), 0.0)
        steep = m.astype(F32) / wave_count
        real, imag = (pick(part, tile_id, lane_id) * weight for part in sources)
        cre = jnp.concatenate([real, -imag * steep], axis=0)
        cim = jnp.concatenate([imag, real * steep], axis=0)
        if tile < 4:
            near_re.append(cre)
            near_im.append(cim)
        else:
            cre_turned, cim_turned = roll_lanes(cre, HALF), roll_lanes(cim, HALF)
            far_re += [jnp.where(low, cre, -cim_turned), jnp.where(low, cre_turned, -cim)]
            far_im += [jnp.where(low, cim, cre_turned), jnp.where(low, cim_turned, cre)]
    lines = [
        jnp.concatenate([near_re[r], -near_im[r], far_re[r]], axis=1) for r in range(4)
    ] + [jnp.concatenate([near_im[r], near_re[r], far_im[r]], axis=1) for r in range(1, 4)]
    for at, line in enumerate(lines):
        left_ref[pl.ds(16 * at, 16), :] = line.astype(BF16)


def middle_kernel(
    axes, wave_count, lon_ref, stiff_hbm, wave_hbm, grid_ref, legendre_ref,
    left_ref, table_ref,
    stiff_ref, wave_ref, wave_row_ref, rows, low_table, flip, send_ref, recv, back_send, back_recv,
    weights, damp, places,
    send_sem, recv_sem, back_send_sem, back_recv_sem, own_sem, swap_send_sem, swap_recv_sem, in_sem,
):
    bands, hemis, sides = axes
    devices = bands * hemis * sides
    w, h, f = lax.axis_index("wave"), lax.axis_index("hemi"), lax.axis_index("fld")
    owner = (w * sides + f) * hemis + h
    groups = weights.shape[0]
    lon_slots = grid_ref.shape[3]
    first = owner * groups * SUB

    def partner(i):
        iz, ix, ih, side = i // 8, i // 4 % 2, i // 2 % 2, i % 2
        z, x = w // 2, lax.rem(w, 2)
        pz = (z, z + 1 - 2 * lax.rem(z, 2), lax.rem(z + 2, 4), 3 - z)[iz]
        px = 1 - x if ix else x
        return pz * 2 + px, (1 - h if ih else h), (1 - f if side else f), ih

    far_first = sorted(
        range(1, devices), key=lambda i: -(i // 8 + i // 4 % 2 + i // 2 % 2 + 0.1 * (i % 2))
    )
    barrier = pltpu.get_barrier_semaphore()
    for i in far_first:
        pl.semaphore_signal(barrier, inc=1, device_id=partner(i)[:3], device_id_type=MESH)

    wave_row_in = pltpu.make_async_copy(wave_hbm, wave_row_ref, in_sem.at[0])
    wave_in = pltpu.make_async_copy(wave_hbm, wave_ref, in_sem.at[1])
    stiff_in = pltpu.make_async_copy(stiff_hbm, stiff_ref, in_sem.at[2])
    wave_row_in.start()
    grid_in = [
        pltpu.make_async_copy(
            grid_ref.at[r // grid_ref.shape[1], r % grid_ref.shape[1]],
            rows.at[pl.ds(r, 1), pl.ds(0, lon_slots)],
            in_sem.at[3 + r],
        )
        for r in range(8)
    ]
    for copy in grid_in:
        copy.start()
    own_in = pltpu.make_async_copy(
        legendre_ref.at[h], weights.at[:, pl.ds(0, LANES)], own_sem.at[0]
    )
    own_in.start()
    wave_in.start()
    stiff_in.start()
    rows[:, pl.ds(lon_slots, rows.shape[1] - lon_slots)] = jnp.zeros(
        (8, rows.shape[1] - lon_slots), F32
    )
    build_tables(lon_ref, rows, table_ref, low_table, None, lon_slots)
    swap = [
        pltpu.make_async_remote_copy(
            src_ref=legendre_ref.at[1 - h, g],
            dst_ref=weights.at[g, pl.ds(LANES, LANES)],
            send_sem=swap_send_sem.at[g],
            recv_sem=swap_recv_sem.at[g],
            device_id=(w, 1 - h, f),
            device_id_type=MESH,
        )
        for g in range(groups)
    ]
    pl.semaphore_wait(barrier, devices - 1)
    for copy in swap:
        copy.start()
    wave_row_in.wait()
    waves = slot_waves(wave_row_ref[...].reshape(1, -1), devices)
    for copy in grid_in:
        copy.wait()
    forward_stage(lon_ref, rows, table_ref, low_table, waves, flip, send_ref, lon_slots)

    def slice_of(ref, place):
        return ref.at[pl.ds(pl.multiple_of(place * SUB, SUB), groups)]

    def everything(ref):
        return ref.at[pl.ds(0, (devices - 1) * groups)]

    def copies(source, target, source_place, target_place, sent, got):
        return [
            pltpu.make_async_remote_copy(
                src_ref=slice_of(source, source_place(*partner(i))),
                dst_ref=slice_of(target, target_place(*partner(i))),
                send_sem=sent.at[0],
                recv_sem=got.at[0],
                device_id=partner(i)[:3],
                device_id_type=MESH,
            )
            for i in far_first
        ]

    def whole(source, target, sent, got):
        return pltpu.make_async_remote_copy(
            src_ref=everything(source),
            dst_ref=everything(target),
            send_sem=sent.at[0],
            recv_sem=got.at[0],
            device_id=partner(1)[:3],
            device_id_type=MESH,
        )

    out_copies = copies(
        send_ref,
        recv,
        lambda pw, ph, pf, ih: (pw * sides + pf) * hemis + ph,
        lambda pw, ph, pf, ih: ih * 2 * bands + f * bands + w,
        send_sem,
        recv_sem,
    )
    out_whole = whole(send_ref, recv, send_sem, recv_sem)
    for copy in out_copies:
        copy.start()
    slice_of(recv, f * bands + w)[...] = slice_of(send_ref, owner)[...]
    wave_in.wait()
    stiff_in.wait()
    damping_table(wave_count, stiff_ref, wave_ref, first, damp)
    find_places(waves, places)
    own_in.wait()
    out_whole.wait_recv()

    lane_slot = iota((SUB, LANES), 1) // 16
    zero = jnp.zeros((SUB, LANES), F32)
    for g in range(groups):
        blocks = []
        for rel in range(hemis):
            base = rel * 2 * bands * SUB + g
            north = recv[pl.ds(base, bands, stride=SUB), :]
            south = recv[pl.ds(base + bands * SUB, bands, stride=SUB), :]
            even, odd = north + south, north - south
            for s in range(SUB):
                blocks.append(
                    jnp.concatenate([jnp.where(lane_slot == s, even, 0.0), zero], axis=1)
                )
                blocks.append(
                    jnp.concatenate([zero, jnp.where(lane_slot == s, odd, 0.0)], axis=1)
                )
        spaced = jnp.concatenate(blocks, axis=0).astype(BF16)
        swap[g].wait_recv()
        spectral = mxu(weights[g], spaced, TN)
        damped = (spectral * damp[g]).astype(BF16)
        full = mxu(weights[g], damped)
        for rel in range(hemis):
            sums = []
            for q in range(2):
                total = None
                for s in range(SUB):
                    at = rel * LANES + s * 16 + q * SUB
                    piece = full[at : at + SUB, q * LANES : (q + 1) * LANES]
                    total = piece if total is None else jnp.where(lane_slot == s, piece, total)
                sums.append(total)
            base = rel * 2 * bands * SUB + g
            back_send[pl.ds(base, bands, stride=SUB), :] = sums[0] + sums[1]
            back_send[pl.ds(base + bands * SUB, bands, stride=SUB), :] = sums[0] - sums[1]

    home_copies = copies(
        back_send,
        back_recv,
        lambda pw, ph, pf, ih: ih * 2 * bands + pf * bands + pw,
        lambda pw, ph, pf, ih: owner,
        back_send_sem,
        back_recv_sem,
    )
    home_whole = whole(back_send, back_recv, back_send_sem, back_recv_sem)
    for copy in home_copies:
        copy.start()
    slice_of(back_recv, owner)[...] = slice_of(back_send, f * bands + w)[...]
    home_whole.wait_recv()
    sources = home_lines(back_recv, flip, len(waves))
    left_lines(lon_ref[0], wave_count, sources, places, left_ref)
    for copy in swap:
        copy.wait_send()
    out_whole.wait_send()
    home_whole.wait_send()


def inverse_kernel(wave_count, lon_ref, left_ref, table_ref, smooth_ref, bracket_ref, acc):
    fields, levels, _, lon_slots = smooth_ref.shape
    quarter = table_ref.shape[1]
    count, fourth, n_float = length_of(lon_ref)
    acc[...] = jnp.zeros_like(acc)
    fold_cos, fold_sin = fold_tables(n_float, quarter)
    sums = mxu(left_ref[...], table_ref[...])
    re = [sums[16 * r : 16 * r + 16] for r in range(4)]
    im = [None] + [sums[48 + 16 * r : 64 + 16 * r] for r in range(1, 4)]
    cos = [fold_cos[r : r + 1] for r in range(4)]
    sin = [fold_sin[r : r + 1] for r in range(4)]
    h0 = re[0]
    h1r, h1i = re[1] * cos[1] - im[1] * sin[1], re[1] * sin[1] + im[1] * cos[1]
    h2 = re[2] * cos[2] - im[2] * sin[2]
    h3r, h3i = re[3] * cos[3] - im[3] * sin[3], re[3] * sin[3] + im[3] * cos[3]
    even, odd, cross, turn = h0 + h2, h0 - h2, h1r + h3r, h3i - h1i
    live = iota((16, quarter), 1) < fourth
    scale = 1.0 / jnp.sqrt(n_float)
    width = quarter + LANES
    for a, value in enumerate((even + cross, odd + turn, even - cross, odd - turn)):
        value = jnp.where(live, value * scale, 0.0)
        smooth, slope = value[0:8], value[8:16]
        flipped = jnp.concatenate([slope[4:8], slope[0:4]], axis=0)
        product = smooth * flipped
        bracket = product - jnp.concatenate([product[4:8], product[0:4]], axis=0)
        segment = jnp.concatenate([smooth, bracket], axis=0)
        segment = jnp.concatenate([segment, jnp.zeros((16, LANES), F32)], axis=1)
        start = fourth * a
        segment = pltpu.roll(segment, lax.rem(start, LANES), 1)
        aligned = pl.multiple_of((start // LANES) * LANES, LANES)
        acc[:, pl.ds(aligned, width)] += segment
    for f in range(fields):
        for l in range(levels):
            smooth_ref[f, l] = acc[pl.ds(f * levels + l, 1), pl.ds(0, lon_slots)]
    for l in range(levels):
        bracket_ref[l] = acc[pl.ds(8 + l, 1), pl.ds(0, lon_slots)]


def in_hbm(x):
    return pltpu.with_memory_space_constraint(x, pltpu.HBM)


def fast_device(axes, grid, lon_count, wave_order, legendre, stiffness):
    bands, hemis, sides = axes
    owners = bands * hemis * sides
    wave_count = wave_order.shape[0]
    fields, levels, _, lon_slots = grid.shape
    groups = wave_count // owners // SUB
    k_count = legendre.shape[4]
    quarter = round_up(lon_slots // 4, LANES)
    waves4 = wave_count // 4
    long_rows = lon_slots + 2 * LANES
    smem = pl.BlockSpec(memory_space=pltpu.SMEM)
    vmem = pl.BlockSpec(memory_space=pltpu.VMEM)
    hbm = pl.BlockSpec(memory_space=pltpu.HBM)
    weights = legendre.reshape(hemis, groups, LANES, k_count)
    message = pltpu.VMEM((owners * SUB, LANES), F32)
    left, table = pl.pallas_call(
        functools.partial(middle_kernel, axes, wave_count),
        out_shape=(
            pltpu.VMEM((7 * 16, 2 * waves4), BF16),
            pltpu.VMEM((2 * waves4, quarter), BF16),
        ),
        in_specs=[smem, hbm, hbm, hbm, hbm],
        out_specs=(vmem, vmem),
        scratch_shapes=[
            pltpu.SMEM(stiffness.shape, F32),
            pltpu.SMEM(wave_order.shape, jnp.int32),
            pltpu.VMEM(wave_order.shape, jnp.int32),
            pltpu.VMEM((8, long_rows), F32),
            pltpu.VMEM((2 * waves4, quarter), BF16),
            pltpu.VMEM((LANES, LANES), F32),
            message,
            message,
            message,
            message,
            pltpu.VMEM((groups, 2 * LANES, k_count), BF16),
            pltpu.VMEM((groups, k_count, 2 * LANES), F32),
            pltpu.VMEM((6 * SUB, LANES), jnp.int32),
            pltpu.SemaphoreType.DMA((1,)),
            pltpu.SemaphoreType.DMA((1,)),
            pltpu.SemaphoreType.DMA((1,)),
            pltpu.SemaphoreType.DMA((1,)),
            pltpu.SemaphoreType.DMA((1,)),
            pltpu.SemaphoreType.DMA((groups,)),
            pltpu.SemaphoreType.DMA((groups,)),
            pltpu.SemaphoreType.DMA((11,)),
        ],
        compiler_params=pltpu.CompilerParams(
            collective_id=0, has_side_effects=True, vmem_limit_bytes=24 << 20
        ),
        name="middle",
    )(lon_count, *[in_hbm(x) for x in (stiffness, wave_order, grid, weights)])
    return pl.pallas_call(
        functools.partial(inverse_kernel, wave_count),
        out_shape=(
            jax.ShapeDtypeStruct(grid.shape, F32),
            jax.ShapeDtypeStruct((levels, 1, lon_slots), F32),
        ),
        in_specs=[smem, vmem, vmem],
        out_specs=(vmem, vmem),
        scratch_shapes=[pltpu.VMEM((16, long_rows), F32)],
        compiler_params=pltpu.CompilerParams(vmem_limit_bytes=24 << 20),
        name="inverse",
    )(lon_count, left, table)


M = 768
FIELDS = 2
LEVELS = 4
K = 384


exact_mode = lax.Precision.HIGHEST


def general_device(grid, lon_count, wave_order, legendre, stiffness):
    lon_slots = grid.shape[3]
    rows_per = FIELDS * LEVELS
    channels = 2 * rows_per
    inner_width = 64
    wave_blocks = M // inner_width
    band_count = lax.axis_size("wave")
    slot_dev = M // (2 * band_count)
    cycle_length = lon_count[0]
    longitudes = jnp.arange(lon_slots, dtype=jnp.int32)
    wavenumbers = jnp.arange(M, dtype=jnp.int32)
    angle_step = 2.0 * jnp.pi / cycle_length.astype(jnp.float32)
    block_starts = jnp.arange(wave_blocks, dtype=jnp.int32) * inner_width
    inner_waves = jnp.arange(inner_width, dtype=jnp.int32)
    outer_angle = angle_step * (block_starts[:, None] * longitudes[None, :] % cycle_length).astype(
        jnp.float32
    )
    outer_cos = jnp.cos(outer_angle)
    outer_sin = jnp.sin(outer_angle)
    inner_angle = angle_step * (longitudes[:, None] * inner_waves[None, :] % cycle_length).astype(
        jnp.float32
    )
    inner_table = jnp.concatenate([jnp.cos(inner_angle), jnp.sin(inner_angle)], axis=1)
    cycle_scale = 1.0 / jnp.sqrt(cycle_length.astype(jnp.float32))
    live_points = longitudes < cycle_length
    wave_live = 2 * wavenumbers < cycle_length
    cycle_rows = jnp.where(live_points[None, :], grid[:, :, 0, :].reshape(rows_per, lon_slots), 0.0)
    modulated = jnp.stack(
        [cycle_rows[:, None, :] * outer_cos[None], -(cycle_rows[:, None, :] * outer_sin[None])]
    )
    product = jnp.dot(
        modulated.reshape(2 * rows_per * wave_blocks, lon_slots), inner_table, precision=exact_mode
    )
    product = product.reshape(2, rows_per, wave_blocks, 2 * inner_width)
    real_part = product[0, :, :, :inner_width] + product[1, :, :, inner_width:]
    imag_part = product[1, :, :, :inner_width] - product[0, :, :, inner_width:]
    fourier = jnp.stack([real_part, imag_part]).reshape(channels, M) * cycle_scale
    fourier = jnp.where(wave_live[None, :], fourier, 0.0)
    slotted = fourier[:, wave_order].reshape(channels, band_count, 2, slot_dev)
    side_index = lax.axis_index("fld")
    arrived = lax.all_to_all(
        lax.all_to_all(slotted[None, :, None], "wave", split_axis=3, concat_axis=2, tiled=True),
        "fld",
        split_axis=4,
        concat_axis=0,
        tiled=True,
    )
    stacked = arrived.reshape(2, channels, band_count, slot_dev)
    even_part = (stacked[0] + stacked[1]).astype(jnp.bfloat16)
    odd_part = (stacked[0] - stacked[1]).astype(jnp.bfloat16)
    parities = jnp.stack([even_part, odd_part])
    weights = legendre[:, 0]
    owner_index = lax.axis_index("wave") * 2 + side_index
    my_waves = lax.dynamic_slice_in_dim(wave_order, owner_index * slot_dev, slot_dev)
    degrees = (
        my_waves[:, None, None]
        + 2 * jnp.arange(K, dtype=jnp.int32)[None, None, :]
        + jnp.arange(2, dtype=jnp.int32)[None, :, None]
    )
    valid_degree = degrees < M
    spectral = jnp.einsum("aqwk,qcwa->aqck", weights, parities, preferred_element_type=jnp.float32)
    spectral = jnp.where(valid_degree[:, :, None, :], spectral, 0.0)
    chan_stiff = jnp.tile(jnp.repeat(stiffness, LEVELS), 2)
    degree_float = degrees.astype(jnp.float32)
    degree_ratio = degree_float * (degree_float + 1.0) / (M * (M - 1))
    summed = lax.psum(spectral, "hemi")
    damped = (
        summed / (1.0 + chan_stiff[None, None, :, None] * degree_ratio[:, :, None, :])
    ).astype(jnp.bfloat16)
    returned = jnp.einsum("aqwk,aqck->qcwa", weights, damped, preferred_element_type=jnp.float32)
    north_vals = returned[0] + returned[1]
    south_vals = returned[0] - returned[1]
    homebound = lax.all_to_all(
        lax.all_to_all(
            jnp.stack([north_vals, south_vals])[:, None, None],
            "wave",
            split_axis=4,
            concat_axis=2,
            tiled=True,
        ),
        "fld",
        split_axis=0,
        concat_axis=1,
        tiled=True,
    )
    homebound = homebound.reshape(2, band_count, channels, slot_dev)
    slot_values = jnp.transpose(homebound, (2, 1, 0, 3)).reshape(channels, M)
    spectra = jnp.zeros((channels, M), jnp.float32).at[:, wave_order].set(slot_values)
    weight_wave = jnp.where(wavenumbers == 0, 1.0, 2.0) * jnp.where(wave_live, cycle_scale, 0.0)
    real_coef = spectra[:rows_per] * weight_wave
    imag_coef = spectra[rows_per:] * weight_wave
    wave_ratio = wavenumbers.astype(jnp.float32) / M
    cos_coef = jnp.stack([real_coef, -(imag_coef * wave_ratio)]).reshape(
        2 * rows_per, wave_blocks, inner_width
    )
    sin_coef = jnp.stack([imag_coef, real_coef * wave_ratio]).reshape(
        2 * rows_per, wave_blocks, inner_width
    )
    left_rows = jnp.stack(
        [
            jnp.concatenate([cos_coef, -sin_coef], axis=2),
            jnp.concatenate([sin_coef, cos_coef], axis=2),
        ]
    )
    cycle_sums = lax.dot_general(
        left_rows.reshape(4 * rows_per * wave_blocks, 2 * inner_width),
        inner_table,
        (((1,), (1,)), ((), ())),
        precision=exact_mode,
    )
    cycle_sums = cycle_sums.reshape(2, 2 * rows_per, wave_blocks, lon_slots)
    values = jnp.sum(cycle_sums[0] * outer_cos[None] - cycle_sums[1] * outer_sin[None], axis=1)
    values = jnp.where(live_points[None, :], values, 0.0)
    smooth_rows = values[:rows_per].reshape(FIELDS, LEVELS, lon_slots)
    slope_rows = values[rows_per:].reshape(FIELDS, LEVELS, lon_slots)
    bracket = smooth_rows[0] * slope_rows[1] - smooth_rows[1] * slope_rows[0]
    return (smooth_rows[:, :, None, :], bracket[:, None, :])


def solution(mesh):
    axes = (mesh.shape["wave"], mesh.shape["hemi"], mesh.shape["fld"])
    bands, hemis, sides = axes
    placed = (
        P(None, None, ("wave", "hemi", "fld"), None),
        P(("wave", "hemi", "fld")),
        P(),
        P(("wave", "fld"), "hemi", None, None, None),
        P(),
    )
    fits = bands == 8 and hemis == 2 and sides == 2 and M == 24 * bands * hemis * sides
    step = functools.partial(fast_device, axes) if fits else general_device
    return jax.shard_map(
        step,
        mesh=mesh,
        in_specs=placed,
        out_specs=(
            P(None, None, ("wave", "hemi", "fld"), None),
            P(None, ("wave", "hemi", "fld"), None),
        ),
        check_vma=False,
    )
```

```python
import functools
import math

import jax
import jax.numpy as jnp
from jax import lax
from jax.experimental import pallas as pl
from jax.experimental.pallas import tpu as pltpu
from jax.sharding import PartitionSpec as P

LANES = 128
SUB = 8
HALF = LANES // 2
F32 = jnp.float32
BF16 = jnp.bfloat16
NN = (((1,), (0,)), ((), ()))
NT = (((1,), (1,)), ((), ()))
TN = (((0,), (0,)), ((), ()))
MESH = pl.DeviceIdType.MESH


def round_up(value, step):
    return -(-value // step) * step


def mxu(a, b, dims=NN):
    return lax.dot_general(a, b, dims, preferred_element_type=F32)


def split(x):
    high = x.astype(BF16)
    return high, (x - high.astype(F32)).astype(BF16)


def iota(shape, axis):
    return lax.broadcasted_iota(jnp.int32, shape, axis)


def sine_turn(x):
    y = x * x
    total = jnp.full_like(y, 0.0)
    for power in (13, 11, 9, 7, 5, 3, 1):
        sign = 1.0 if power % 4 == 1 else -1.0
        total = total * y + sign * (2.0 * math.pi) ** power / math.factorial(power)
    return total * x


def turn_tables(steps, period):
    inverse = 1.0 / period
    rest = steps - jnp.floor(steps * inverse) * period
    turn = rest * inverse
    turn = turn - jnp.floor(turn + 0.5)
    shifted = turn - 0.25
    shifted = jnp.where(shifted < -0.5, shifted + 1.0, shifted)
    return sine_turn(0.25 - jnp.abs(turn)), sine_turn(0.25 - jnp.abs(shifted))


def length_of(lon_ref):
    count = lon_ref[0]
    return count, lax.shift_right_logical(count, 2), jnp.full((1, 1), count.astype(F32), F32)


def fold_tables(n_float, quarter):
    steps = iota((8, quarter), 0) * iota((8, quarter), 1)
    return turn_tables(steps.astype(F32), n_float)


def roll_lanes(x, amount):
    amount = amount % x.shape[1]
    return x if amount == 0 else pltpu.roll(x, amount, 1)


def lane_gather(tile, index):
    return jnp.take_along_axis(tile, index, axis=1, mode="promise_in_bounds")


def window_at(tiles, start, most, count):
    whole = lax.shift_right_logical(start, 7)
    bits = (most // LANES).bit_length()
    for bit in reversed(range(bits)):
        step = 1 << bit
        keep = count + step
        hit = jnp.full(tiles[0].shape, whole, jnp.int32) & step != 0
        tiles = [
            jnp.where(hit, tiles[i + step], tiles[i]) if i + step < len(tiles) else tiles[i]
            for i in range(min(keep, len(tiles)))
        ]
    lane = iota(tiles[0].shape, 1) + jnp.full(tiles[0].shape, start & (LANES - 1), jnp.int32)
    index = lane & (LANES - 1)
    turned = [lane_gather(tile, index) for tile in tiles[: count + 1]]
    inside = lane < LANES
    return jnp.concatenate(
        [jnp.where(inside, turned[i], turned[i + 1]) for i in range(count)], axis=1
    )


def half_low(shape):
    return iota(shape, 1) < HALF


def wave_of(tile, shape):
    lane = iota(shape, 1)
    if tile < 4:
        return 4 * lane + tile
    step = jnp.where(lane < HALF, lane, lane - HALF)
    return 4 * (LANES + step) + 2 * (tile - 4) + jnp.where(lane < HALF, 0, 1)


def pick(tiles, tile_id, lane_id):
    out = None
    for i, tile in enumerate(tiles):
        moved = lane_gather(tile, lane_id)
        out = moved if out is None else jnp.where(tile_id == i, moved, out)
    return out


def slot_waves(wave_row, owners):
    row = jnp.broadcast_to(wave_row.astype(F32), (SUB, wave_row.shape[1]))
    tiles = [row[:, i * LANES : (i + 1) * LANES] for i in range(row.shape[1] // LANES)]
    slots = row.shape[1] // owners
    lane = iota((SUB, LANES), 1)
    out = []
    for group in range(slots // SUB):
        for part in range(owners // 16):
            slot = (part * 16 + lane // SUB) * slots + group * SUB + lane % SUB
            first = part * 16 * slots // LANES
            last = ((part * 16 + 15) * slots + group * SUB + SUB - 1) // LANES
            out.append(pick(tiles[first : last + 1], slot // LANES - first, slot % LANES))
    return out


def build_tables(lon_ref, rows, table_ref, low_table, pieces, lon_slots):
    quarter = table_ref.shape[1]
    waves4 = table_ref.shape[0] // 2
    _, fourth, _ = length_of(lon_ref)
    fourth_float = jnp.full((1, 1), fourth.astype(F32), F32)
    c_steps = iota((waves4, LANES), 0)
    lane_steps = iota((waves4, LANES), 1)
    near_cos, near_sin = turn_tables((c_steps * lane_steps).astype(F32), fourth_float)
    far_cos, far_sin = turn_tables((c_steps * lane_steps * LANES).astype(F32), fourth_float)
    rest = waves4 - LANES
    for block in range(quarter // LANES):
        fc, fs = far_cos[:, block : block + 1], far_sin[:, block : block + 1]
        cols = pl.ds(block * LANES, LANES)
        for part, value in enumerate(
            (near_cos * fc - near_sin * fs, near_cos * fs + near_sin * fc)
        ):
            high, low = split(value)
            for ref, half in ((table_ref, high), (low_table, low)):
                ref[pl.ds(part * LANES, LANES), cols] = half[:LANES]
                ref[pl.ds(2 * LANES + part * rest, rest), cols] = half[LANES:]


def forward_stage(lon_ref, rows, table_ref, low_table, waves, flip, send_ref, lon_slots):
    quarter = table_ref.shape[1]
    count, fourth, n_float = length_of(lon_ref)
    live = iota((8, quarter), 1) < fourth
    tiles = [rows[:, i * LANES : (i + 1) * LANES] for i in range(rows.shape[1] // LANES)]
    parts = [rows[:, :quarter]]
    for a in range(1, 4):
        parts.append(window_at(tiles, fourth * a, a * (lon_slots // 4), quarter // LANES))
    x0, x1, x2, x3 = [jnp.where(live, part, 0.0) for part in parts]
    fold_cos, fold_sin = fold_tables(n_float, quarter)
    c1, s1, c2, s2 = fold_cos[1:2], fold_sin[1:2], fold_cos[2:3], fold_sin[2:3]
    c3, s3 = fold_cos[3:4], fold_sin[3:4]
    a02, d02, a13, d13 = x0 + x2, x0 - x2, x1 + x3, x1 - x3
    even = a02 - a13
    z = jnp.concatenate(
        [
            a02 + a13,
            d02 * c1 - d13 * s1,
            even * c2,
            d02 * c3 + d13 * s3,
            jnp.zeros_like(x0),
            -d13 * c1 - d02 * s1,
            -even * s2,
            d13 * c3 - d02 * s3,
        ],
        axis=0,
    )
    z_high, z_low = split(z)
    both = mxu(jnp.concatenate([z_high, z_low], axis=0), table_ref[...], NT)
    total = both[:64] + both[64:] + mxu(z_high, low_table[...], NT)
    t0, t1, t2 = (total[:, i * LANES : (i + 1) * LANES] for i in range(3))
    near = [t0[:32] + t1[32:], t0[32:] - t1[:32]]
    turned = roll_lanes(t2, HALF)
    low = half_low((32, LANES))
    far = [
        jnp.where(low, t2[:32], turned[:32]) + jnp.where(low, turned[32:], t2[32:]),
        jnp.where(low, t2[32:], turned[32:]) - jnp.where(low, turned[:32], t2[:32]),
    ]
    scale = 1.0 / jnp.sqrt(n_float)
    low = half_low((8, LANES))
    sources = []
    for tile in range(6):
        if tile < 4:
            halves = [part[8 * tile : 8 * tile + 8] for part in near]
        else:
            r = 2 * (tile - 4)
            halves = [
                jnp.where(low, part[8 * r : 8 * r + 8], part[8 * r + 8 : 8 * r + 16])
                for part in far
            ]
        keep = 2 * wave_of(tile, (8, LANES)) < count
        sources.append([jnp.where(keep, half * scale, 0.0) for half in halves])
    moved = []
    for wave in waves:
        m = wave.astype(jnp.int32)
        r, c = m % 4, m // 4
        tile_id = jnp.where(c < LANES, r, 4 + r // 2)
        lane_id = jnp.where(c < LANES, c, c - LANES + HALF * (r % 2))
        for part in range(2):
            moved.append(pick([source[part] for source in sources], tile_id, lane_id))
    moved.append(jnp.zeros((LANES - 8 * len(moved), LANES), F32))
    flip[...] = jnp.concatenate(moved, axis=0).T
    lane_block = iota((16, LANES), 1) // 16
    lines = [flip[pl.ds(s, 16, stride=SUB), :] for s in range(SUB)]
    for t in range(len(waves)):
        out = None
        for s in range(SUB):
            line = roll_lanes(lines[s], 16 * (s - t))
            out = line if out is None else jnp.where(lane_block == s, line, out)
        send_ref[pl.ds(16 * SUB * (t % 2) + t // 2, 16, stride=SUB), :] = out


def home_lines(back_recv, flip, tile_count):
    lane_block = iota((16, LANES), 1) // 16
    lines = [
        back_recv[pl.ds(16 * SUB * (t % 2) + t // 2, 16, stride=SUB), :] for t in range(tile_count)
    ]
    for s in range(SUB):
        out = jnp.zeros((16, LANES), F32)
        for t in range(tile_count):
            out = jnp.where(lane_block == t, roll_lanes(lines[t], 16 * (t - s)), out)
        flip[pl.ds(s, 16, stride=SUB), :] = out
    turned = flip[...].T
    return [
        [turned[16 * t + 8 * part : 16 * t + 8 * part + 8] for t in range(tile_count)]
        for part in range(2)
    ]


def find_places(waves, places):
    stacked = jnp.concatenate(
        [wave[0:1] for wave in waves] + [jnp.zeros((LANES - len(waves), LANES), F32)], axis=0
    ).T
    place = iota((LANES, LANES), 0).astype(F32)
    for tile in range(6):
        want = wave_of(tile, (LANES, LANES)).astype(F32)
        total = jnp.zeros((LANES, LANES), F32)
        for t in range(len(waves)):
            total = jnp.where(stacked[:, t : t + 1] == want, place + float(LANES * t), total)
        places[pl.ds(tile * SUB, SUB), :] = jnp.broadcast_to(
            jnp.sum(total, axis=0, keepdims=True), (SUB, LANES)
        ).astype(jnp.int32)


def damping_table(wave_count, stiff_ref, wave_ref, first, damp):
    groups, k_count, width = damp.shape
    lane = iota((SUB, width), 1)
    field = lane // 4 % 2
    stiff = jnp.where(field == 0, stiff_ref[0], stiff_ref[1])
    for g in range(groups):
        wave = lane // LANES
        for s in range(SUB):
            wave = wave + jnp.where(lane // 16 % SUB == s, wave_ref[first + g * SUB + s], 0)
        degrees = wave[0:1] + 2 * iota((k_count, width), 0)
        degree_float = degrees.astype(F32)
        ratio = degree_float * (degree_float + 1.0) / (wave_count * (wave_count - 1))
        damp[g] = jnp.where(degrees < wave_count, 1.0 / (1.0 + stiff[0:1] * ratio), 0.0)


def left_lines(count, wave_count, sources, places, left_ref):
    low = half_low((16, LANES))
    near_re, near_im, far_re, far_im = [], [], [], []
    for tile in range(6):
        code = places[pl.ds(tile * SUB, SUB), :]
        tile_id, lane_id = code // LANES, code % LANES
        m = wave_of(tile, (8, LANES))
        weight = jnp.where(2 * m < count, jnp.where(m == 0, 1.0, 2.0), 0.0)
        steep = m.astype(F32) / wave_count
        real, imag = (pick(part, tile_id, lane_id) * weight for part in sources)
        cre = jnp.concatenate([real, -imag * steep], axis=0)
        cim = jnp.concatenate([imag, real * steep], axis=0)
        if tile < 4:
            near_re.append(cre)
            near_im.append(cim)
        else:
            cre_turned, cim_turned = roll_lanes(cre, HALF), roll_lanes(cim, HALF)
            far_re += [jnp.where(low, cre, -cim_turned), jnp.where(low, cre_turned, -cim)]
            far_im += [jnp.where(low, cim, cre_turned), jnp.where(low, cim_turned, cre)]
    lines = [
        jnp.concatenate([near_re[r], -near_im[r], far_re[r]], axis=1) for r in range(4)
    ] + [jnp.concatenate([near_im[r], near_re[r], far_im[r]], axis=1) for r in range(1, 4)]
    for at, line in enumerate(lines):
        left_ref[pl.ds(16 * at, 16), :] = line.astype(BF16)


def middle_kernel(
    axes, wave_count, lon_ref, stiff_hbm, wave_hbm, grid_ref, legendre_ref,
    left_ref, table_ref,
    stiff_ref, wave_ref, wave_row_ref, rows, low_table, flip, send_ref, recv, back_send, back_recv,
    weights, damp, places,
    send_sem, recv_sem, back_send_sem, back_recv_sem, own_sem, swap_send_sem, swap_recv_sem, in_sem,
):
    bands, hemis, sides = axes
    devices = bands * hemis * sides
    w, h, f = lax.axis_index("wave"), lax.axis_index("hemi"), lax.axis_index("fld")
    owner = (w * sides + f) * hemis + h
    groups = weights.shape[0]
    lon_slots = grid_ref.shape[3]
    first = owner * groups * SUB

    def partner(i):
        iz, ix, ih, side = i // 8, i // 4 % 2, i // 2 % 2, i % 2
        z, x = w // 2, lax.rem(w, 2)
        pz = (z, z + 1 - 2 * lax.rem(z, 2), lax.rem(z + 2, 4), 3 - z)[iz]
        px = 1 - x if ix else x
        return pz * 2 + px, (1 - h if ih else h), (1 - f if side else f), ih

    far_first = sorted(
        range(1, devices), key=lambda i: -(i // 8 + i // 4 % 2 + i // 2 % 2 + 0.1 * (i % 2))
    )
    barrier = pltpu.get_barrier_semaphore()
    for i in far_first:
        pl.semaphore_signal(barrier, inc=1, device_id=partner(i)[:3], device_id_type=MESH)

    wave_row_in = pltpu.make_async_copy(wave_hbm, wave_row_ref, in_sem.at[0])
    wave_in = pltpu.make_async_copy(wave_hbm, wave_ref, in_sem.at[1])
    stiff_in = pltpu.make_async_copy(stiff_hbm, stiff_ref, in_sem.at[2])
    wave_row_in.start()
    grid_in = [
        pltpu.make_async_copy(
            grid_ref.at[r // grid_ref.shape[1], r % grid_ref.shape[1]],
            rows.at[pl.ds(r, 1), pl.ds(0, lon_slots)],
            in_sem.at[3 + r],
        )
        for r in range(8)
    ]
    for copy in grid_in:
        copy.start()
    own_in = pltpu.make_async_copy(
        legendre_ref.at[h], weights.at[:, pl.ds(0, LANES)], own_sem.at[0]
    )
    own_in.start()
    wave_in.start()
    stiff_in.start()
    rows[:, pl.ds(lon_slots, rows.shape[1] - lon_slots)] = jnp.zeros(
        (8, rows.shape[1] - lon_slots), F32
    )
    swap = [
        pltpu.make_async_remote_copy(
            src_ref=legendre_ref.at[1 - h, g],
            dst_ref=weights.at[g, pl.ds(LANES, LANES)],
            send_sem=swap_send_sem.at[g],
            recv_sem=swap_recv_sem.at[g],
            device_id=(w, 1 - h, f),
            device_id_type=MESH,
        )
        for g in range(groups)
    ]
    late = w // 2 + lax.rem(w, 2) + h >= 4

    @pl.when(late)
    def _():
        pl.semaphore_wait(barrier, devices - 1)
        for copy in swap[:1]:
            copy.start()

    build_tables(lon_ref, rows, table_ref, low_table, None, lon_slots)
    wave_row_in.wait()
    waves = slot_waves(wave_row_ref[...].reshape(1, -1), devices)
    for copy in grid_in:
        copy.wait()
    forward_stage(lon_ref, rows, table_ref, low_table, waves, flip, send_ref, lon_slots)

    def slice_of(ref, place):
        return ref.at[pl.ds(pl.multiple_of(place * SUB, SUB), groups)]

    def everything(ref):
        return ref.at[pl.ds(0, (devices - 1) * groups)]

    def copies(source, target, source_place, target_place, sent, got):
        return [
            pltpu.make_async_remote_copy(
                src_ref=slice_of(source, source_place(*partner(i))),
                dst_ref=slice_of(target, target_place(*partner(i))),
                send_sem=sent.at[0],
                recv_sem=got.at[0],
                device_id=partner(i)[:3],
                device_id_type=MESH,
            )
            for i in far_first
        ]

    def whole(source, target, sent, got):
        return pltpu.make_async_remote_copy(
            src_ref=everything(source),
            dst_ref=everything(target),
            send_sem=sent.at[0],
            recv_sem=got.at[0],
            device_id=partner(1)[:3],
            device_id_type=MESH,
        )

    out_copies = copies(
        send_ref,
        recv,
        lambda pw, ph, pf, ih: (pw * sides + pf) * hemis + ph,
        lambda pw, ph, pf, ih: ih * 2 * bands + f * bands + w,
        send_sem,
        recv_sem,
    )
    out_whole = whole(send_ref, recv, send_sem, recv_sem)
    @pl.when(jnp.logical_not(late))
    def _():
        pl.semaphore_wait(barrier, devices - 1)

    for copy in out_copies:
        copy.start()

    @pl.when(jnp.logical_not(late))
    def _():
        for copy in swap[:1]:
            copy.start()

    for copy in swap[1:]:
        copy.start()
    slice_of(recv, f * bands + w)[...] = slice_of(send_ref, owner)[...]
    wave_in.wait()
    stiff_in.wait()
    damping_table(wave_count, stiff_ref, wave_ref, first, damp)
    find_places(waves, places)
    own_in.wait()
    out_whole.wait_recv()

    lane_slot = iota((SUB, LANES), 1) // 16
    zero = jnp.zeros((SUB, LANES), F32)
    for g in range(groups):
        blocks = []
        for rel in range(hemis):
            base = rel * 2 * bands * SUB + g
            north = recv[pl.ds(base, bands, stride=SUB), :]
            south = recv[pl.ds(base + bands * SUB, bands, stride=SUB), :]
            even, odd = north + south, north - south
            for s in range(SUB):
                blocks.append(
                    jnp.concatenate([jnp.where(lane_slot == s, even, 0.0), zero], axis=1)
                )
                blocks.append(
                    jnp.concatenate([zero, jnp.where(lane_slot == s, odd, 0.0)], axis=1)
                )
        spaced = jnp.concatenate(blocks, axis=0).astype(BF16)
        swap[g].wait_recv()
        spectral = mxu(weights[g], spaced, TN)
        damped = (spectral * damp[g]).astype(BF16)
        full = mxu(weights[g], damped)
        for rel in range(hemis):
            sums = []
            for q in range(2):
                total = None
                for s in range(SUB):
                    at = rel * LANES + s * 16 + q * SUB
                    piece = full[at : at + SUB, q * LANES : (q + 1) * LANES]
                    total = piece if total is None else jnp.where(lane_slot == s, piece, total)
                sums.append(total)
            base = rel * 2 * bands * SUB + g
            back_send[pl.ds(base, bands, stride=SUB), :] = sums[0] + sums[1]
            back_send[pl.ds(base + bands * SUB, bands, stride=SUB), :] = sums[0] - sums[1]

    home_copies = copies(
        back_send,
        back_recv,
        lambda pw, ph, pf, ih: ih * 2 * bands + pf * bands + pw,
        lambda pw, ph, pf, ih: owner,
        back_send_sem,
        back_recv_sem,
    )
    home_whole = whole(back_send, back_recv, back_send_sem, back_recv_sem)
    for copy in home_copies:
        copy.start()
    slice_of(back_recv, owner)[...] = slice_of(back_send, f * bands + w)[...]
    home_whole.wait_recv()
    sources = home_lines(back_recv, flip, len(waves))
    left_lines(lon_ref[0], wave_count, sources, places, left_ref)
    for copy in swap:
        copy.wait_send()
    out_whole.wait_send()
    home_whole.wait_send()


def inverse_kernel(wave_count, lon_ref, left_ref, table_ref, smooth_ref, bracket_ref, acc):
    fields, levels, _, lon_slots = smooth_ref.shape
    quarter = table_ref.shape[1]
    count, fourth, n_float = length_of(lon_ref)
    acc[...] = jnp.zeros_like(acc)
    fold_cos, fold_sin = fold_tables(n_float, quarter)
    sums = mxu(left_ref[...], table_ref[...])
    re = [sums[16 * r : 16 * r + 16] for r in range(4)]
    im = [None] + [sums[48 + 16 * r : 64 + 16 * r] for r in range(1, 4)]
    cos = [fold_cos[r : r + 1] for r in range(4)]
    sin = [fold_sin[r : r + 1] for r in range(4)]
    h0 = re[0]
    h1r, h1i = re[1] * cos[1] - im[1] * sin[1], re[1] * sin[1] + im[1] * cos[1]
    h2 = re[2] * cos[2] - im[2] * sin[2]
    h3r, h3i = re[3] * cos[3] - im[3] * sin[3], re[3] * sin[3] + im[3] * cos[3]
    even, odd, cross, turn = h0 + h2, h0 - h2, h1r + h3r, h3i - h1i
    live = iota((16, quarter), 1) < fourth
    scale = 1.0 / jnp.sqrt(n_float)
    width = quarter + LANES
    for a, value in enumerate((even + cross, odd + turn, even - cross, odd - turn)):
        value = jnp.where(live, value * scale, 0.0)
        smooth, slope = value[0:8], value[8:16]
        flipped = jnp.concatenate([slope[4:8], slope[0:4]], axis=0)
        product = smooth * flipped
        bracket = product - jnp.concatenate([product[4:8], product[0:4]], axis=0)
        segment = jnp.concatenate([smooth, bracket], axis=0)
        segment = jnp.concatenate([segment, jnp.zeros((16, LANES), F32)], axis=1)
        start = fourth * a
        segment = pltpu.roll(segment, lax.rem(start, LANES), 1)
        aligned = pl.multiple_of((start // LANES) * LANES, LANES)
        acc[:, pl.ds(aligned, width)] += segment
    for f in range(fields):
        for l in range(levels):
            smooth_ref[f, l] = acc[pl.ds(f * levels + l, 1), pl.ds(0, lon_slots)]
    for l in range(levels):
        bracket_ref[l] = acc[pl.ds(8 + l, 1), pl.ds(0, lon_slots)]


def in_hbm(x):
    return pltpu.with_memory_space_constraint(x, pltpu.HBM)


def fast_device(axes, grid, lon_count, wave_order, legendre, stiffness):
    bands, hemis, sides = axes
    owners = bands * hemis * sides
    wave_count = wave_order.shape[0]
    fields, levels, _, lon_slots = grid.shape
    groups = wave_count // owners // SUB
    k_count = legendre.shape[4]
    quarter = round_up(lon_slots // 4, LANES)
    waves4 = wave_count // 4
    long_rows = lon_slots + 2 * LANES
    smem = pl.BlockSpec(memory_space=pltpu.SMEM)
    vmem = pl.BlockSpec(memory_space=pltpu.VMEM)
    hbm = pl.BlockSpec(memory_space=pltpu.HBM)
    weights = legendre.reshape(hemis, groups, LANES, k_count)
    message = pltpu.VMEM((owners * SUB, LANES), F32)
    left, table = pl.pallas_call(
        functools.partial(middle_kernel, axes, wave_count),
        out_shape=(
            pltpu.VMEM((7 * 16, 2 * waves4), BF16),
            pltpu.VMEM((2 * waves4, quarter), BF16),
        ),
        in_specs=[smem, hbm, hbm, hbm, hbm],
        out_specs=(vmem, vmem),
        scratch_shapes=[
            pltpu.SMEM(stiffness.shape, F32),
            pltpu.SMEM(wave_order.shape, jnp.int32),
            pltpu.VMEM(wave_order.shape, jnp.int32),
            pltpu.VMEM((8, long_rows), F32),
            pltpu.VMEM((2 * waves4, quarter), BF16),
            pltpu.VMEM((LANES, LANES), F32),
            message,
            message,
            message,
            message,
            pltpu.VMEM((groups, 2 * LANES, k_count), BF16),
            pltpu.VMEM((groups, k_count, 2 * LANES), F32),
            pltpu.VMEM((6 * SUB, LANES), jnp.int32),
            pltpu.SemaphoreType.DMA((1,)),
            pltpu.SemaphoreType.DMA((1,)),
            pltpu.SemaphoreType.DMA((1,)),
            pltpu.SemaphoreType.DMA((1,)),
            pltpu.SemaphoreType.DMA((1,)),
            pltpu.SemaphoreType.DMA((groups,)),
            pltpu.SemaphoreType.DMA((groups,)),
            pltpu.SemaphoreType.DMA((11,)),
        ],
        compiler_params=pltpu.CompilerParams(
            collective_id=0, has_side_effects=True, vmem_limit_bytes=24 << 20
        ),
        name="middle",
    )(lon_count, *[in_hbm(x) for x in (stiffness, wave_order, grid, weights)])
    return pl.pallas_call(
        functools.partial(inverse_kernel, wave_count),
        out_shape=(
            jax.ShapeDtypeStruct(grid.shape, F32),
            jax.ShapeDtypeStruct((levels, 1, lon_slots), F32),
        ),
        in_specs=[smem, vmem, vmem],
        out_specs=(vmem, vmem),
        scratch_shapes=[pltpu.VMEM((16, long_rows), F32)],
        compiler_params=pltpu.CompilerParams(vmem_limit_bytes=24 << 20),
        name="inverse",
    )(lon_count, left, table)


M = 768
FIELDS = 2
LEVELS = 4
K = 384


exact_mode = lax.Precision.HIGHEST


def general_device(grid, lon_count, wave_order, legendre, stiffness):
    lon_slots = grid.shape[3]
    rows_per = FIELDS * LEVELS
    channels = 2 * rows_per
    inner_width = 64
    wave_blocks = M // inner_width
    band_count = lax.axis_size("wave")
    slot_dev = M // (2 * band_count)
    cycle_length = lon_count[0]
    longitudes = jnp.arange(lon_slots, dtype=jnp.int32)
    wavenumbers = jnp.arange(M, dtype=jnp.int32)
    angle_step = 2.0 * jnp.pi / cycle_length.astype(jnp.float32)
    block_starts = jnp.arange(wave_blocks, dtype=jnp.int32) * inner_width
    inner_waves = jnp.arange(inner_width, dtype=jnp.int32)
    outer_angle = angle_step * (block_starts[:, None] * longitudes[None, :] % cycle_length).astype(
        jnp.float32
    )
    outer_cos = jnp.cos(outer_angle)
    outer_sin = jnp.sin(outer_angle)
    inner_angle = angle_step * (longitudes[:, None] * inner_waves[None, :] % cycle_length).astype(
        jnp.float32
    )
    inner_table = jnp.concatenate([jnp.cos(inner_angle), jnp.sin(inner_angle)], axis=1)
    cycle_scale = 1.0 / jnp.sqrt(cycle_length.astype(jnp.float32))
    live_points = longitudes < cycle_length
    wave_live = 2 * wavenumbers < cycle_length
    cycle_rows = jnp.where(live_points[None, :], grid[:, :, 0, :].reshape(rows_per, lon_slots), 0.0)
    modulated = jnp.stack(
        [cycle_rows[:, None, :] * outer_cos[None], -(cycle_rows[:, None, :] * outer_sin[None])]
    )
    product = jnp.dot(
        modulated.reshape(2 * rows_per * wave_blocks, lon_slots), inner_table, precision=exact_mode
    )
    product = product.reshape(2, rows_per, wave_blocks, 2 * inner_width)
    real_part = product[0, :, :, :inner_width] + product[1, :, :, inner_width:]
    imag_part = product[1, :, :, :inner_width] - product[0, :, :, inner_width:]
    fourier = jnp.stack([real_part, imag_part]).reshape(channels, M) * cycle_scale
    fourier = jnp.where(wave_live[None, :], fourier, 0.0)
    slotted = fourier[:, wave_order].reshape(channels, band_count, 2, slot_dev)
    side_index = lax.axis_index("fld")
    arrived = lax.all_to_all(
        lax.all_to_all(slotted[None, :, None], "wave", split_axis=3, concat_axis=2, tiled=True),
        "fld",
        split_axis=4,
        concat_axis=0,
        tiled=True,
    )
    stacked = arrived.reshape(2, channels, band_count, slot_dev)
    even_part = (stacked[0] + stacked[1]).astype(jnp.bfloat16)
    odd_part = (stacked[0] - stacked[1]).astype(jnp.bfloat16)
    parities = jnp.stack([even_part, odd_part])
    weights = legendre[:, 0]
    owner_index = lax.axis_index("wave") * 2 + side_index
    my_waves = lax.dynamic_slice_in_dim(wave_order, owner_index * slot_dev, slot_dev)
    degrees = (
        my_waves[:, None, None]
        + 2 * jnp.arange(K, dtype=jnp.int32)[None, None, :]
        + jnp.arange(2, dtype=jnp.int32)[None, :, None]
    )
    valid_degree = degrees < M
    spectral = jnp.einsum("aqwk,qcwa->aqck", weights, parities, preferred_element_type=jnp.float32)
    spectral = jnp.where(valid_degree[:, :, None, :], spectral, 0.0)
    chan_stiff = jnp.tile(jnp.repeat(stiffness, LEVELS), 2)
    degree_float = degrees.astype(jnp.float32)
    degree_ratio = degree_float * (degree_float + 1.0) / (M * (M - 1))
    summed = lax.psum(spectral, "hemi")
    damped = (
        summed / (1.0 + chan_stiff[None, None, :, None] * degree_ratio[:, :, None, :])
    ).astype(jnp.bfloat16)
    returned = jnp.einsum("aqwk,aqck->qcwa", weights, damped, preferred_element_type=jnp.float32)
    north_vals = returned[0] + returned[1]
    south_vals = returned[0] - returned[1]
    homebound = lax.all_to_all(
        lax.all_to_all(
            jnp.stack([north_vals, south_vals])[:, None, None],
            "wave",
            split_axis=4,
            concat_axis=2,
            tiled=True,
        ),
        "fld",
        split_axis=0,
        concat_axis=1,
        tiled=True,
    )
    homebound = homebound.reshape(2, band_count, channels, slot_dev)
    slot_values = jnp.transpose(homebound, (2, 1, 0, 3)).reshape(channels, M)
    spectra = jnp.zeros((channels, M), jnp.float32).at[:, wave_order].set(slot_values)
    weight_wave = jnp.where(wavenumbers == 0, 1.0, 2.0) * jnp.where(wave_live, cycle_scale, 0.0)
    real_coef = spectra[:rows_per] * weight_wave
    imag_coef = spectra[rows_per:] * weight_wave
    wave_ratio = wavenumbers.astype(jnp.float32) / M
    cos_coef = jnp.stack([real_coef, -(imag_coef * wave_ratio)]).reshape(
        2 * rows_per, wave_blocks, inner_width
    )
    sin_coef = jnp.stack([imag_coef, real_coef * wave_ratio]).reshape(
        2 * rows_per, wave_blocks, inner_width
    )
    left_rows = jnp.stack(
        [
            jnp.concatenate([cos_coef, -sin_coef], axis=2),
            jnp.concatenate([sin_coef, cos_coef], axis=2),
        ]
    )
    cycle_sums = lax.dot_general(
        left_rows.reshape(4 * rows_per * wave_blocks, 2 * inner_width),
        inner_table,
        (((1,), (1,)), ((), ())),
        precision=exact_mode,
    )
    cycle_sums = cycle_sums.reshape(2, 2 * rows_per, wave_blocks, lon_slots)
    values = jnp.sum(cycle_sums[0] * outer_cos[None] - cycle_sums[1] * outer_sin[None], axis=1)
    values = jnp.where(live_points[None, :], values, 0.0)
    smooth_rows = values[:rows_per].reshape(FIELDS, LEVELS, lon_slots)
    slope_rows = values[rows_per:].reshape(FIELDS, LEVELS, lon_slots)
    bracket = smooth_rows[0] * slope_rows[1] - smooth_rows[1] * slope_rows[0]
    return (smooth_rows[:, :, None, :], bracket[:, None, :])


def solution(mesh):
    axes = (mesh.shape["wave"], mesh.shape["hemi"], mesh.shape["fld"])
    bands, hemis, sides = axes
    placed = (
        P(None, None, ("wave", "hemi", "fld"), None),
        P(("wave", "hemi", "fld")),
        P(),
        P(("wave", "fld"), "hemi", None, None, None),
        P(),
    )
    fits = bands == 8 and hemis == 2 and sides == 2 and M == 24 * bands * hemis * sides
    step = functools.partial(fast_device, axes) if fits else general_device
    return jax.shard_map(
        step,
        mesh=mesh,
        in_specs=placed,
        out_specs=(
            P(None, None, ("wave", "hemi", "fld"), None),
            P(None, ("wave", "hemi", "fld"), None),
        ),
        check_vma=False,
    )
```

```python
import functools
import math

import jax
import jax.numpy as jnp
from jax import lax
from jax.experimental import pallas as pl
from jax.experimental.pallas import tpu as pltpu
from jax.sharding import PartitionSpec as P

LANES = 128
SUB = 8
HALF = LANES // 2
F32 = jnp.float32
BF16 = jnp.bfloat16
NN = (((1,), (0,)), ((), ()))
NT = (((1,), (1,)), ((), ()))
TN = (((0,), (0,)), ((), ()))
MESH = pl.DeviceIdType.MESH


def round_up(value, step):
    return -(-value // step) * step


def mxu(a, b, dims=NN):
    return lax.dot_general(a, b, dims, preferred_element_type=F32)


def split(x):
    high = x.astype(BF16)
    return high, (x - high.astype(F32)).astype(BF16)


def iota(shape, axis):
    return lax.broadcasted_iota(jnp.int32, shape, axis)


def sine_turn(x):
    y = x * x
    total = jnp.full_like(y, 0.0)
    for power in (13, 11, 9, 7, 5, 3, 1):
        sign = 1.0 if power % 4 == 1 else -1.0
        total = total * y + sign * (2.0 * math.pi) ** power / math.factorial(power)
    return total * x


def turn_tables(steps, period):
    inverse = 1.0 / period
    rest = steps - jnp.floor(steps * inverse) * period
    turn = rest * inverse
    turn = turn - jnp.floor(turn + 0.5)
    shifted = turn - 0.25
    shifted = jnp.where(shifted < -0.5, shifted + 1.0, shifted)
    return sine_turn(0.25 - jnp.abs(turn)), sine_turn(0.25 - jnp.abs(shifted))


def length_of(lon_ref):
    count = lon_ref[0]
    return count, lax.shift_right_logical(count, 2), jnp.full((1, 1), count.astype(F32), F32)


def fold_tables(n_float, quarter):
    steps = iota((8, quarter), 0) * iota((8, quarter), 1)
    return turn_tables(steps.astype(F32), n_float)


def roll_lanes(x, amount):
    amount = amount % x.shape[1]
    return x if amount == 0 else pltpu.roll(x, amount, 1)


def lane_gather(tile, index):
    return jnp.take_along_axis(tile, index, axis=1, mode="promise_in_bounds")


def window_at(tiles, start, most, count):
    whole = lax.shift_right_logical(start, 7)
    bits = (most // LANES).bit_length()
    for bit in reversed(range(bits)):
        step = 1 << bit
        keep = count + step
        hit = jnp.full(tiles[0].shape, whole, jnp.int32) & step != 0
        tiles = [
            jnp.where(hit, tiles[i + step], tiles[i]) if i + step < len(tiles) else tiles[i]
            for i in range(min(keep, len(tiles)))
        ]
    lane = iota(tiles[0].shape, 1) + jnp.full(tiles[0].shape, start & (LANES - 1), jnp.int32)
    index = lane & (LANES - 1)
    turned = [lane_gather(tile, index) for tile in tiles[: count + 1]]
    inside = lane < LANES
    return jnp.concatenate(
        [jnp.where(inside, turned[i], turned[i + 1]) for i in range(count)], axis=1
    )


def half_low(shape):
    return iota(shape, 1) < HALF


def wave_of(tile, shape):
    lane = iota(shape, 1)
    if tile < 4:
        return 4 * lane + tile
    step = jnp.where(lane < HALF, lane, lane - HALF)
    return 4 * (LANES + step) + 2 * (tile - 4) + jnp.where(lane < HALF, 0, 1)


def pick(tiles, tile_id, lane_id):
    out = None
    for i, tile in enumerate(tiles):
        moved = lane_gather(tile, lane_id)
        out = moved if out is None else jnp.where(tile_id == i, moved, out)
    return out


def slot_waves(wave_row, owners):
    row = jnp.broadcast_to(wave_row.astype(F32), (SUB, wave_row.shape[1]))
    tiles = [row[:, i * LANES : (i + 1) * LANES] for i in range(row.shape[1] // LANES)]
    slots = row.shape[1] // owners
    lane = iota((SUB, LANES), 1)
    out = []
    for group in range(slots // SUB):
        for part in range(owners // 16):
            slot = (part * 16 + lane // SUB) * slots + group * SUB + lane % SUB
            first = part * 16 * slots // LANES
            last = ((part * 16 + 15) * slots + group * SUB + SUB - 1) // LANES
            out.append(pick(tiles[first : last + 1], slot // LANES - first, slot % LANES))
    return out


def build_tables(lon_ref, rows, table_ref, low_table, pieces, lon_slots):
    quarter = table_ref.shape[1]
    waves4 = table_ref.shape[0] // 2
    _, fourth, _ = length_of(lon_ref)
    fourth_float = jnp.full((1, 1), fourth.astype(F32), F32)
    c_steps = iota((waves4, LANES), 0)
    lane_steps = iota((waves4, LANES), 1)
    near_cos, near_sin = turn_tables((c_steps * lane_steps).astype(F32), fourth_float)
    far_cos, far_sin = turn_tables((c_steps * lane_steps * LANES).astype(F32), fourth_float)
    rest = waves4 - LANES
    for block in range(quarter // LANES):
        fc, fs = far_cos[:, block : block + 1], far_sin[:, block : block + 1]
        cols = pl.ds(block * LANES, LANES)
        for part, value in enumerate(
            (near_cos * fc - near_sin * fs, near_cos * fs + near_sin * fc)
        ):
            high, low = split(value)
            for ref, half in ((table_ref, high), (low_table, low)):
                ref[pl.ds(part * LANES, LANES), cols] = half[:LANES]
                ref[pl.ds(2 * LANES + part * rest, rest), cols] = half[LANES:]


def forward_stage(lon_ref, rows, table_ref, low_table, waves, flip, send_ref, lon_slots):
    quarter = table_ref.shape[1]
    count, fourth, n_float = length_of(lon_ref)
    live = iota((8, quarter), 1) < fourth
    tiles = [rows[:, i * LANES : (i + 1) * LANES] for i in range(rows.shape[1] // LANES)]
    parts = [rows[:, :quarter]]
    for a in range(1, 4):
        parts.append(window_at(tiles, fourth * a, a * (lon_slots // 4), quarter // LANES))
    x0, x1, x2, x3 = [jnp.where(live, part, 0.0) for part in parts]
    fold_cos, fold_sin = fold_tables(n_float, quarter)
    c1, s1, c2, s2 = fold_cos[1:2], fold_sin[1:2], fold_cos[2:3], fold_sin[2:3]
    c3, s3 = fold_cos[3:4], fold_sin[3:4]
    a02, d02, a13, d13 = x0 + x2, x0 - x2, x1 + x3, x1 - x3
    even = a02 - a13
    z = jnp.concatenate(
        [
            a02 + a13,
            d02 * c1 - d13 * s1,
            even * c2,
            d02 * c3 + d13 * s3,
            jnp.zeros_like(x0),
            -d13 * c1 - d02 * s1,
            -even * s2,
            d13 * c3 - d02 * s3,
        ],
        axis=0,
    )
    z_high, z_low = split(z)
    both = mxu(jnp.concatenate([z_high, z_low], axis=0), table_ref[...], NT)
    total = both[:64] + both[64:] + mxu(z_high, low_table[...], NT)
    t0, t1, t2 = (total[:, i * LANES : (i + 1) * LANES] for i in range(3))
    near = [t0[:32] + t1[32:], t0[32:] - t1[:32]]
    turned = roll_lanes(t2, HALF)
    low = half_low((32, LANES))
    far = [
        jnp.where(low, t2[:32], turned[:32]) + jnp.where(low, turned[32:], t2[32:]),
        jnp.where(low, t2[32:], turned[32:]) - jnp.where(low, turned[:32], t2[:32]),
    ]
    scale = 1.0 / jnp.sqrt(n_float)
    low = half_low((8, LANES))
    sources = []
    for tile in range(6):
        if tile < 4:
            halves = [part[8 * tile : 8 * tile + 8] for part in near]
        else:
            r = 2 * (tile - 4)
            halves = [
                jnp.where(low, part[8 * r : 8 * r + 8], part[8 * r + 8 : 8 * r + 16])
                for part in far
            ]
        keep = 2 * wave_of(tile, (8, LANES)) < count
        sources.append([jnp.where(keep, half * scale, 0.0) for half in halves])
    moved = []
    for wave in waves:
        m = wave.astype(jnp.int32)
        r, c = m % 4, m // 4
        tile_id = jnp.where(c < LANES, r, 4 + r // 2)
        lane_id = jnp.where(c < LANES, c, c - LANES + HALF * (r % 2))
        for part in range(2):
            moved.append(pick([source[part] for source in sources], tile_id, lane_id))
    moved.append(jnp.zeros((LANES - 8 * len(moved), LANES), F32))
    flip[...] = jnp.concatenate(moved, axis=0).T
    lane_block = iota((16, LANES), 1) // 16
    lines = [flip[pl.ds(s, 16, stride=SUB), :] for s in range(SUB)]
    for t in range(len(waves)):
        out = None
        for s in range(SUB):
            line = roll_lanes(lines[s], 16 * (s - t))
            out = line if out is None else jnp.where(lane_block == s, line, out)
        send_ref[pl.ds(16 * SUB * (t % 2) + t // 2, 16, stride=SUB), :] = out


def home_lines(back_recv, flip, tile_count):
    lane_block = iota((16, LANES), 1) // 16
    lines = [
        back_recv[pl.ds(16 * SUB * (t % 2) + t // 2, 16, stride=SUB), :] for t in range(tile_count)
    ]
    for s in range(SUB):
        out = jnp.zeros((16, LANES), F32)
        for t in range(tile_count):
            out = jnp.where(lane_block == t, roll_lanes(lines[t], 16 * (t - s)), out)
        flip[pl.ds(s, 16, stride=SUB), :] = out
    turned = flip[...].T
    return [
        [turned[16 * t + 8 * part : 16 * t + 8 * part + 8] for t in range(tile_count)]
        for part in range(2)
    ]


def find_places(waves, places):
    stacked = jnp.concatenate(
        [wave[0:1] for wave in waves] + [jnp.zeros((LANES - len(waves), LANES), F32)], axis=0
    ).T
    place = iota((LANES, LANES), 0).astype(F32)
    for tile in range(6):
        want = wave_of(tile, (LANES, LANES)).astype(F32)
        total = jnp.zeros((LANES, LANES), F32)
        for t in range(len(waves)):
            total = jnp.where(stacked[:, t : t + 1] == want, place + float(LANES * t), total)
        places[pl.ds(tile * SUB, SUB), :] = jnp.broadcast_to(
            jnp.sum(total, axis=0, keepdims=True), (SUB, LANES)
        ).astype(jnp.int32)


def damping_table(wave_count, stiff_ref, wave_ref, first, damp):
    groups, k_count, width = damp.shape
    lane = iota((SUB, width), 1)
    field = lane // 4 % 2
    stiff = jnp.where(field == 0, stiff_ref[0], stiff_ref[1])
    for g in range(groups):
        wave = lane // LANES
        for s in range(SUB):
            wave = wave + jnp.where(lane // 16 % SUB == s, wave_ref[first + g * SUB + s], 0)
        degrees = wave[0:1] + 2 * iota((k_count, width), 0)
        degree_float = degrees.astype(F32)
        ratio = degree_float * (degree_float + 1.0) / (wave_count * (wave_count - 1))
        damp[g] = jnp.where(degrees < wave_count, 1.0 / (1.0 + stiff[0:1] * ratio), 0.0)


def left_lines(count, wave_count, sources, places, left_ref):
    low = half_low((16, LANES))
    near_re, near_im, far_re, far_im = [], [], [], []
    for tile in range(6):
        code = places[pl.ds(tile * SUB, SUB), :]
        tile_id, lane_id = code // LANES, code % LANES
        m = wave_of(tile, (8, LANES))
        weight = jnp.where(2 * m < count, jnp.where(m == 0, 1.0, 2.0), 0.0)
        steep = m.astype(F32) / wave_count
        real, imag = (pick(part, tile_id, lane_id) * weight for part in sources)
        cre = jnp.concatenate([real, -imag * steep], axis=0)
        cim = jnp.concatenate([imag, real * steep], axis=0)
        if tile < 4:
            near_re.append(cre)
            near_im.append(cim)
        else:
            cre_turned, cim_turned = roll_lanes(cre, HALF), roll_lanes(cim, HALF)
            far_re += [jnp.where(low, cre, -cim_turned), jnp.where(low, cre_turned, -cim)]
            far_im += [jnp.where(low, cim, cre_turned), jnp.where(low, cim_turned, cre)]
    lines = [
        jnp.concatenate([near_re[r], -near_im[r], far_re[r]], axis=1) for r in range(4)
    ] + [jnp.concatenate([near_im[r], near_re[r], far_im[r]], axis=1) for r in range(1, 4)]
    for at, line in enumerate(lines):
        left_ref[pl.ds(16 * at, 16), :] = line.astype(BF16)


def middle_kernel(
    axes, wave_count, lon_ref, stiff_hbm, wave_hbm, grid_ref, legendre_ref,
    left_ref, table_ref,
    stiff_ref, wave_ref, wave_row_ref, rows, low_table, flip, send_ref, recv, back_send, back_recv,
    weights, damp, places,
    send_sem, recv_sem, back_send_sem, back_recv_sem, own_sem, swap_send_sem, swap_recv_sem, in_sem, near_sem, all_sem,
):
    bands, hemis, sides = axes
    devices = bands * hemis * sides
    w, h, f = lax.axis_index("wave"), lax.axis_index("hemi"), lax.axis_index("fld")
    owner = (w * sides + f) * hemis + h
    groups = weights.shape[0]
    lon_slots = grid_ref.shape[3]
    first = owner * groups * SUB

    def partner(i):
        iz, ix, ih, side = i // 8, i // 4 % 2, i // 2 % 2, i % 2
        z, x = w // 2, lax.rem(w, 2)
        pz = (z, z + 1 - 2 * lax.rem(z, 2), lax.rem(z + 2, 4), 3 - z)[iz]
        px = 1 - x if ix else x
        return pz * 2 + px, (1 - h if ih else h), (1 - f if side else f), ih

    far_first = sorted(
        range(1, devices), key=lambda i: -(i // 8 + i // 4 % 2 + i // 2 % 2 + 0.1 * (i % 2))
    )
    barrier = pltpu.get_barrier_semaphore()
    greeted = [partner(i)[:2] + (0,) for i in far_first if i > 1 and i % 2 == 0]
    for device in greeted + [(w, h, 1 - f), (w, 1 - h, 1)]:
        pl.semaphore_signal(barrier, inc=1, device_id=device, device_id_type=MESH)

    wave_row_in = pltpu.make_async_copy(wave_hbm, wave_row_ref, in_sem.at[0])
    wave_in = pltpu.make_async_copy(wave_hbm, wave_ref, in_sem.at[1])
    stiff_in = pltpu.make_async_copy(stiff_hbm, stiff_ref, in_sem.at[2])
    wave_row_in.start()
    grid_in = [
        pltpu.make_async_copy(
            grid_ref.at[r // grid_ref.shape[1], r % grid_ref.shape[1]],
            rows.at[pl.ds(r, 1), pl.ds(0, lon_slots)],
            in_sem.at[3 + r],
        )
        for r in range(8)
    ]
    for copy in grid_in:
        copy.start()
    own_in = pltpu.make_async_copy(
        legendre_ref.at[h], weights.at[:, pl.ds(0, LANES)], own_sem.at[0]
    )
    own_in.start()
    wave_in.start()
    stiff_in.start()
    rows[:, pl.ds(lon_slots, rows.shape[1] - lon_slots)] = jnp.zeros(
        (8, rows.shape[1] - lon_slots), F32
    )
    build_tables(lon_ref, rows, table_ref, low_table, None, lon_slots)
    swap = [
        pltpu.make_async_remote_copy(
            src_ref=legendre_ref.at[1 - h, g],
            dst_ref=weights.at[g, pl.ds(LANES, LANES)],
            send_sem=swap_send_sem.at[g],
            recv_sem=swap_recv_sem.at[g],
            device_id=(w, 1 - h, f),
            device_id_type=MESH,
        )
        for g in range(groups)
    ]

    @pl.when(f == 1)
    def _():
        pl.semaphore_wait(barrier, hemis * sides - 1)
        pl.semaphore_signal(near_sem, inc=1, device_id=(w, h, 0), device_id_type=MESH)

    @pl.when(f == 0)
    def _():
        pl.semaphore_wait(near_sem, 1)

    for copy in swap[:1]:
        copy.start()
    wave_row_in.wait()
    waves = slot_waves(wave_row_ref[...].reshape(1, -1), devices)
    for copy in grid_in:
        copy.wait()
    forward_stage(lon_ref, rows, table_ref, low_table, waves, flip, send_ref, lon_slots)

    def slice_of(ref, place):
        return ref.at[pl.ds(pl.multiple_of(place * SUB, SUB), groups)]

    def everything(ref):
        return ref.at[pl.ds(0, (devices - 1) * groups)]

    def copies(source, target, source_place, target_place, sent, got):
        return [
            pltpu.make_async_remote_copy(
                src_ref=slice_of(source, source_place(*partner(i))),
                dst_ref=slice_of(target, target_place(*partner(i))),
                send_sem=sent.at[0],
                recv_sem=got.at[0],
                device_id=partner(i)[:3],
                device_id_type=MESH,
            )
            for i in far_first
        ]

    def whole(source, target, sent, got):
        return pltpu.make_async_remote_copy(
            src_ref=everything(source),
            dst_ref=everything(target),
            send_sem=sent.at[0],
            recv_sem=got.at[0],
            device_id=partner(1)[:3],
            device_id_type=MESH,
        )

    out_copies = copies(
        send_ref,
        recv,
        lambda pw, ph, pf, ih: (pw * sides + pf) * hemis + ph,
        lambda pw, ph, pf, ih: ih * 2 * bands + f * bands + w,
        send_sem,
        recv_sem,
    )
    out_whole = whole(send_ref, recv, send_sem, recv_sem)
    @pl.when(f == 0)
    def _():
        pl.semaphore_wait(barrier, devices - 1)
        pl.semaphore_signal(all_sem, inc=1, device_id=(w, h, 1), device_id_type=MESH)

    @pl.when(f == 1)
    def _():
        pl.semaphore_wait(all_sem, 1)

    for copy in out_copies:
        copy.start()
    for copy in swap[1:]:
        copy.start()
    slice_of(recv, f * bands + w)[...] = slice_of(send_ref, owner)[...]
    wave_in.wait()
    stiff_in.wait()
    damping_table(wave_count, stiff_ref, wave_ref, first, damp)
    find_places(waves, places)
    own_in.wait()
    out_whole.wait_recv()

    lane_slot = iota((SUB, LANES), 1) // 16
    zero = jnp.zeros((SUB, LANES), F32)
    for g in range(groups):
        blocks = []
        for rel in range(hemis):
            base = rel * 2 * bands * SUB + g
            north = recv[pl.ds(base, bands, stride=SUB), :]
            south = recv[pl.ds(base + bands * SUB, bands, stride=SUB), :]
            even, odd = north + south, north - south
            for s in range(SUB):
                blocks.append(
                    jnp.concatenate([jnp.where(lane_slot == s, even, 0.0), zero], axis=1)
                )
                blocks.append(
                    jnp.concatenate([zero, jnp.where(lane_slot == s, odd, 0.0)], axis=1)
                )
        spaced = jnp.concatenate(blocks, axis=0).astype(BF16)
        swap[g].wait_recv()
        spectral = mxu(weights[g], spaced, TN)
        damped = (spectral * damp[g]).astype(BF16)
        full = mxu(weights[g], damped)
        for rel in range(hemis):
            sums = []
            for q in range(2):
                total = None
                for s in range(SUB):
                    at = rel * LANES + s * 16 + q * SUB
                    piece = full[at : at + SUB, q * LANES : (q + 1) * LANES]
                    total = piece if total is None else jnp.where(lane_slot == s, piece, total)
                sums.append(total)
            base = rel * 2 * bands * SUB + g
            back_send[pl.ds(base, bands, stride=SUB), :] = sums[0] + sums[1]
            back_send[pl.ds(base + bands * SUB, bands, stride=SUB), :] = sums[0] - sums[1]

    home_copies = copies(
        back_send,
        back_recv,
        lambda pw, ph, pf, ih: ih * 2 * bands + pf * bands + pw,
        lambda pw, ph, pf, ih: owner,
        back_send_sem,
        back_recv_sem,
    )
    home_whole = whole(back_send, back_recv, back_send_sem, back_recv_sem)
    for copy in home_copies:
        copy.start()
    slice_of(back_recv, owner)[...] = slice_of(back_send, f * bands + w)[...]
    home_whole.wait_recv()
    sources = home_lines(back_recv, flip, len(waves))
    left_lines(lon_ref[0], wave_count, sources, places, left_ref)
    for copy in swap:
        copy.wait_send()
    out_whole.wait_send()
    home_whole.wait_send()


def inverse_kernel(wave_count, lon_ref, left_ref, table_ref, smooth_ref, bracket_ref, acc):
    fields, levels, _, lon_slots = smooth_ref.shape
    quarter = table_ref.shape[1]
    count, fourth, n_float = length_of(lon_ref)
    acc[...] = jnp.zeros_like(acc)
    fold_cos, fold_sin = fold_tables(n_float, quarter)
    sums = mxu(left_ref[...], table_ref[...])
    re = [sums[16 * r : 16 * r + 16] for r in range(4)]
    im = [None] + [sums[48 + 16 * r : 64 + 16 * r] for r in range(1, 4)]
    cos = [fold_cos[r : r + 1] for r in range(4)]
    sin = [fold_sin[r : r + 1] for r in range(4)]
    h0 = re[0]
    h1r, h1i = re[1] * cos[1] - im[1] * sin[1], re[1] * sin[1] + im[1] * cos[1]
    h2 = re[2] * cos[2] - im[2] * sin[2]
    h3r, h3i = re[3] * cos[3] - im[3] * sin[3], re[3] * sin[3] + im[3] * cos[3]
    even, odd, cross, turn = h0 + h2, h0 - h2, h1r + h3r, h3i - h1i
    live = iota((16, quarter), 1) < fourth
    scale = 1.0 / jnp.sqrt(n_float)
    width = quarter + LANES
    for a, value in enumerate((even + cross, odd + turn, even - cross, odd - turn)):
        value = jnp.where(live, value * scale, 0.0)
        smooth, slope = value[0:8], value[8:16]
        flipped = jnp.concatenate([slope[4:8], slope[0:4]], axis=0)
        product = smooth * flipped
        bracket = product - jnp.concatenate([product[4:8], product[0:4]], axis=0)
        segment = jnp.concatenate([smooth, bracket], axis=0)
        segment = jnp.concatenate([segment, jnp.zeros((16, LANES), F32)], axis=1)
        start = fourth * a
        segment = pltpu.roll(segment, lax.rem(start, LANES), 1)
        aligned = pl.multiple_of((start // LANES) * LANES, LANES)
        acc[:, pl.ds(aligned, width)] += segment
    for f in range(fields):
        for l in range(levels):
            smooth_ref[f, l] = acc[pl.ds(f * levels + l, 1), pl.ds(0, lon_slots)]
    for l in range(levels):
        bracket_ref[l] = acc[pl.ds(8 + l, 1), pl.ds(0, lon_slots)]


def in_hbm(x):
    return pltpu.with_memory_space_constraint(x, pltpu.HBM)


def fast_device(axes, grid, lon_count, wave_order, legendre, stiffness):
    bands, hemis, sides = axes
    owners = bands * hemis * sides
    wave_count = wave_order.shape[0]
    fields, levels, _, lon_slots = grid.shape
    groups = wave_count // owners // SUB
    k_count = legendre.shape[4]
    quarter = round_up(lon_slots // 4, LANES)
    waves4 = wave_count // 4
    long_rows = lon_slots + 2 * LANES
    smem = pl.BlockSpec(memory_space=pltpu.SMEM)
    vmem = pl.BlockSpec(memory_space=pltpu.VMEM)
    hbm = pl.BlockSpec(memory_space=pltpu.HBM)
    weights = legendre.reshape(hemis, groups, LANES, k_count)
    message = pltpu.VMEM((owners * SUB, LANES), F32)
    left, table = pl.pallas_call(
        functools.partial(middle_kernel, axes, wave_count),
        out_shape=(
            pltpu.VMEM((7 * 16, 2 * waves4), BF16),
            pltpu.VMEM((2 * waves4, quarter), BF16),
        ),
        in_specs=[smem, hbm, hbm, hbm, hbm],
        out_specs=(vmem, vmem),
        scratch_shapes=[
            pltpu.SMEM(stiffness.shape, F32),
            pltpu.SMEM(wave_order.shape, jnp.int32),
            pltpu.VMEM(wave_order.shape, jnp.int32),
            pltpu.VMEM((8, long_rows), F32),
            pltpu.VMEM((2 * waves4, quarter), BF16),
            pltpu.VMEM((LANES, LANES), F32),
            message,
            message,
            message,
            message,
            pltpu.VMEM((groups, 2 * LANES, k_count), BF16),
            pltpu.VMEM((groups, k_count, 2 * LANES), F32),
            pltpu.VMEM((6 * SUB, LANES), jnp.int32),
            pltpu.SemaphoreType.DMA((1,)),
            pltpu.SemaphoreType.DMA((1,)),
            pltpu.SemaphoreType.DMA((1,)),
            pltpu.SemaphoreType.DMA((1,)),
            pltpu.SemaphoreType.DMA((1,)),
            pltpu.SemaphoreType.DMA((groups,)),
            pltpu.SemaphoreType.DMA((groups,)),
            pltpu.SemaphoreType.DMA((11,)),
            pltpu.SemaphoreType.REGULAR,
            pltpu.SemaphoreType.REGULAR,
        ],
        compiler_params=pltpu.CompilerParams(
            collective_id=0, has_side_effects=True, vmem_limit_bytes=24 << 20
        ),
        name="middle",
    )(lon_count, *[in_hbm(x) for x in (stiffness, wave_order, grid, weights)])
    return pl.pallas_call(
        functools.partial(inverse_kernel, wave_count),
        out_shape=(
            jax.ShapeDtypeStruct(grid.shape, F32),
            jax.ShapeDtypeStruct((levels, 1, lon_slots), F32),
        ),
        in_specs=[smem, vmem, vmem],
        out_specs=(vmem, vmem),
        scratch_shapes=[pltpu.VMEM((16, long_rows), F32)],
        compiler_params=pltpu.CompilerParams(vmem_limit_bytes=24 << 20),
        name="inverse",
    )(lon_count, left, table)


M = 768
FIELDS = 2
LEVELS = 4
K = 384


exact_mode = lax.Precision.HIGHEST


def general_device(grid, lon_count, wave_order, legendre, stiffness):
    lon_slots = grid.shape[3]
    rows_per = FIELDS * LEVELS
    channels = 2 * rows_per
    inner_width = 64
    wave_blocks = M // inner_width
    band_count = lax.axis_size("wave")
    slot_dev = M // (2 * band_count)
    cycle_length = lon_count[0]
    longitudes = jnp.arange(lon_slots, dtype=jnp.int32)
    wavenumbers = jnp.arange(M, dtype=jnp.int32)
    angle_step = 2.0 * jnp.pi / cycle_length.astype(jnp.float32)
    block_starts = jnp.arange(wave_blocks, dtype=jnp.int32) * inner_width
    inner_waves = jnp.arange(inner_width, dtype=jnp.int32)
    outer_angle = angle_step * (block_starts[:, None] * longitudes[None, :] % cycle_length).astype(
        jnp.float32
    )
    outer_cos = jnp.cos(outer_angle)
    outer_sin = jnp.sin(outer_angle)
    inner_angle = angle_step * (longitudes[:, None] * inner_waves[None, :] % cycle_length).astype(
        jnp.float32
    )
    inner_table = jnp.concatenate([jnp.cos(inner_angle), jnp.sin(inner_angle)], axis=1)
    cycle_scale = 1.0 / jnp.sqrt(cycle_length.astype(jnp.float32))
    live_points = longitudes < cycle_length
    wave_live = 2 * wavenumbers < cycle_length
    cycle_rows = jnp.where(live_points[None, :], grid[:, :, 0, :].reshape(rows_per, lon_slots), 0.0)
    modulated = jnp.stack(
        [cycle_rows[:, None, :] * outer_cos[None], -(cycle_rows[:, None, :] * outer_sin[None])]
    )
    product = jnp.dot(
        modulated.reshape(2 * rows_per * wave_blocks, lon_slots), inner_table, precision=exact_mode
    )
    product = product.reshape(2, rows_per, wave_blocks, 2 * inner_width)
    real_part = product[0, :, :, :inner_width] + product[1, :, :, inner_width:]
    imag_part = product[1, :, :, :inner_width] - product[0, :, :, inner_width:]
    fourier = jnp.stack([real_part, imag_part]).reshape(channels, M) * cycle_scale
    fourier = jnp.where(wave_live[None, :], fourier, 0.0)
    slotted = fourier[:, wave_order].reshape(channels, band_count, 2, slot_dev)
    side_index = lax.axis_index("fld")
    arrived = lax.all_to_all(
        lax.all_to_all(slotted[None, :, None], "wave", split_axis=3, concat_axis=2, tiled=True),
        "fld",
        split_axis=4,
        concat_axis=0,
        tiled=True,
    )
    stacked = arrived.reshape(2, channels, band_count, slot_dev)
    even_part = (stacked[0] + stacked[1]).astype(jnp.bfloat16)
    odd_part = (stacked[0] - stacked[1]).astype(jnp.bfloat16)
    parities = jnp.stack([even_part, odd_part])
    weights = legendre[:, 0]
    owner_index = lax.axis_index("wave") * 2 + side_index
    my_waves = lax.dynamic_slice_in_dim(wave_order, owner_index * slot_dev, slot_dev)
    degrees = (
        my_waves[:, None, None]
        + 2 * jnp.arange(K, dtype=jnp.int32)[None, None, :]
        + jnp.arange(2, dtype=jnp.int32)[None, :, None]
    )
    valid_degree = degrees < M
    spectral = jnp.einsum("aqwk,qcwa->aqck", weights, parities, preferred_element_type=jnp.float32)
    spectral = jnp.where(valid_degree[:, :, None, :], spectral, 0.0)
    chan_stiff = jnp.tile(jnp.repeat(stiffness, LEVELS), 2)
    degree_float = degrees.astype(jnp.float32)
    degree_ratio = degree_float * (degree_float + 1.0) / (M * (M - 1))
    summed = lax.psum(spectral, "hemi")
    damped = (
        summed / (1.0 + chan_stiff[None, None, :, None] * degree_ratio[:, :, None, :])
    ).astype(jnp.bfloat16)
    returned = jnp.einsum("aqwk,aqck->qcwa", weights, damped, preferred_element_type=jnp.float32)
    north_vals = returned[0] + returned[1]
    south_vals = returned[0] - returned[1]
    homebound = lax.all_to_all(
        lax.all_to_all(
            jnp.stack([north_vals, south_vals])[:, None, None],
            "wave",
            split_axis=4,
            concat_axis=2,
            tiled=True,
        ),
        "fld",
        split_axis=0,
        concat_axis=1,
        tiled=True,
    )
    homebound = homebound.reshape(2, band_count, channels, slot_dev)
    slot_values = jnp.transpose(homebound, (2, 1, 0, 3)).reshape(channels, M)
    spectra = jnp.zeros((channels, M), jnp.float32).at[:, wave_order].set(slot_values)
    weight_wave = jnp.where(wavenumbers == 0, 1.0, 2.0) * jnp.where(wave_live, cycle_scale, 0.0)
    real_coef = spectra[:rows_per] * weight_wave
    imag_coef = spectra[rows_per:] * weight_wave
    wave_ratio = wavenumbers.astype(jnp.float32) / M
    cos_coef = jnp.stack([real_coef, -(imag_coef * wave_ratio)]).reshape(
        2 * rows_per, wave_blocks, inner_width
    )
    sin_coef = jnp.stack([imag_coef, real_coef * wave_ratio]).reshape(
        2 * rows_per, wave_blocks, inner_width
    )
    left_rows = jnp.stack(
        [
            jnp.concatenate([cos_coef, -sin_coef], axis=2),
            jnp.concatenate([sin_coef, cos_coef], axis=2),
        ]
    )
    cycle_sums = lax.dot_general(
        left_rows.reshape(4 * rows_per * wave_blocks, 2 * inner_width),
        inner_table,
        (((1,), (1,)), ((), ())),
        precision=exact_mode,
    )
    cycle_sums = cycle_sums.reshape(2, 2 * rows_per, wave_blocks, lon_slots)
    values = jnp.sum(cycle_sums[0] * outer_cos[None] - cycle_sums[1] * outer_sin[None], axis=1)
    values = jnp.where(live_points[None, :], values, 0.0)
    smooth_rows = values[:rows_per].reshape(FIELDS, LEVELS, lon_slots)
    slope_rows = values[rows_per:].reshape(FIELDS, LEVELS, lon_slots)
    bracket = smooth_rows[0] * slope_rows[1] - smooth_rows[1] * slope_rows[0]
    return (smooth_rows[:, :, None, :], bracket[:, None, :])


def solution(mesh):
    axes = (mesh.shape["wave"], mesh.shape["hemi"], mesh.shape["fld"])
    bands, hemis, sides = axes
    placed = (
        P(None, None, ("wave", "hemi", "fld"), None),
        P(("wave", "hemi", "fld")),
        P(),
        P(("wave", "fld"), "hemi", None, None, None),
        P(),
    )
    fits = bands == 8 and hemis == 2 and sides == 2 and M == 24 * bands * hemis * sides
    step = functools.partial(fast_device, axes) if fits else general_device
    return jax.shard_map(
        step,
        mesh=mesh,
        in_specs=placed,
        out_specs=(
            P(None, None, ("wave", "hemi", "fld"), None),
            P(None, ("wave", "hemi", "fld"), None),
        ),
        check_vma=False,
    )
```

```python
import functools
import math

import jax
import jax.numpy as jnp
from jax import lax
from jax.experimental import pallas as pl
from jax.experimental.pallas import tpu as pltpu
from jax.sharding import PartitionSpec as P

LANES = 128
SUB = 8
HALF = LANES // 2
F32 = jnp.float32
BF16 = jnp.bfloat16
NN = (((1,), (0,)), ((), ()))
NT = (((1,), (1,)), ((), ()))
TN = (((0,), (0,)), ((), ()))
MESH = pl.DeviceIdType.MESH


def round_up(value, step):
    return -(-value // step) * step


def mxu(a, b, dims=NN):
    return lax.dot_general(a, b, dims, preferred_element_type=F32)


def split(x):
    high = x.astype(BF16)
    return high, (x - high.astype(F32)).astype(BF16)


def iota(shape, axis):
    return lax.broadcasted_iota(jnp.int32, shape, axis)


def sine_turn(x):
    y = x * x
    total = jnp.full_like(y, 0.0)
    for power in (13, 11, 9, 7, 5, 3, 1):
        sign = 1.0 if power % 4 == 1 else -1.0
        total = total * y + sign * (2.0 * math.pi) ** power / math.factorial(power)
    return total * x


def turn_tables(steps, period):
    inverse = 1.0 / period
    rest = steps - jnp.floor(steps * inverse) * period
    turn = rest * inverse
    turn = turn - jnp.floor(turn + 0.5)
    shifted = turn - 0.25
    shifted = jnp.where(shifted < -0.5, shifted + 1.0, shifted)
    return sine_turn(0.25 - jnp.abs(turn)), sine_turn(0.25 - jnp.abs(shifted))


def length_of(lon_ref):
    count = lon_ref[0]
    return count, lax.shift_right_logical(count, 2), jnp.full((1, 1), count.astype(F32), F32)


def fold_tables(n_float, quarter):
    steps = iota((8, quarter), 0) * iota((8, quarter), 1)
    return turn_tables(steps.astype(F32), n_float)


def roll_lanes(x, amount):
    amount = amount % x.shape[1]
    return x if amount == 0 else pltpu.roll(x, amount, 1)


def lane_gather(tile, index):
    return jnp.take_along_axis(tile, index, axis=1, mode="promise_in_bounds")


def window_at(tiles, start, most, count):
    whole = lax.shift_right_logical(start, 7)
    bits = (most // LANES).bit_length()
    for bit in reversed(range(bits)):
        step = 1 << bit
        keep = count + step
        hit = jnp.full(tiles[0].shape, whole, jnp.int32) & step != 0
        tiles = [
            jnp.where(hit, tiles[i + step], tiles[i]) if i + step < len(tiles) else tiles[i]
            for i in range(min(keep, len(tiles)))
        ]
    lane = iota(tiles[0].shape, 1) + jnp.full(tiles[0].shape, start & (LANES - 1), jnp.int32)
    index = lane & (LANES - 1)
    turned = [lane_gather(tile, index) for tile in tiles[: count + 1]]
    inside = lane < LANES
    return jnp.concatenate(
        [jnp.where(inside, turned[i], turned[i + 1]) for i in range(count)], axis=1
    )


def half_low(shape):
    return iota(shape, 1) < HALF


def wave_of(tile, shape):
    lane = iota(shape, 1)
    if tile < 4:
        return 4 * lane + tile
    step = jnp.where(lane < HALF, lane, lane - HALF)
    return 4 * (LANES + step) + 2 * (tile - 4) + jnp.where(lane < HALF, 0, 1)


def pick(tiles, tile_id, lane_id):
    out = None
    for i, tile in enumerate(tiles):
        moved = lane_gather(tile, lane_id)
        out = moved if out is None else jnp.where(tile_id == i, moved, out)
    return out


def slot_waves(wave_row, owners):
    row = jnp.broadcast_to(wave_row.astype(F32), (SUB, wave_row.shape[1]))
    tiles = [row[:, i * LANES : (i + 1) * LANES] for i in range(row.shape[1] // LANES)]
    slots = row.shape[1] // owners
    lane = iota((SUB, LANES), 1)
    out = []
    for group in range(slots // SUB):
        for part in range(owners // 16):
            slot = (part * 16 + lane // SUB) * slots + group * SUB + lane % SUB
            first = part * 16 * slots // LANES
            last = ((part * 16 + 15) * slots + group * SUB + SUB - 1) // LANES
            out.append(pick(tiles[first : last + 1], slot // LANES - first, slot % LANES))
    return out


def build_tables(lon_ref, rows, table_ref, low_table, pieces, lon_slots):
    quarter = table_ref.shape[1]
    waves4 = table_ref.shape[0] // 2
    _, fourth, _ = length_of(lon_ref)
    fourth_float = jnp.full((1, 1), fourth.astype(F32), F32)
    c_steps = iota((waves4, LANES), 0)
    lane_steps = iota((waves4, LANES), 1)
    near_cos, near_sin = turn_tables((c_steps * lane_steps).astype(F32), fourth_float)
    far_cos, far_sin = turn_tables((c_steps * lane_steps * LANES).astype(F32), fourth_float)
    rest = waves4 - LANES
    for block in range(quarter // LANES):
        fc, fs = far_cos[:, block : block + 1], far_sin[:, block : block + 1]
        cols = pl.ds(block * LANES, LANES)
        for part, value in enumerate(
            (near_cos * fc - near_sin * fs, near_cos * fs + near_sin * fc)
        ):
            high, low = split(value)
            for ref, half in ((table_ref, high), (low_table, low)):
                ref[pl.ds(part * LANES, LANES), cols] = half[:LANES]
                ref[pl.ds(2 * LANES + part * rest, rest), cols] = half[LANES:]


def forward_stage(lon_ref, rows, table_ref, low_table, waves, flip, send_ref, lon_slots):
    quarter = table_ref.shape[1]
    count, fourth, n_float = length_of(lon_ref)
    live = iota((8, quarter), 1) < fourth
    tiles = [rows[:, i * LANES : (i + 1) * LANES] for i in range(rows.shape[1] // LANES)]
    parts = [rows[:, :quarter]]
    for a in range(1, 4):
        parts.append(window_at(tiles, fourth * a, a * (lon_slots // 4), quarter // LANES))
    x0, x1, x2, x3 = [jnp.where(live, part, 0.0) for part in parts]
    fold_cos, fold_sin = fold_tables(n_float, quarter)
    c1, s1, c2, s2 = fold_cos[1:2], fold_sin[1:2], fold_cos[2:3], fold_sin[2:3]
    c3, s3 = fold_cos[3:4], fold_sin[3:4]
    a02, d02, a13, d13 = x0 + x2, x0 - x2, x1 + x3, x1 - x3
    even = a02 - a13
    z = jnp.concatenate(
        [
            a02 + a13,
            d02 * c1 - d13 * s1,
            even * c2,
            d02 * c3 + d13 * s3,
            jnp.zeros_like(x0),
            -d13 * c1 - d02 * s1,
            -even * s2,
            d13 * c3 - d02 * s3,
        ],
        axis=0,
    )
    z_high, z_low = split(z)
    both = mxu(jnp.concatenate([z_high, z_low], axis=0), table_ref[...], NT)
    total = both[:64] + both[64:] + mxu(z_high, low_table[...], NT)
    t0, t1, t2 = (total[:, i * LANES : (i + 1) * LANES] for i in range(3))
    near = [t0[:32] + t1[32:], t0[32:] - t1[:32]]
    turned = roll_lanes(t2, HALF)
    low = half_low((32, LANES))
    far = [
        jnp.where(low, t2[:32], turned[:32]) + jnp.where(low, turned[32:], t2[32:]),
        jnp.where(low, t2[32:], turned[32:]) - jnp.where(low, turned[:32], t2[:32]),
    ]
    scale = 1.0 / jnp.sqrt(n_float)
    low = half_low((8, LANES))
    sources = []
    for tile in range(6):
        if tile < 4:
            halves = [part[8 * tile : 8 * tile + 8] for part in near]
        else:
            r = 2 * (tile - 4)
            halves = [
                jnp.where(low, part[8 * r : 8 * r + 8], part[8 * r + 8 : 8 * r + 16])
                for part in far
            ]
        keep = 2 * wave_of(tile, (8, LANES)) < count
        sources.append([jnp.where(keep, half * scale, 0.0) for half in halves])
    moved = []
    for wave in waves:
        m = wave.astype(jnp.int32)
        r, c = m % 4, m // 4
        tile_id = jnp.where(c < LANES, r, 4 + r // 2)
        lane_id = jnp.where(c < LANES, c, c - LANES + HALF * (r % 2))
        for part in range(2):
            moved.append(pick([source[part] for source in sources], tile_id, lane_id))
    moved.append(jnp.zeros((LANES - 8 * len(moved), LANES), F32))
    flip[...] = jnp.concatenate(moved, axis=0).T
    lane_block = iota((16, LANES), 1) // 16
    lines = [flip[pl.ds(s, 16, stride=SUB), :] for s in range(SUB)]
    for t in range(len(waves)):
        out = None
        for s in range(SUB):
            line = roll_lanes(lines[s], 16 * (s - t))
            out = line if out is None else jnp.where(lane_block == s, line, out)
        send_ref[pl.ds(16 * SUB * (t % 2) + t // 2, 16, stride=SUB), :] = out


def home_part(back_recv, flip, places, part, groups):
    lane_block = iota((16, LANES), 1) // 16
    lines = [
        back_recv[pl.ds(16 * SUB * part + g, 16, stride=SUB), :] for g in range(groups)
    ]
    for s in range(SUB):
        out = None
        for g in range(groups):
            line = roll_lanes(lines[g], 16 * (g - s))
            out = line if out is None else jnp.where(lane_block == g, line, out)
        flip[pl.ds(s, 16, stride=SUB), :] = out
    turned = flip[...].T
    picked = []
    for tile in range(6):
        code = places[pl.ds(tile * SUB, SUB), :]
        group, lane_id = code // (2 * LANES), code % LANES
        picked.append(
            [
                pick([turned[16 * g + at : 16 * g + at + 8] for g in range(groups)], group, lane_id)
                for at in (0, 8)
            ]
        )
    return picked


def find_places(waves, places):
    stacked = jnp.concatenate(
        [wave[0:1] for wave in waves] + [jnp.zeros((LANES - len(waves), LANES), F32)], axis=0
    ).T
    place = iota((LANES, LANES), 0).astype(F32)
    for tile in range(6):
        want = wave_of(tile, (LANES, LANES)).astype(F32)
        total = jnp.zeros((LANES, LANES), F32)
        for t in range(len(waves)):
            total = jnp.where(stacked[:, t : t + 1] == want, place + float(LANES * t), total)
        places[pl.ds(tile * SUB, SUB), :] = jnp.broadcast_to(
            jnp.sum(total, axis=0, keepdims=True), (SUB, LANES)
        ).astype(jnp.int32)


def damping_table(wave_count, stiff_ref, wave_ref, first, damp):
    groups, k_count, width = damp.shape
    lane = iota((SUB, width), 1)
    field = lane // 4 % 2
    stiff = jnp.where(field == 0, stiff_ref[0], stiff_ref[1])
    for g in range(groups):
        wave = lane // LANES
        for s in range(SUB):
            wave = wave + jnp.where(lane // 16 % SUB == s, wave_ref[first + g * SUB + s], 0)
        degrees = wave[0:1] + 2 * iota((k_count, width), 0)
        degree_float = degrees.astype(F32)
        ratio = degree_float * (degree_float + 1.0) / (wave_count * (wave_count - 1))
        damp[g] = jnp.where(degrees < wave_count, 1.0 / (1.0 + stiff[0:1] * ratio), 0.0)


def left_lines(count, wave_count, halves, places, left_ref):
    low = half_low((16, LANES))
    near_re, near_im, far_re, far_im = [], [], [], []
    for tile in range(6):
        first = places[pl.ds(tile * SUB, SUB), :] // LANES % 2 == 0
        m = wave_of(tile, (8, LANES))
        weight = jnp.where(2 * m < count, jnp.where(m == 0, 1.0, 2.0), 0.0)
        steep = m.astype(F32) / wave_count
        real, imag = (
            jnp.where(first, early, late) * weight
            for early, late in zip(halves[0][tile], halves[1][tile])
        )
        cre = jnp.concatenate([real, -imag * steep], axis=0)
        cim = jnp.concatenate([imag, real * steep], axis=0)
        if tile < 4:
            near_re.append(cre)
            near_im.append(cim)
        else:
            cre_turned, cim_turned = roll_lanes(cre, HALF), roll_lanes(cim, HALF)
            far_re += [jnp.where(low, cre, -cim_turned), jnp.where(low, cre_turned, -cim)]
            far_im += [jnp.where(low, cim, cre_turned), jnp.where(low, cim_turned, cre)]
    lines = [
        jnp.concatenate([near_re[r], -near_im[r], far_re[r]], axis=1) for r in range(4)
    ] + [jnp.concatenate([near_im[r], near_re[r], far_im[r]], axis=1) for r in range(1, 4)]
    for at, line in enumerate(lines):
        left_ref[pl.ds(16 * at, 16), :] = line.astype(BF16)


def middle_kernel(
    axes, wave_count, lon_ref, stiff_hbm, wave_hbm, grid_ref, legendre_ref,
    left_ref, table_ref,
    stiff_ref, wave_ref, wave_row_ref, rows, low_table, flip, send_ref, recv, back_send, back_recv,
    weights, damp, places, other_flip,
    send_sem, recv_sem, back_send_sem, back_recv_sem, own_sem, swap_send_sem, swap_recv_sem, in_sem, near_sem, all_sem,
):
    bands, hemis, sides = axes
    devices = bands * hemis * sides
    w, h, f = lax.axis_index("wave"), lax.axis_index("hemi"), lax.axis_index("fld")
    owner = (w * sides + f) * hemis + h
    groups = weights.shape[0]
    lon_slots = grid_ref.shape[3]
    first = owner * groups * SUB

    def partner(i):
        iz, ix, ih, side = i // 8, i // 4 % 2, i // 2 % 2, i % 2
        z, x = w // 2, lax.rem(w, 2)
        pz = (z, z + 1 - 2 * lax.rem(z, 2), lax.rem(z + 2, 4), 3 - z)[iz]
        px = 1 - x if ix else x
        return pz * 2 + px, (1 - h if ih else h), (1 - f if side else f), ih

    far_first = sorted(
        range(1, devices), key=lambda i: -(i // 8 + i // 4 % 2 + i // 2 % 2 + 0.1 * (i % 2))
    )
    barrier = pltpu.get_barrier_semaphore()
    greeted = [partner(i)[:2] + (0,) for i in far_first if i > 1 and i % 2 == 0]
    for device in greeted + [(w, h, 1 - f), (w, 1 - h, 1)]:
        pl.semaphore_signal(barrier, inc=1, device_id=device, device_id_type=MESH)

    wave_row_in = pltpu.make_async_copy(wave_hbm, wave_row_ref, in_sem.at[0])
    wave_in = pltpu.make_async_copy(wave_hbm, wave_ref, in_sem.at[1])
    stiff_in = pltpu.make_async_copy(stiff_hbm, stiff_ref, in_sem.at[2])
    wave_row_in.start()
    grid_in = [
        pltpu.make_async_copy(
            grid_ref.at[r // grid_ref.shape[1], r % grid_ref.shape[1]],
            rows.at[pl.ds(r, 1), pl.ds(0, lon_slots)],
            in_sem.at[3 + r],
        )
        for r in range(8)
    ]
    for copy in grid_in:
        copy.start()
    own_in = pltpu.make_async_copy(
        legendre_ref.at[h], weights.at[:, pl.ds(0, LANES)], own_sem.at[0]
    )
    own_in.start()
    wave_in.start()
    stiff_in.start()
    rows[:, pl.ds(lon_slots, rows.shape[1] - lon_slots)] = jnp.zeros(
        (8, rows.shape[1] - lon_slots), F32
    )
    build_tables(lon_ref, rows, table_ref, low_table, None, lon_slots)
    swap = [
        pltpu.make_async_remote_copy(
            src_ref=legendre_ref.at[1 - h, g],
            dst_ref=weights.at[g, pl.ds(LANES, LANES)],
            send_sem=swap_send_sem.at[g],
            recv_sem=swap_recv_sem.at[g],
            device_id=(w, 1 - h, f),
            device_id_type=MESH,
        )
        for g in range(groups)
    ]

    @pl.when(f == 1)
    def _():
        pl.semaphore_wait(barrier, hemis * sides - 1)
        pl.semaphore_signal(near_sem, inc=1, device_id=(w, h, 0), device_id_type=MESH)

    @pl.when(f == 0)
    def _():
        pl.semaphore_wait(near_sem, 1)

    for copy in swap[:1]:
        copy.start()
    wave_row_in.wait()
    waves = slot_waves(wave_row_ref[...].reshape(1, -1), devices)
    for copy in grid_in:
        copy.wait()
    forward_stage(lon_ref, rows, table_ref, low_table, waves, flip, send_ref, lon_slots)

    def slice_of(ref, place):
        return ref.at[pl.ds(pl.multiple_of(place * SUB, SUB), groups)]

    def everything(ref):
        return ref.at[pl.ds(0, (devices - 1) * groups)]

    my_part = w // (bands // 2)

    def copies(source, target, source_place, target_place, sent, got):
        return [
            pltpu.make_async_remote_copy(
                src_ref=slice_of(source, source_place(*partner(i))),
                dst_ref=slice_of(target, target_place(*partner(i))),
                send_sem=sent.at[0],
                recv_sem=got,
                device_id=partner(i)[:3],
                device_id_type=MESH,
            )
            for i in far_first
        ]

    def whole(source, target, sent, got):
        return pltpu.make_async_remote_copy(
            src_ref=everything(source),
            dst_ref=everything(target),
            send_sem=sent.at[0],
            recv_sem=got,
            device_id=partner(1)[:3],
            device_id_type=MESH,
        )

    out_copies = copies(
        send_ref,
        recv,
        lambda pw, ph, pf, ih: (pw * sides + pf) * hemis + ph,
        lambda pw, ph, pf, ih: ih * 2 * bands + f * bands + w,
        send_sem,
        recv_sem.at[0],
    )
    out_whole = whole(send_ref, recv, send_sem, recv_sem.at[0])
    @pl.when(f == 0)
    def _():
        pl.semaphore_wait(barrier, devices - 1)
        pl.semaphore_signal(all_sem, inc=1, device_id=(w, h, 1), device_id_type=MESH)

    @pl.when(f == 1)
    def _():
        pl.semaphore_wait(all_sem, 1)

    for copy in out_copies:
        copy.start()
    for copy in swap[1:]:
        copy.start()
    slice_of(recv, f * bands + w)[...] = slice_of(send_ref, owner)[...]
    wave_in.wait()
    stiff_in.wait()
    damping_table(wave_count, stiff_ref, wave_ref, first, damp)
    find_places(waves, places)
    own_in.wait()
    out_whole.wait_recv()

    lane_slot = iota((SUB, LANES), 1) // 16
    zero = jnp.zeros((SUB, LANES), F32)
    for g in range(groups):
        blocks = []
        for rel in range(hemis):
            base = rel * 2 * bands * SUB + g
            north = recv[pl.ds(base, bands, stride=SUB), :]
            south = recv[pl.ds(base + bands * SUB, bands, stride=SUB), :]
            even, odd = north + south, north - south
            for s in range(SUB):
                blocks.append(
                    jnp.concatenate([jnp.where(lane_slot == s, even, 0.0), zero], axis=1)
                )
                blocks.append(
                    jnp.concatenate([zero, jnp.where(lane_slot == s, odd, 0.0)], axis=1)
                )
        spaced = jnp.concatenate(blocks, axis=0).astype(BF16)
        swap[g].wait_recv()
        spectral = mxu(weights[g], spaced, TN)
        damped = (spectral * damp[g]).astype(BF16)
        full = mxu(weights[g], damped)
        for rel in range(hemis):
            sums = []
            for q in range(2):
                total = None
                for s in range(SUB):
                    at = rel * LANES + s * 16 + q * SUB
                    piece = full[at : at + SUB, q * LANES : (q + 1) * LANES]
                    total = piece if total is None else jnp.where(lane_slot == s, piece, total)
                sums.append(total)
            base = rel * 2 * bands * SUB + g
            back_send[pl.ds(base, bands, stride=SUB), :] = sums[0] + sums[1]
            back_send[pl.ds(base + bands * SUB, bands, stride=SUB), :] = sums[0] - sums[1]

    home_copies = copies(
        back_send,
        back_recv,
        lambda pw, ph, pf, ih: ih * 2 * bands + pf * bands + pw,
        lambda pw, ph, pf, ih: owner,
        back_send_sem,
        back_recv_sem.at[my_part],
    )
    home_whole = whole(back_send, back_recv, back_send_sem, back_recv_sem.at[0])
    for copy in home_copies:
        copy.start()
    slice_of(back_recv, owner)[...] = slice_of(back_send, f * bands + w)[...]
    halves = []
    for part in range(2):
        for mine in range(2):

            @pl.when((my_part == part) == (mine == 1))
            def _():
                lines = pl.ds(0, (devices // 2 - mine) * groups)
                pltpu.make_async_remote_copy(
                    src_ref=back_send.at[lines],
                    dst_ref=back_recv.at[lines],
                    send_sem=back_send_sem.at[0],
                    recv_sem=back_recv_sem.at[part],
                    device_id=partner(1)[:3],
                    device_id_type=MESH,
                ).wait_recv()

        halves.append(home_part(back_recv, (flip, other_flip)[part], places, part, groups))
    left_lines(lon_ref[0], wave_count, halves, places, left_ref)
    for copy in swap:
        copy.wait_send()
    out_whole.wait_send()
    home_whole.wait_send()


def inverse_kernel(wave_count, lon_ref, left_ref, table_ref, smooth_ref, bracket_ref, acc):
    fields, levels, _, lon_slots = smooth_ref.shape
    quarter = table_ref.shape[1]
    count, fourth, n_float = length_of(lon_ref)
    acc[...] = jnp.zeros_like(acc)
    fold_cos, fold_sin = fold_tables(n_float, quarter)
    sums = mxu(left_ref[...], table_ref[...])
    re = [sums[16 * r : 16 * r + 16] for r in range(4)]
    im = [None] + [sums[48 + 16 * r : 64 + 16 * r] for r in range(1, 4)]
    cos = [fold_cos[r : r + 1] for r in range(4)]
    sin = [fold_sin[r : r + 1] for r in range(4)]
    h0 = re[0]
    h1r, h1i = re[1] * cos[1] - im[1] * sin[1], re[1] * sin[1] + im[1] * cos[1]
    h2 = re[2] * cos[2] - im[2] * sin[2]
    h3r, h3i = re[3] * cos[3] - im[3] * sin[3], re[3] * sin[3] + im[3] * cos[3]
    even, odd, cross, turn = h0 + h2, h0 - h2, h1r + h3r, h3i - h1i
    live = iota((16, quarter), 1) < fourth
    scale = 1.0 / jnp.sqrt(n_float)
    width = quarter + LANES
    for a, value in enumerate((even + cross, odd + turn, even - cross, odd - turn)):
        value = jnp.where(live, value * scale, 0.0)
        smooth, slope = value[0:8], value[8:16]
        flipped = jnp.concatenate([slope[4:8], slope[0:4]], axis=0)
        product = smooth * flipped
        bracket = product - jnp.concatenate([product[4:8], product[0:4]], axis=0)
        segment = jnp.concatenate([smooth, bracket], axis=0)
        segment = jnp.concatenate([segment, jnp.zeros((16, LANES), F32)], axis=1)
        start = fourth * a
        segment = pltpu.roll(segment, lax.rem(start, LANES), 1)
        aligned = pl.multiple_of((start // LANES) * LANES, LANES)
        acc[:, pl.ds(aligned, width)] += segment
    for f in range(fields):
        for l in range(levels):
            smooth_ref[f, l] = acc[pl.ds(f * levels + l, 1), pl.ds(0, lon_slots)]
    for l in range(levels):
        bracket_ref[l] = acc[pl.ds(8 + l, 1), pl.ds(0, lon_slots)]


def in_hbm(x):
    return pltpu.with_memory_space_constraint(x, pltpu.HBM)


def fast_device(axes, grid, lon_count, wave_order, legendre, stiffness):
    bands, hemis, sides = axes
    owners = bands * hemis * sides
    wave_count = wave_order.shape[0]
    fields, levels, _, lon_slots = grid.shape
    groups = wave_count // owners // SUB
    k_count = legendre.shape[4]
    quarter = round_up(lon_slots // 4, LANES)
    waves4 = wave_count // 4
    long_rows = lon_slots + 2 * LANES
    smem = pl.BlockSpec(memory_space=pltpu.SMEM)
    vmem = pl.BlockSpec(memory_space=pltpu.VMEM)
    hbm = pl.BlockSpec(memory_space=pltpu.HBM)
    weights = legendre.reshape(hemis, groups, LANES, k_count)
    message = pltpu.VMEM((owners * SUB, LANES), F32)
    left, table = pl.pallas_call(
        functools.partial(middle_kernel, axes, wave_count),
        out_shape=(
            pltpu.VMEM((7 * 16, 2 * waves4), BF16),
            pltpu.VMEM((2 * waves4, quarter), BF16),
        ),
        in_specs=[smem, hbm, hbm, hbm, hbm],
        out_specs=(vmem, vmem),
        scratch_shapes=[
            pltpu.SMEM(stiffness.shape, F32),
            pltpu.SMEM(wave_order.shape, jnp.int32),
            pltpu.VMEM(wave_order.shape, jnp.int32),
            pltpu.VMEM((8, long_rows), F32),
            pltpu.VMEM((2 * waves4, quarter), BF16),
            pltpu.VMEM((LANES, LANES), F32),
            message,
            message,
            message,
            message,
            pltpu.VMEM((groups, 2 * LANES, k_count), BF16),
            pltpu.VMEM((groups, k_count, 2 * LANES), F32),
            pltpu.VMEM((6 * SUB, LANES), jnp.int32),
            pltpu.VMEM((LANES, LANES), F32),
            pltpu.SemaphoreType.DMA((1,)),
            pltpu.SemaphoreType.DMA((1,)),
            pltpu.SemaphoreType.DMA((1,)),
            pltpu.SemaphoreType.DMA((2,)),
            pltpu.SemaphoreType.DMA((1,)),
            pltpu.SemaphoreType.DMA((groups,)),
            pltpu.SemaphoreType.DMA((groups,)),
            pltpu.SemaphoreType.DMA((11,)),
            pltpu.SemaphoreType.REGULAR,
            pltpu.SemaphoreType.REGULAR,
        ],
        compiler_params=pltpu.CompilerParams(
            collective_id=0, has_side_effects=True, vmem_limit_bytes=24 << 20
        ),
        name="middle",
    )(lon_count, *[in_hbm(x) for x in (stiffness, wave_order, grid, weights)])
    return pl.pallas_call(
        functools.partial(inverse_kernel, wave_count),
        out_shape=(
            jax.ShapeDtypeStruct(grid.shape, F32),
            jax.ShapeDtypeStruct((levels, 1, lon_slots), F32),
        ),
        in_specs=[smem, vmem, vmem],
        out_specs=(vmem, vmem),
        scratch_shapes=[pltpu.VMEM((16, long_rows), F32)],
        compiler_params=pltpu.CompilerParams(vmem_limit_bytes=24 << 20),
        name="inverse",
    )(lon_count, left, table)


M = 768
FIELDS = 2
LEVELS = 4
K = 384


exact_mode = lax.Precision.HIGHEST


def general_device(grid, lon_count, wave_order, legendre, stiffness):
    lon_slots = grid.shape[3]
    rows_per = FIELDS * LEVELS
    channels = 2 * rows_per
    inner_width = 64
    wave_blocks = M // inner_width
    band_count = lax.axis_size("wave")
    slot_dev = M // (2 * band_count)
    cycle_length = lon_count[0]
    longitudes = jnp.arange(lon_slots, dtype=jnp.int32)
    wavenumbers = jnp.arange(M, dtype=jnp.int32)
    angle_step = 2.0 * jnp.pi / cycle_length.astype(jnp.float32)
    block_starts = jnp.arange(wave_blocks, dtype=jnp.int32) * inner_width
    inner_waves = jnp.arange(inner_width, dtype=jnp.int32)
    outer_angle = angle_step * (block_starts[:, None] * longitudes[None, :] % cycle_length).astype(
        jnp.float32
    )
    outer_cos = jnp.cos(outer_angle)
    outer_sin = jnp.sin(outer_angle)
    inner_angle = angle_step * (longitudes[:, None] * inner_waves[None, :] % cycle_length).astype(
        jnp.float32
    )
    inner_table = jnp.concatenate([jnp.cos(inner_angle), jnp.sin(inner_angle)], axis=1)
    cycle_scale = 1.0 / jnp.sqrt(cycle_length.astype(jnp.float32))
    live_points = longitudes < cycle_length
    wave_live = 2 * wavenumbers < cycle_length
    cycle_rows = jnp.where(live_points[None, :], grid[:, :, 0, :].reshape(rows_per, lon_slots), 0.0)
    modulated = jnp.stack(
        [cycle_rows[:, None, :] * outer_cos[None], -(cycle_rows[:, None, :] * outer_sin[None])]
    )
    product = jnp.dot(
        modulated.reshape(2 * rows_per * wave_blocks, lon_slots), inner_table, precision=exact_mode
    )
    product = product.reshape(2, rows_per, wave_blocks, 2 * inner_width)
    real_part = product[0, :, :, :inner_width] + product[1, :, :, inner_width:]
    imag_part = product[1, :, :, :inner_width] - product[0, :, :, inner_width:]
    fourier = jnp.stack([real_part, imag_part]).reshape(channels, M) * cycle_scale
    fourier = jnp.where(wave_live[None, :], fourier, 0.0)
    slotted = fourier[:, wave_order].reshape(channels, band_count, 2, slot_dev)
    side_index = lax.axis_index("fld")
    arrived = lax.all_to_all(
        lax.all_to_all(slotted[None, :, None], "wave", split_axis=3, concat_axis=2, tiled=True),
        "fld",
        split_axis=4,
        concat_axis=0,
        tiled=True,
    )
    stacked = arrived.reshape(2, channels, band_count, slot_dev)
    even_part = (stacked[0] + stacked[1]).astype(jnp.bfloat16)
    odd_part = (stacked[0] - stacked[1]).astype(jnp.bfloat16)
    parities = jnp.stack([even_part, odd_part])
    weights = legendre[:, 0]
    owner_index = lax.axis_index("wave") * 2 + side_index
    my_waves = lax.dynamic_slice_in_dim(wave_order, owner_index * slot_dev, slot_dev)
    degrees = (
        my_waves[:, None, None]
        + 2 * jnp.arange(K, dtype=jnp.int32)[None, None, :]
        + jnp.arange(2, dtype=jnp.int32)[None, :, None]
    )
    valid_degree = degrees < M
    spectral = jnp.einsum("aqwk,qcwa->aqck", weights, parities, preferred_element_type=jnp.float32)
    spectral = jnp.where(valid_degree[:, :, None, :], spectral, 0.0)
    chan_stiff = jnp.tile(jnp.repeat(stiffness, LEVELS), 2)
    degree_float = degrees.astype(jnp.float32)
    degree_ratio = degree_float * (degree_float + 1.0) / (M * (M - 1))
    summed = lax.psum(spectral, "hemi")
    damped = (
        summed / (1.0 + chan_stiff[None, None, :, None] * degree_ratio[:, :, None, :])
    ).astype(jnp.bfloat16)
    returned = jnp.einsum("aqwk,aqck->qcwa", weights, damped, preferred_element_type=jnp.float32)
    north_vals = returned[0] + returned[1]
    south_vals = returned[0] - returned[1]
    homebound = lax.all_to_all(
        lax.all_to_all(
            jnp.stack([north_vals, south_vals])[:, None, None],
            "wave",
            split_axis=4,
            concat_axis=2,
            tiled=True,
        ),
        "fld",
        split_axis=0,
        concat_axis=1,
        tiled=True,
    )
    homebound = homebound.reshape(2, band_count, channels, slot_dev)
    slot_values = jnp.transpose(homebound, (2, 1, 0, 3)).reshape(channels, M)
    spectra = jnp.zeros((channels, M), jnp.float32).at[:, wave_order].set(slot_values)
    weight_wave = jnp.where(wavenumbers == 0, 1.0, 2.0) * jnp.where(wave_live, cycle_scale, 0.0)
    real_coef = spectra[:rows_per] * weight_wave
    imag_coef = spectra[rows_per:] * weight_wave
    wave_ratio = wavenumbers.astype(jnp.float32) / M
    cos_coef = jnp.stack([real_coef, -(imag_coef * wave_ratio)]).reshape(
        2 * rows_per, wave_blocks, inner_width
    )
    sin_coef = jnp.stack([imag_coef, real_coef * wave_ratio]).reshape(
        2 * rows_per, wave_blocks, inner_width
    )
    left_rows = jnp.stack(
        [
            jnp.concatenate([cos_coef, -sin_coef], axis=2),
            jnp.concatenate([sin_coef, cos_coef], axis=2),
        ]
    )
    cycle_sums = lax.dot_general(
        left_rows.reshape(4 * rows_per * wave_blocks, 2 * inner_width),
        inner_table,
        (((1,), (1,)), ((), ())),
        precision=exact_mode,
    )
    cycle_sums = cycle_sums.reshape(2, 2 * rows_per, wave_blocks, lon_slots)
    values = jnp.sum(cycle_sums[0] * outer_cos[None] - cycle_sums[1] * outer_sin[None], axis=1)
    values = jnp.where(live_points[None, :], values, 0.0)
    smooth_rows = values[:rows_per].reshape(FIELDS, LEVELS, lon_slots)
    slope_rows = values[rows_per:].reshape(FIELDS, LEVELS, lon_slots)
    bracket = smooth_rows[0] * slope_rows[1] - smooth_rows[1] * slope_rows[0]
    return (smooth_rows[:, :, None, :], bracket[:, None, :])


def solution(mesh):
    axes = (mesh.shape["wave"], mesh.shape["hemi"], mesh.shape["fld"])
    bands, hemis, sides = axes
    placed = (
        P(None, None, ("wave", "hemi", "fld"), None),
        P(("wave", "hemi", "fld")),
        P(),
        P(("wave", "fld"), "hemi", None, None, None),
        P(),
    )
    fits = bands == 8 and hemis == 2 and sides == 2 and M == 24 * bands * hemis * sides
    step = functools.partial(fast_device, axes) if fits else general_device
    return jax.shard_map(
        step,
        mesh=mesh,
        in_specs=placed,
        out_specs=(
            P(None, None, ("wave", "hemi", "fld"), None),
            P(None, ("wave", "hemi", "fld"), None),
        ),
        check_vma=False,
    )
```

```python
import functools
import math

import jax
import jax.numpy as jnp
from jax import lax
from jax.experimental import pallas as pl
from jax.experimental.pallas import tpu as pltpu
from jax.sharding import PartitionSpec as P

LANES = 128
SUB = 8
HALF = LANES // 2
F32 = jnp.float32
BF16 = jnp.bfloat16
NN = (((1,), (0,)), ((), ()))
NT = (((1,), (1,)), ((), ()))
TN = (((0,), (0,)), ((), ()))
MESH = pl.DeviceIdType.MESH


def round_up(value, step):
    return -(-value // step) * step


def mxu(a, b, dims=NN):
    return lax.dot_general(a, b, dims, preferred_element_type=F32)


def split(x):
    high = x.astype(BF16)
    return high, (x - high.astype(F32)).astype(BF16)


def iota(shape, axis):
    return lax.broadcasted_iota(jnp.int32, shape, axis)


def sine_turn(x):
    y = x * x
    total = jnp.full_like(y, 0.0)
    for power in (13, 11, 9, 7, 5, 3, 1):
        sign = 1.0 if power % 4 == 1 else -1.0
        total = total * y + sign * (2.0 * math.pi) ** power / math.factorial(power)
    return total * x


def turn_tables(steps, period):
    inverse = 1.0 / period
    rest = steps - jnp.floor(steps * inverse) * period
    turn = rest * inverse
    turn = turn - jnp.floor(turn + 0.5)
    shifted = turn - 0.25
    shifted = jnp.where(shifted < -0.5, shifted + 1.0, shifted)
    return sine_turn(0.25 - jnp.abs(turn)), sine_turn(0.25 - jnp.abs(shifted))


def length_of(lon_ref):
    count = lon_ref[0]
    return count, lax.shift_right_logical(count, 2), jnp.full((1, 1), count.astype(F32), F32)


def fold_tables(n_float, quarter):
    steps = iota((8, quarter), 0) * iota((8, quarter), 1)
    return turn_tables(steps.astype(F32), n_float)


def roll_lanes(x, amount):
    amount = amount % x.shape[1]
    return x if amount == 0 else pltpu.roll(x, amount, 1)


def lane_gather(tile, index):
    return jnp.take_along_axis(tile, index, axis=1, mode="promise_in_bounds")


def window_at(tiles, start, most, count):
    whole = lax.shift_right_logical(start, 7)
    bits = (most // LANES).bit_length()
    for bit in reversed(range(bits)):
        step = 1 << bit
        keep = count + step
        hit = jnp.full(tiles[0].shape, whole, jnp.int32) & step != 0
        tiles = [
            jnp.where(hit, tiles[i + step], tiles[i]) if i + step < len(tiles) else tiles[i]
            for i in range(min(keep, len(tiles)))
        ]
    lane = iota(tiles[0].shape, 1) + jnp.full(tiles[0].shape, start & (LANES - 1), jnp.int32)
    index = lane & (LANES - 1)
    turned = [lane_gather(tile, index) for tile in tiles[: count + 1]]
    inside = lane < LANES
    return jnp.concatenate(
        [jnp.where(inside, turned[i], turned[i + 1]) for i in range(count)], axis=1
    )


def half_low(shape):
    return iota(shape, 1) < HALF


def wave_of(tile, shape):
    lane = iota(shape, 1)
    if tile < 4:
        return 4 * lane + tile
    step = jnp.where(lane < HALF, lane, lane - HALF)
    return 4 * (LANES + step) + 2 * (tile - 4) + jnp.where(lane < HALF, 0, 1)


def pick(tiles, tile_id, lane_id):
    out = None
    for i, tile in enumerate(tiles):
        moved = lane_gather(tile, lane_id)
        out = moved if out is None else jnp.where(tile_id == i, moved, out)
    return out


def slot_waves(wave_row, owners):
    row = jnp.broadcast_to(wave_row.astype(F32), (SUB, wave_row.shape[1]))
    tiles = [row[:, i * LANES : (i + 1) * LANES] for i in range(row.shape[1] // LANES)]
    slots = row.shape[1] // owners
    lane = iota((SUB, LANES), 1)
    out = []
    for group in range(slots // SUB):
        for part in range(owners // 16):
            slot = (part * 16 + lane // SUB) * slots + group * SUB + lane % SUB
            first = part * 16 * slots // LANES
            last = ((part * 16 + 15) * slots + group * SUB + SUB - 1) // LANES
            out.append(pick(tiles[first : last + 1], slot // LANES - first, slot % LANES))
    return out


def build_tables(lon_ref, rows, table_ref, low_table, pieces, lon_slots):
    quarter = table_ref.shape[1]
    waves4 = table_ref.shape[0] // 2
    _, fourth, _ = length_of(lon_ref)
    fourth_float = jnp.full((1, 1), fourth.astype(F32), F32)
    c_steps = iota((waves4, LANES), 0)
    lane_steps = iota((waves4, LANES), 1)
    near_cos, near_sin = turn_tables((c_steps * lane_steps).astype(F32), fourth_float)
    far_cos, far_sin = turn_tables((c_steps * lane_steps * LANES).astype(F32), fourth_float)
    rest = waves4 - LANES
    for block in range(quarter // LANES):
        fc, fs = far_cos[:, block : block + 1], far_sin[:, block : block + 1]
        cols = pl.ds(block * LANES, LANES)
        for part, value in enumerate(
            (near_cos * fc - near_sin * fs, near_cos * fs + near_sin * fc)
        ):
            high, low = split(value)
            for ref, half in ((table_ref, high), (low_table, low)):
                ref[pl.ds(part * LANES, LANES), cols] = half[:LANES]
                ref[pl.ds(2 * LANES + part * rest, rest), cols] = half[LANES:]


def forward_stage(lon_ref, rows, table_ref, low_table, waves, flip, send_ref, lon_slots):
    quarter = table_ref.shape[1]
    count, fourth, n_float = length_of(lon_ref)
    live = iota((8, quarter), 1) < fourth
    tiles = [rows[:, i * LANES : (i + 1) * LANES] for i in range(rows.shape[1] // LANES)]
    parts = [rows[:, :quarter]]
    for a in range(1, 4):
        parts.append(window_at(tiles, fourth * a, a * (lon_slots // 4), quarter // LANES))
    x0, x1, x2, x3 = [jnp.where(live, part, 0.0) for part in parts]
    fold_cos, fold_sin = fold_tables(n_float, quarter)
    c1, s1, c2, s2 = fold_cos[1:2], fold_sin[1:2], fold_cos[2:3], fold_sin[2:3]
    c3, s3 = fold_cos[3:4], fold_sin[3:4]
    a02, d02, a13, d13 = x0 + x2, x0 - x2, x1 + x3, x1 - x3
    even = a02 - a13
    z = jnp.concatenate(
        [
            a02 + a13,
            d02 * c1 - d13 * s1,
            even * c2,
            d02 * c3 + d13 * s3,
            jnp.zeros_like(x0),
            -d13 * c1 - d02 * s1,
            -even * s2,
            d13 * c3 - d02 * s3,
        ],
        axis=0,
    )
    z_high, z_low = split(z)
    both = mxu(jnp.concatenate([z_high, z_low], axis=0), table_ref[...], NT)
    total = both[:64] + both[64:] + mxu(z_high, low_table[...], NT)
    t0, t1, t2 = (total[:, i * LANES : (i + 1) * LANES] for i in range(3))
    near = [t0[:32] + t1[32:], t0[32:] - t1[:32]]
    turned = roll_lanes(t2, HALF)
    low = half_low((32, LANES))
    far = [
        jnp.where(low, t2[:32], turned[:32]) + jnp.where(low, turned[32:], t2[32:]),
        jnp.where(low, t2[32:], turned[32:]) - jnp.where(low, turned[:32], t2[:32]),
    ]
    scale = 1.0 / jnp.sqrt(n_float)
    low = half_low((8, LANES))
    sources = []
    for tile in range(6):
        if tile < 4:
            halves = [part[8 * tile : 8 * tile + 8] for part in near]
        else:
            r = 2 * (tile - 4)
            halves = [
                jnp.where(low, part[8 * r : 8 * r + 8], part[8 * r + 8 : 8 * r + 16])
                for part in far
            ]
        keep = 2 * wave_of(tile, (8, LANES)) < count
        sources.append([jnp.where(keep, half * scale, 0.0) for half in halves])
    moved = []
    for wave in waves:
        m = wave.astype(jnp.int32)
        r, c = m % 4, m // 4
        tile_id = jnp.where(c < LANES, r, 4 + r // 2)
        lane_id = jnp.where(c < LANES, c, c - LANES + HALF * (r % 2))
        for part in range(2):
            moved.append(pick([source[part] for source in sources], tile_id, lane_id))
    moved.append(jnp.zeros((LANES - 8 * len(moved), LANES), F32))
    flip[...] = jnp.concatenate(moved, axis=0).T
    lane_block = iota((16, LANES), 1) // 16
    lines = [flip[pl.ds(s, 16, stride=SUB), :] for s in range(SUB)]
    for t in range(len(waves)):
        out = None
        for s in range(SUB):
            line = roll_lanes(lines[s], 16 * (s - t))
            out = line if out is None else jnp.where(lane_block == s, line, out)
        send_ref[pl.ds(16 * SUB * (t % 2) + t // 2, 16, stride=SUB), :] = out


def home_part(back_recv, flip, places, groups, first):
    lane_block = iota((16, LANES), 1) // 16
    tiles = [(g, part) for g in range(groups) for part in range(2)]
    lines = [
        back_recv[pl.ds(16 * SUB * part + g, 16, stride=SUB), :] for g, part in tiles
    ]
    for s in range(SUB):
        out = None
        for t in range(len(tiles)):
            line = roll_lanes(lines[t], 16 * (t - s))
            out = line if out is None else jnp.where(lane_block == t, line, out)
        flip[pl.ds(s, 16, stride=SUB), :] = out
    turned = flip[...].T
    picked = []
    for tile in range(6):
        code = places[pl.ds(tile * SUB, SUB), :]
        tile_id, lane_id = code // LANES - first, code % LANES
        picked.append(
            [
                pick(
                    [turned[16 * t + at : 16 * t + at + 8] for t in range(len(tiles))],
                    tile_id,
                    lane_id,
                )
                for at in (0, 8)
            ]
        )
    return picked


def find_places(waves, places):
    stacked = jnp.concatenate(
        [wave[0:1] for wave in waves] + [jnp.zeros((LANES - len(waves), LANES), F32)], axis=0
    ).T
    place = iota((LANES, LANES), 0).astype(F32)
    for tile in range(6):
        want = wave_of(tile, (LANES, LANES)).astype(F32)
        total = jnp.zeros((LANES, LANES), F32)
        for t in range(len(waves)):
            total = jnp.where(stacked[:, t : t + 1] == want, place + float(LANES * t), total)
        places[pl.ds(tile * SUB, SUB), :] = jnp.broadcast_to(
            jnp.sum(total, axis=0, keepdims=True), (SUB, LANES)
        ).astype(jnp.int32)


def damping_table(wave_count, stiff_ref, wave_ref, first, damp):
    groups, k_count, width = damp.shape
    lane = iota((SUB, width), 1)
    field = lane // 4 % 2
    stiff = jnp.where(field == 0, stiff_ref[0], stiff_ref[1])
    for g in range(groups):
        wave = lane // LANES
        for s in range(SUB):
            wave = wave + jnp.where(lane // 16 % SUB == s, wave_ref[first + g * SUB + s], 0)
        degrees = wave[0:1] + 2 * iota((k_count, width), 0)
        degree_float = degrees.astype(F32)
        ratio = degree_float * (degree_float + 1.0) / (wave_count * (wave_count - 1))
        damp[g] = jnp.where(degrees < wave_count, 1.0 / (1.0 + stiff[0:1] * ratio), 0.0)


def left_lines(count, wave_count, halves, last, places, left_ref):
    low = half_low((16, LANES))
    near_re, near_im, far_re, far_im = [], [], [], []
    for tile in range(6):
        first = places[pl.ds(tile * SUB, SUB), :] < last * LANES
        m = wave_of(tile, (8, LANES))
        weight = jnp.where(2 * m < count, jnp.where(m == 0, 1.0, 2.0), 0.0)
        steep = m.astype(F32) / wave_count
        real, imag = (
            jnp.where(first, early, late) * weight
            for early, late in zip(halves[0][tile], halves[1][tile])
        )
        cre = jnp.concatenate([real, -imag * steep], axis=0)
        cim = jnp.concatenate([imag, real * steep], axis=0)
        if tile < 4:
            near_re.append(cre)
            near_im.append(cim)
        else:
            cre_turned, cim_turned = roll_lanes(cre, HALF), roll_lanes(cim, HALF)
            far_re += [jnp.where(low, cre, -cim_turned), jnp.where(low, cre_turned, -cim)]
            far_im += [jnp.where(low, cim, cre_turned), jnp.where(low, cim_turned, cre)]
    lines = [
        jnp.concatenate([near_re[r], -near_im[r], far_re[r]], axis=1) for r in range(4)
    ] + [jnp.concatenate([near_im[r], near_re[r], far_im[r]], axis=1) for r in range(1, 4)]
    for at, line in enumerate(lines):
        left_ref[pl.ds(16 * at, 16), :] = line.astype(BF16)


def middle_kernel(
    axes, wave_count, lon_ref, stiff_hbm, wave_hbm, grid_ref, legendre_ref,
    left_ref, table_ref,
    stiff_ref, wave_ref, wave_row_ref, rows, low_table, flip, send_ref, recv, back_send, back_recv,
    weights, damp, places, other_flip, last_send, last_recv,
    send_sem, recv_sem, back_send_sem, back_recv_sem, own_sem, swap_send_sem, swap_recv_sem, in_sem, near_sem, all_sem,
):
    bands, hemis, sides = axes
    devices = bands * hemis * sides
    w, h, f = lax.axis_index("wave"), lax.axis_index("hemi"), lax.axis_index("fld")
    owner = (w * sides + f) * hemis + h
    groups = weights.shape[0]
    lon_slots = grid_ref.shape[3]
    first = owner * groups * SUB

    def partner(i):
        iz, ix, ih, side = i // 8, i // 4 % 2, i // 2 % 2, i % 2
        z, x = w // 2, lax.rem(w, 2)
        pz = (z, z + 1 - 2 * lax.rem(z, 2), lax.rem(z + 2, 4), 3 - z)[iz]
        px = 1 - x if ix else x
        return pz * 2 + px, (1 - h if ih else h), (1 - f if side else f), ih

    far_first = sorted(
        range(1, devices), key=lambda i: -(i // 8 + i // 4 % 2 + i // 2 % 2 + 0.1 * (i % 2))
    )
    barrier = pltpu.get_barrier_semaphore()
    greeted = [partner(i)[:2] + (0,) for i in far_first if i > 1 and i % 2 == 0]
    for device in greeted + [(w, h, 1 - f), (w, 1 - h, 1)]:
        pl.semaphore_signal(barrier, inc=1, device_id=device, device_id_type=MESH)

    wave_row_in = pltpu.make_async_copy(wave_hbm, wave_row_ref, in_sem.at[0])
    wave_in = pltpu.make_async_copy(wave_hbm, wave_ref, in_sem.at[1])
    stiff_in = pltpu.make_async_copy(stiff_hbm, stiff_ref, in_sem.at[2])
    wave_row_in.start()
    grid_in = [
        pltpu.make_async_copy(
            grid_ref.at[r // grid_ref.shape[1], r % grid_ref.shape[1]],
            rows.at[pl.ds(r, 1), pl.ds(0, lon_slots)],
            in_sem.at[3 + r],
        )
        for r in range(8)
    ]
    for copy in grid_in:
        copy.start()
    own_in = pltpu.make_async_copy(
        legendre_ref.at[h], weights.at[:, pl.ds(0, LANES)], own_sem.at[0]
    )
    own_in.start()
    wave_in.start()
    stiff_in.start()
    rows[:, pl.ds(lon_slots, rows.shape[1] - lon_slots)] = jnp.zeros(
        (8, rows.shape[1] - lon_slots), F32
    )
    build_tables(lon_ref, rows, table_ref, low_table, None, lon_slots)
    swap = [
        pltpu.make_async_remote_copy(
            src_ref=legendre_ref.at[1 - h, g],
            dst_ref=weights.at[g, pl.ds(LANES, LANES)],
            send_sem=swap_send_sem.at[g],
            recv_sem=swap_recv_sem.at[g],
            device_id=(w, 1 - h, f),
            device_id_type=MESH,
        )
        for g in range(groups)
    ]

    @pl.when(f == 1)
    def _():
        pl.semaphore_wait(barrier, hemis * sides - 1)
        pl.semaphore_signal(near_sem, inc=1, device_id=(w, h, 0), device_id_type=MESH)

    @pl.when(f == 0)
    def _():
        pl.semaphore_wait(near_sem, 1)

    for copy in swap[:2]:
        copy.start()
    wave_row_in.wait()
    waves = slot_waves(wave_row_ref[...].reshape(1, -1), devices)
    for copy in grid_in:
        copy.wait()
    forward_stage(lon_ref, rows, table_ref, low_table, waves, flip, send_ref, lon_slots)

    def slice_of(ref, place, count):
        return ref.at[pl.ds(pl.multiple_of(place * SUB, SUB), count)]

    def everything(ref, count):
        return ref.at[pl.ds(0, (devices - 1) * count)]

    def copies(source, target, source_place, target_place, sent, got, count):
        return [
            pltpu.make_async_remote_copy(
                src_ref=slice_of(source, source_place(*partner(i)), count),
                dst_ref=slice_of(target, target_place(*partner(i)), count),
                send_sem=sent,
                recv_sem=got,
                device_id=partner(i)[:3],
                device_id_type=MESH,
            )
            for i in far_first
        ]

    def whole(source, target, sent, got, count):
        return pltpu.make_async_remote_copy(
            src_ref=everything(source, count),
            dst_ref=everything(target, count),
            send_sem=sent,
            recv_sem=got,
            device_id=partner(1)[:3],
            device_id_type=MESH,
        )

    out_copies = copies(
        send_ref,
        recv,
        lambda pw, ph, pf, ih: (pw * sides + pf) * hemis + ph,
        lambda pw, ph, pf, ih: ih * 2 * bands + f * bands + w,
        send_sem.at[0],
        recv_sem.at[0],
        groups,
    )
    out_whole = whole(send_ref, recv, send_sem.at[0], recv_sem.at[0], groups)
    @pl.when(f == 0)
    def _():
        pl.semaphore_wait(barrier, devices - 1)
        pl.semaphore_signal(all_sem, inc=1, device_id=(w, h, 1), device_id_type=MESH)

    @pl.when(f == 1)
    def _():
        pl.semaphore_wait(all_sem, 1)

    for copy in out_copies:
        copy.start()
    for copy in swap[2:]:
        copy.start()
    slice_of(recv, f * bands + w, groups)[...] = slice_of(send_ref, owner, groups)[...]
    wave_in.wait()
    stiff_in.wait()
    damping_table(wave_count, stiff_ref, wave_ref, first, damp)
    find_places(waves, places)
    own_in.wait()
    out_whole.wait_recv()

    home_rows = (groups - 1, 1)
    home_whole = [
        whole(source, target, back_send_sem.at[at], back_recv_sem.at[at], home_rows[at])
        for at, (source, target) in enumerate(((back_send, back_recv), (last_send, last_recv)))
    ]

    def send_home(at):
        source, target = ((back_send, back_recv), (last_send, last_recv))[at]
        for copy in copies(
            source,
            target,
            lambda pw, ph, pf, ih: ih * 2 * bands + pf * bands + pw,
            lambda pw, ph, pf, ih: owner,
            back_send_sem.at[at],
            back_recv_sem.at[at],
            home_rows[at],
        ):
            copy.start()
        slice_of(target, owner, home_rows[at])[...] = slice_of(
            source, f * bands + w, home_rows[at]
        )[...]

    lane_slot = iota((SUB, LANES), 1) // 16
    zero = jnp.zeros((SUB, LANES), F32)
    for g in range(groups):
        blocks = []
        for rel in range(hemis):
            base = rel * 2 * bands * SUB + g
            north = recv[pl.ds(base, bands, stride=SUB), :]
            south = recv[pl.ds(base + bands * SUB, bands, stride=SUB), :]
            even, odd = north + south, north - south
            for s in range(SUB):
                blocks.append(
                    jnp.concatenate([jnp.where(lane_slot == s, even, 0.0), zero], axis=1)
                )
                blocks.append(
                    jnp.concatenate([zero, jnp.where(lane_slot == s, odd, 0.0)], axis=1)
                )
        spaced = jnp.concatenate(blocks, axis=0).astype(BF16)
        swap[g].wait_recv()
        spectral = mxu(weights[g], spaced, TN)
        damped = (spectral * damp[g]).astype(BF16)
        full = mxu(weights[g], damped)
        for rel in range(hemis):
            sums = []
            for q in range(2):
                total = None
                for s in range(SUB):
                    at = rel * LANES + s * 16 + q * SUB
                    piece = full[at : at + SUB, q * LANES : (q + 1) * LANES]
                    total = piece if total is None else jnp.where(lane_slot == s, piece, total)
                sums.append(total)
            target, base = back_send, rel * 2 * bands * SUB + g
            if g == groups - 1:
                target, base = last_send, rel * 2 * bands * SUB
            target[pl.ds(base, bands, stride=SUB), :] = sums[0] + sums[1]
            target[pl.ds(base + bands * SUB, bands, stride=SUB), :] = sums[0] - sums[1]
        if g >= groups - 2:
            send_home(g - groups + 2)

    halves = []
    for at in range(2):
        home_whole[at].wait_recv()
        halves.append(
            home_part(
                (back_recv, last_recv)[at], (flip, other_flip)[at], places, home_rows[at],
                2 * (groups - 1) * at,
            )
        )
    left_lines(lon_ref[0], wave_count, halves, 2 * (groups - 1), places, left_ref)
    for copy in swap:
        copy.wait_send()
    out_whole.wait_send()
    for copy in home_whole:
        copy.wait_send()


def inverse_kernel(wave_count, lon_ref, left_ref, table_ref, smooth_ref, bracket_ref, acc):
    fields, levels, _, lon_slots = smooth_ref.shape
    quarter = table_ref.shape[1]
    count, fourth, n_float = length_of(lon_ref)
    acc[...] = jnp.zeros_like(acc)
    fold_cos, fold_sin = fold_tables(n_float, quarter)
    sums = mxu(left_ref[...], table_ref[...])
    re = [sums[16 * r : 16 * r + 16] for r in range(4)]
    im = [None] + [sums[48 + 16 * r : 64 + 16 * r] for r in range(1, 4)]
    cos = [fold_cos[r : r + 1] for r in range(4)]
    sin = [fold_sin[r : r + 1] for r in range(4)]
    h0 = re[0]
    h1r, h1i = re[1] * cos[1] - im[1] * sin[1], re[1] * sin[1] + im[1] * cos[1]
    h2 = re[2] * cos[2] - im[2] * sin[2]
    h3r, h3i = re[3] * cos[3] - im[3] * sin[3], re[3] * sin[3] + im[3] * cos[3]
    even, odd, cross, turn = h0 + h2, h0 - h2, h1r + h3r, h3i - h1i
    live = iota((16, quarter), 1) < fourth
    scale = 1.0 / jnp.sqrt(n_float)
    width = quarter + LANES
    for a, value in enumerate((even + cross, odd + turn, even - cross, odd - turn)):
        value = jnp.where(live, value * scale, 0.0)
        smooth, slope = value[0:8], value[8:16]
        flipped = jnp.concatenate([slope[4:8], slope[0:4]], axis=0)
        product = smooth * flipped
        bracket = product - jnp.concatenate([product[4:8], product[0:4]], axis=0)
        segment = jnp.concatenate([smooth, bracket], axis=0)
        segment = jnp.concatenate([segment, jnp.zeros((16, LANES), F32)], axis=1)
        start = fourth * a
        segment = pltpu.roll(segment, lax.rem(start, LANES), 1)
        aligned = pl.multiple_of((start // LANES) * LANES, LANES)
        acc[:, pl.ds(aligned, width)] += segment
    for f in range(fields):
        for l in range(levels):
            smooth_ref[f, l] = acc[pl.ds(f * levels + l, 1), pl.ds(0, lon_slots)]
    for l in range(levels):
        bracket_ref[l] = acc[pl.ds(8 + l, 1), pl.ds(0, lon_slots)]


def in_hbm(x):
    return pltpu.with_memory_space_constraint(x, pltpu.HBM)


def fast_device(axes, grid, lon_count, wave_order, legendre, stiffness):
    bands, hemis, sides = axes
    owners = bands * hemis * sides
    wave_count = wave_order.shape[0]
    fields, levels, _, lon_slots = grid.shape
    groups = wave_count // owners // SUB
    k_count = legendre.shape[4]
    quarter = round_up(lon_slots // 4, LANES)
    waves4 = wave_count // 4
    long_rows = lon_slots + 2 * LANES
    smem = pl.BlockSpec(memory_space=pltpu.SMEM)
    vmem = pl.BlockSpec(memory_space=pltpu.VMEM)
    hbm = pl.BlockSpec(memory_space=pltpu.HBM)
    weights = legendre.reshape(hemis, groups, LANES, k_count)
    message = pltpu.VMEM((owners * SUB, LANES), F32)
    left, table = pl.pallas_call(
        functools.partial(middle_kernel, axes, wave_count),
        out_shape=(
            pltpu.VMEM((7 * 16, 2 * waves4), BF16),
            pltpu.VMEM((2 * waves4, quarter), BF16),
        ),
        in_specs=[smem, hbm, hbm, hbm, hbm],
        out_specs=(vmem, vmem),
        scratch_shapes=[
            pltpu.SMEM(stiffness.shape, F32),
            pltpu.SMEM(wave_order.shape, jnp.int32),
            pltpu.VMEM(wave_order.shape, jnp.int32),
            pltpu.VMEM((8, long_rows), F32),
            pltpu.VMEM((2 * waves4, quarter), BF16),
            pltpu.VMEM((LANES, LANES), F32),
            message,
            message,
            message,
            message,
            pltpu.VMEM((groups, 2 * LANES, k_count), BF16),
            pltpu.VMEM((groups, k_count, 2 * LANES), F32),
            pltpu.VMEM((6 * SUB, LANES), jnp.int32),
            pltpu.VMEM((LANES, LANES), F32),
            message,
            message,
            pltpu.SemaphoreType.DMA((1,)),
            pltpu.SemaphoreType.DMA((1,)),
            pltpu.SemaphoreType.DMA((2,)),
            pltpu.SemaphoreType.DMA((2,)),
            pltpu.SemaphoreType.DMA((1,)),
            pltpu.SemaphoreType.DMA((groups,)),
            pltpu.SemaphoreType.DMA((groups,)),
            pltpu.SemaphoreType.DMA((11,)),
            pltpu.SemaphoreType.REGULAR,
            pltpu.SemaphoreType.REGULAR,
        ],
        compiler_params=pltpu.CompilerParams(
            collective_id=0, has_side_effects=True, vmem_limit_bytes=24 << 20
        ),
        name="middle",
    )(lon_count, *[in_hbm(x) for x in (stiffness, wave_order, grid, weights)])
    return pl.pallas_call(
        functools.partial(inverse_kernel, wave_count),
        out_shape=(
            jax.ShapeDtypeStruct(grid.shape, F32),
            jax.ShapeDtypeStruct((levels, 1, lon_slots), F32),
        ),
        in_specs=[smem, vmem, vmem],
        out_specs=(vmem, vmem),
        scratch_shapes=[pltpu.VMEM((16, long_rows), F32)],
        compiler_params=pltpu.CompilerParams(vmem_limit_bytes=24 << 20),
        name="inverse",
    )(lon_count, left, table)


M = 768
FIELDS = 2
LEVELS = 4
K = 384


exact_mode = lax.Precision.HIGHEST


def general_device(grid, lon_count, wave_order, legendre, stiffness):
    lon_slots = grid.shape[3]
    rows_per = FIELDS * LEVELS
    channels = 2 * rows_per
    inner_width = 64
    wave_blocks = M // inner_width
    band_count = lax.axis_size("wave")
    slot_dev = M // (2 * band_count)
    cycle_length = lon_count[0]
    longitudes = jnp.arange(lon_slots, dtype=jnp.int32)
    wavenumbers = jnp.arange(M, dtype=jnp.int32)
    angle_step = 2.0 * jnp.pi / cycle_length.astype(jnp.float32)
    block_starts = jnp.arange(wave_blocks, dtype=jnp.int32) * inner_width
    inner_waves = jnp.arange(inner_width, dtype=jnp.int32)
    outer_angle = angle_step * (block_starts[:, None] * longitudes[None, :] % cycle_length).astype(
        jnp.float32
    )
    outer_cos = jnp.cos(outer_angle)
    outer_sin = jnp.sin(outer_angle)
    inner_angle = angle_step * (longitudes[:, None] * inner_waves[None, :] % cycle_length).astype(
        jnp.float32
    )
    inner_table = jnp.concatenate([jnp.cos(inner_angle), jnp.sin(inner_angle)], axis=1)
    cycle_scale = 1.0 / jnp.sqrt(cycle_length.astype(jnp.float32))
    live_points = longitudes < cycle_length
    wave_live = 2 * wavenumbers < cycle_length
    cycle_rows = jnp.where(live_points[None, :], grid[:, :, 0, :].reshape(rows_per, lon_slots), 0.0)
    modulated = jnp.stack(
        [cycle_rows[:, None, :] * outer_cos[None], -(cycle_rows[:, None, :] * outer_sin[None])]
    )
    product = jnp.dot(
        modulated.reshape(2 * rows_per * wave_blocks, lon_slots), inner_table, precision=exact_mode
    )
    product = product.reshape(2, rows_per, wave_blocks, 2 * inner_width)
    real_part = product[0, :, :, :inner_width] + product[1, :, :, inner_width:]
    imag_part = product[1, :, :, :inner_width] - product[0, :, :, inner_width:]
    fourier = jnp.stack([real_part, imag_part]).reshape(channels, M) * cycle_scale
    fourier = jnp.where(wave_live[None, :], fourier, 0.0)
    slotted = fourier[:, wave_order].reshape(channels, band_count, 2, slot_dev)
    side_index = lax.axis_index("fld")
    arrived = lax.all_to_all(
        lax.all_to_all(slotted[None, :, None], "wave", split_axis=3, concat_axis=2, tiled=True),
        "fld",
        split_axis=4,
        concat_axis=0,
        tiled=True,
    )
    stacked = arrived.reshape(2, channels, band_count, slot_dev)
    even_part = (stacked[0] + stacked[1]).astype(jnp.bfloat16)
    odd_part = (stacked[0] - stacked[1]).astype(jnp.bfloat16)
    parities = jnp.stack([even_part, odd_part])
    weights = legendre[:, 0]
    owner_index = lax.axis_index("wave") * 2 + side_index
    my_waves = lax.dynamic_slice_in_dim(wave_order, owner_index * slot_dev, slot_dev)
    degrees = (
        my_waves[:, None, None]
        + 2 * jnp.arange(K, dtype=jnp.int32)[None, None, :]
        + jnp.arange(2, dtype=jnp.int32)[None, :, None]
    )
    valid_degree = degrees < M
    spectral = jnp.einsum("aqwk,qcwa->aqck", weights, parities, preferred_element_type=jnp.float32)
    spectral = jnp.where(valid_degree[:, :, None, :], spectral, 0.0)
    chan_stiff = jnp.tile(jnp.repeat(stiffness, LEVELS), 2)
    degree_float = degrees.astype(jnp.float32)
    degree_ratio = degree_float * (degree_float + 1.0) / (M * (M - 1))
    summed = lax.psum(spectral, "hemi")
    damped = (
        summed / (1.0 + chan_stiff[None, None, :, None] * degree_ratio[:, :, None, :])
    ).astype(jnp.bfloat16)
    returned = jnp.einsum("aqwk,aqck->qcwa", weights, damped, preferred_element_type=jnp.float32)
    north_vals = returned[0] + returned[1]
    south_vals = returned[0] - returned[1]
    homebound = lax.all_to_all(
        lax.all_to_all(
            jnp.stack([north_vals, south_vals])[:, None, None],
            "wave",
            split_axis=4,
            concat_axis=2,
            tiled=True,
        ),
        "fld",
        split_axis=0,
        concat_axis=1,
        tiled=True,
    )
    homebound = homebound.reshape(2, band_count, channels, slot_dev)
    slot_values = jnp.transpose(homebound, (2, 1, 0, 3)).reshape(channels, M)
    spectra = jnp.zeros((channels, M), jnp.float32).at[:, wave_order].set(slot_values)
    weight_wave = jnp.where(wavenumbers == 0, 1.0, 2.0) * jnp.where(wave_live, cycle_scale, 0.0)
    real_coef = spectra[:rows_per] * weight_wave
    imag_coef = spectra[rows_per:] * weight_wave
    wave_ratio = wavenumbers.astype(jnp.float32) / M
    cos_coef = jnp.stack([real_coef, -(imag_coef * wave_ratio)]).reshape(
        2 * rows_per, wave_blocks, inner_width
    )
    sin_coef = jnp.stack([imag_coef, real_coef * wave_ratio]).reshape(
        2 * rows_per, wave_blocks, inner_width
    )
    left_rows = jnp.stack(
        [
            jnp.concatenate([cos_coef, -sin_coef], axis=2),
            jnp.concatenate([sin_coef, cos_coef], axis=2),
        ]
    )
    cycle_sums = lax.dot_general(
        left_rows.reshape(4 * rows_per * wave_blocks, 2 * inner_width),
        inner_table,
        (((1,), (1,)), ((), ())),
        precision=exact_mode,
    )
    cycle_sums = cycle_sums.reshape(2, 2 * rows_per, wave_blocks, lon_slots)
    values = jnp.sum(cycle_sums[0] * outer_cos[None] - cycle_sums[1] * outer_sin[None], axis=1)
    values = jnp.where(live_points[None, :], values, 0.0)
    smooth_rows = values[:rows_per].reshape(FIELDS, LEVELS, lon_slots)
    slope_rows = values[rows_per:].reshape(FIELDS, LEVELS, lon_slots)
    bracket = smooth_rows[0] * slope_rows[1] - smooth_rows[1] * slope_rows[0]
    return (smooth_rows[:, :, None, :], bracket[:, None, :])


def solution(mesh):
    axes = (mesh.shape["wave"], mesh.shape["hemi"], mesh.shape["fld"])
    bands, hemis, sides = axes
    placed = (
        P(None, None, ("wave", "hemi", "fld"), None),
        P(("wave", "hemi", "fld")),
        P(),
        P(("wave", "fld"), "hemi", None, None, None),
        P(),
    )
    fits = bands == 8 and hemis == 2 and sides == 2 and M == 24 * bands * hemis * sides
    step = functools.partial(fast_device, axes) if fits else general_device
    return jax.shard_map(
        step,
        mesh=mesh,
        in_specs=placed,
        out_specs=(
            P(None, None, ("wave", "hemi", "fld"), None),
            P(None, ("wave", "hemi", "fld"), None),
        ),
        check_vma=False,
    )
```

```python
import functools
import math

import jax
import jax.numpy as jnp
from jax import lax
from jax.experimental import pallas as pl
from jax.experimental.pallas import tpu as pltpu
from jax.sharding import PartitionSpec as P

LANES = 128
SUB = 8
HALF = LANES // 2
F32 = jnp.float32
BF16 = jnp.bfloat16
NN = (((1,), (0,)), ((), ()))
NT = (((1,), (1,)), ((), ()))
TN = (((0,), (0,)), ((), ()))
MESH = pl.DeviceIdType.MESH


def round_up(value, step):
    return -(-value // step) * step


def mxu(a, b, dims=NN):
    return lax.dot_general(a, b, dims, preferred_element_type=F32)


def split(x):
    high = x.astype(BF16)
    return high, (x - high.astype(F32)).astype(BF16)


def iota(shape, axis):
    return lax.broadcasted_iota(jnp.int32, shape, axis)


def sine_turn(x):
    y = x * x
    total = jnp.full_like(y, 0.0)
    for power in (13, 11, 9, 7, 5, 3, 1):
        sign = 1.0 if power % 4 == 1 else -1.0
        total = total * y + sign * (2.0 * math.pi) ** power / math.factorial(power)
    return total * x


def turn_tables(steps, period):
    inverse = 1.0 / period
    rest = steps - jnp.floor(steps * inverse) * period
    turn = rest * inverse
    turn = turn - jnp.floor(turn + 0.5)
    shifted = turn - 0.25
    shifted = jnp.where(shifted < -0.5, shifted + 1.0, shifted)
    return sine_turn(0.25 - jnp.abs(turn)), sine_turn(0.25 - jnp.abs(shifted))


def length_of(lon_ref):
    count = lon_ref[0]
    return count, lax.shift_right_logical(count, 2), jnp.full((1, 1), count.astype(F32), F32)


def fold_tables(n_float, quarter):
    steps = iota((8, quarter), 0) * iota((8, quarter), 1)
    return turn_tables(steps.astype(F32), n_float)


def roll_lanes(x, amount):
    amount = amount % x.shape[1]
    return x if amount == 0 else pltpu.roll(x, amount, 1)


def lane_gather(tile, index):
    return jnp.take_along_axis(tile, index, axis=1, mode="promise_in_bounds")


def window_at(tiles, start, most, count):
    whole = lax.shift_right_logical(start, 7)
    bits = (most // LANES).bit_length()
    for bit in reversed(range(bits)):
        step = 1 << bit
        keep = count + step
        hit = jnp.full(tiles[0].shape, whole, jnp.int32) & step != 0
        tiles = [
            jnp.where(hit, tiles[i + step], tiles[i]) if i + step < len(tiles) else tiles[i]
            for i in range(min(keep, len(tiles)))
        ]
    lane = iota(tiles[0].shape, 1) + jnp.full(tiles[0].shape, start & (LANES - 1), jnp.int32)
    index = lane & (LANES - 1)
    turned = [lane_gather(tile, index) for tile in tiles[: count + 1]]
    inside = lane < LANES
    return jnp.concatenate(
        [jnp.where(inside, turned[i], turned[i + 1]) for i in range(count)], axis=1
    )


def half_low(shape):
    return iota(shape, 1) < HALF


def wave_of(tile, shape):
    lane = iota(shape, 1)
    if tile < 4:
        return 4 * lane + tile
    step = jnp.where(lane < HALF, lane, lane - HALF)
    return 4 * (LANES + step) + 2 * (tile - 4) + jnp.where(lane < HALF, 0, 1)


def pick(tiles, tile_id, lane_id):
    out = None
    for i, tile in enumerate(tiles):
        moved = lane_gather(tile, lane_id)
        out = moved if out is None else jnp.where(tile_id == i, moved, out)
    return out


def slot_waves(wave_row, owners):
    row = jnp.broadcast_to(wave_row.astype(F32), (SUB, wave_row.shape[1]))
    tiles = [row[:, i * LANES : (i + 1) * LANES] for i in range(row.shape[1] // LANES)]
    slots = row.shape[1] // owners
    lane = iota((SUB, LANES), 1)
    out = []
    for group in range(slots // SUB):
        for part in range(owners // 16):
            slot = (part * 16 + lane // SUB) * slots + group * SUB + lane % SUB
            first = part * 16 * slots // LANES
            last = ((part * 16 + 15) * slots + group * SUB + SUB - 1) // LANES
            out.append(pick(tiles[first : last + 1], slot // LANES - first, slot % LANES))
    return out


def build_tables(lon_ref, rows, table_ref, low_table, pieces, lon_slots):
    quarter = table_ref.shape[1]
    waves4 = table_ref.shape[0] // 2
    _, fourth, _ = length_of(lon_ref)
    fourth_float = jnp.full((1, 1), fourth.astype(F32), F32)
    c_steps = iota((waves4, LANES), 0)
    lane_steps = iota((waves4, LANES), 1)
    near_cos, near_sin = turn_tables((c_steps * lane_steps).astype(F32), fourth_float)
    far_cos, far_sin = turn_tables((c_steps * lane_steps * LANES).astype(F32), fourth_float)
    rest = waves4 - LANES
    for block in range(quarter // LANES):
        fc, fs = far_cos[:, block : block + 1], far_sin[:, block : block + 1]
        cols = pl.ds(block * LANES, LANES)
        for part, value in enumerate(
            (near_cos * fc - near_sin * fs, near_cos * fs + near_sin * fc)
        ):
            high, low = split(value)
            for ref, half in ((table_ref, high), (low_table, low)):
                ref[pl.ds(part * LANES, LANES), cols] = half[:LANES]
                ref[pl.ds(2 * LANES + part * rest, rest), cols] = half[LANES:]


def forward_stage(lon_ref, rows, table_ref, low_table, waves, flip, send_ref, lon_slots):
    quarter = table_ref.shape[1]
    count, fourth, n_float = length_of(lon_ref)
    live = iota((8, quarter), 1) < fourth
    tiles = [rows[:, i * LANES : (i + 1) * LANES] for i in range(rows.shape[1] // LANES)]
    parts = [rows[:, :quarter]]
    for a in range(1, 4):
        parts.append(window_at(tiles, fourth * a, a * (lon_slots // 4), quarter // LANES))
    x0, x1, x2, x3 = [jnp.where(live, part, 0.0) for part in parts]
    fold_cos, fold_sin = fold_tables(n_float, quarter)
    c1, s1, c2, s2 = fold_cos[1:2], fold_sin[1:2], fold_cos[2:3], fold_sin[2:3]
    c3, s3 = fold_cos[3:4], fold_sin[3:4]
    a02, d02, a13, d13 = x0 + x2, x0 - x2, x1 + x3, x1 - x3
    even = a02 - a13
    z = jnp.concatenate(
        [
            a02 + a13,
            d02 * c1 - d13 * s1,
            even * c2,
            d02 * c3 + d13 * s3,
            jnp.zeros_like(x0),
            -d13 * c1 - d02 * s1,
            -even * s2,
            d13 * c3 - d02 * s3,
        ],
        axis=0,
    )
    z_high, z_low = split(z)
    both = mxu(jnp.concatenate([z_high, z_low], axis=0), table_ref[...], NT)
    total = both[:64] + both[64:] + mxu(z_high, low_table[...], NT)
    t0, t1, t2 = (total[:, i * LANES : (i + 1) * LANES] for i in range(3))
    near = [t0[:32] + t1[32:], t0[32:] - t1[:32]]
    turned = roll_lanes(t2, HALF)
    low = half_low((32, LANES))
    far = [
        jnp.where(low, t2[:32], turned[:32]) + jnp.where(low, turned[32:], t2[32:]),
        jnp.where(low, t2[32:], turned[32:]) - jnp.where(low, turned[:32], t2[:32]),
    ]
    scale = 1.0 / jnp.sqrt(n_float)
    low = half_low((8, LANES))
    sources = []
    for tile in range(6):
        if tile < 4:
            halves = [part[8 * tile : 8 * tile + 8] for part in near]
        else:
            r = 2 * (tile - 4)
            halves = [
                jnp.where(low, part[8 * r : 8 * r + 8], part[8 * r + 8 : 8 * r + 16])
                for part in far
            ]
        keep = 2 * wave_of(tile, (8, LANES)) < count
        sources.append([jnp.where(keep, half * scale, 0.0) for half in halves])
    moved = []
    for wave in waves:
        m = wave.astype(jnp.int32)
        r, c = m % 4, m // 4
        tile_id = jnp.where(c < LANES, r, 4 + r // 2)
        lane_id = jnp.where(c < LANES, c, c - LANES + HALF * (r % 2))
        for part in range(2):
            moved.append(pick([source[part] for source in sources], tile_id, lane_id))
    moved.append(jnp.zeros((LANES - 8 * len(moved), LANES), F32))
    flip[...] = jnp.concatenate(moved, axis=0).T
    lane_block = iota((16, LANES), 1) // 16
    lines = [flip[pl.ds(s, 16, stride=SUB), :] for s in range(SUB)]
    for t in range(len(waves)):
        out = None
        for s in range(SUB):
            line = roll_lanes(lines[s], 16 * (s - t))
            out = line if out is None else jnp.where(lane_block == s, line, out)
        send_ref[pl.ds(16 * SUB * (t % 2) + t // 2, 16, stride=SUB), :] = out


def home_part(back_recv, flip, places, groups, first):
    lane_block = iota((16, LANES), 1) // 16
    tiles = [(g, part) for g in range(groups) for part in range(2)]
    lines = [
        back_recv[pl.ds(16 * SUB * part + g, 16, stride=SUB), :] for g, part in tiles
    ]
    for s in range(SUB):
        out = None
        for t in range(len(tiles)):
            line = roll_lanes(lines[t], 16 * (t - s))
            out = line if out is None else jnp.where(lane_block == t, line, out)
        flip[pl.ds(s, 16, stride=SUB), :] = out
    turned = flip[...].T
    picked = []
    for tile in range(6):
        code = places[pl.ds(tile * SUB, SUB), :]
        tile_id, lane_id = code // LANES - first, code % LANES
        picked.append(
            [
                pick(
                    [turned[16 * t + at : 16 * t + at + 8] for t in range(len(tiles))],
                    tile_id,
                    lane_id,
                )
                for at in (0, 8)
            ]
        )
    return picked


def find_places(waves, places):
    stacked = jnp.concatenate(
        [wave[0:1] for wave in waves] + [jnp.zeros((LANES - len(waves), LANES), F32)], axis=0
    ).T
    place = iota((LANES, LANES), 0).astype(F32)
    for tile in range(6):
        want = wave_of(tile, (LANES, LANES)).astype(F32)
        total = jnp.zeros((LANES, LANES), F32)
        for t in range(len(waves)):
            total = jnp.where(stacked[:, t : t + 1] == want, place + float(LANES * t), total)
        places[pl.ds(tile * SUB, SUB), :] = jnp.broadcast_to(
            jnp.sum(total, axis=0, keepdims=True), (SUB, LANES)
        ).astype(jnp.int32)


def damping_table(wave_count, stiff_ref, wave_ref, first, damp):
    groups, k_count, width = damp.shape
    lane = iota((SUB, width), 1)
    field = lane // 4 % 2
    stiff = jnp.where(field == 0, stiff_ref[0], stiff_ref[1])
    for g in range(groups):
        wave = lane // LANES
        for s in range(SUB):
            wave = wave + jnp.where(lane // 16 % SUB == s, wave_ref[first + g * SUB + s], 0)
        degrees = wave[0:1] + 2 * iota((k_count, width), 0)
        degree_float = degrees.astype(F32)
        ratio = degree_float * (degree_float + 1.0) / (wave_count * (wave_count - 1))
        damp[g] = jnp.where(degrees < wave_count, 1.0 / (1.0 + stiff[0:1] * ratio), 0.0)


def left_lines(count, wave_count, halves, last, places, left_ref):
    low = half_low((16, LANES))
    near_re, near_im, far_re, far_im = [], [], [], []
    for tile in range(6):
        first = places[pl.ds(tile * SUB, SUB), :] < last * LANES
        m = wave_of(tile, (8, LANES))
        weight = jnp.where(2 * m < count, jnp.where(m == 0, 1.0, 2.0), 0.0)
        steep = m.astype(F32) / wave_count
        real, imag = (
            jnp.where(first, early, late) * weight
            for early, late in zip(halves[0][tile], halves[1][tile])
        )
        cre = jnp.concatenate([real, -imag * steep], axis=0)
        cim = jnp.concatenate([imag, real * steep], axis=0)
        if tile < 4:
            near_re.append(cre)
            near_im.append(cim)
        else:
            cre_turned, cim_turned = roll_lanes(cre, HALF), roll_lanes(cim, HALF)
            far_re += [jnp.where(low, cre, -cim_turned), jnp.where(low, cre_turned, -cim)]
            far_im += [jnp.where(low, cim, cre_turned), jnp.where(low, cim_turned, cre)]
    lines = [
        jnp.concatenate([near_re[r], -near_im[r], far_re[r]], axis=1) for r in range(4)
    ] + [jnp.concatenate([near_im[r], near_re[r], far_im[r]], axis=1) for r in range(1, 4)]
    for at, line in enumerate(lines):
        left_ref[pl.ds(16 * at, 16), :] = line.astype(BF16)


def middle_kernel(
    axes, wave_count, lon_ref, stiff_hbm, wave_hbm, grid_ref, legendre_ref,
    left_ref, table_ref,
    stiff_ref, wave_ref, wave_row_ref, rows, low_table, flip, send_ref, recv, back_send, back_recv,
    weights, damp, places, other_flip, last_send, last_recv,
    send_sem, recv_sem, back_send_sem, back_recv_sem, own_sem, swap_send_sem, swap_recv_sem, in_sem, near_sem, all_sem,
):
    bands, hemis, sides = axes
    devices = bands * hemis * sides
    w, h, f = lax.axis_index("wave"), lax.axis_index("hemi"), lax.axis_index("fld")
    owner = (w * sides + f) * hemis + h
    groups = weights.shape[0]
    lon_slots = grid_ref.shape[3]
    first = owner * groups * SUB

    def partner(i):
        iz, ix, ih, side = i // 8, i // 4 % 2, i // 2 % 2, i % 2
        z, x = w // 2, lax.rem(w, 2)
        pz = (z, z + 1 - 2 * lax.rem(z, 2), lax.rem(z + 2, 4), 3 - z)[iz]
        px = 1 - x if ix else x
        return pz * 2 + px, (1 - h if ih else h), (1 - f if side else f), ih

    far_first = sorted(
        range(1, devices), key=lambda i: -(i // 8 + i // 4 % 2 + i // 2 % 2 + 0.1 * (i % 2))
    )
    barrier = pltpu.get_barrier_semaphore()
    greeted = [partner(i)[:2] + (0,) for i in far_first if i > 1 and i % 2 == 0]
    for device in greeted + [(w, h, 1 - f), (w, 1 - h, 1)]:
        pl.semaphore_signal(barrier, inc=1, device_id=device, device_id_type=MESH)

    wave_row_in = pltpu.make_async_copy(wave_hbm, wave_row_ref, in_sem.at[0])
    wave_in = pltpu.make_async_copy(wave_hbm, wave_ref, in_sem.at[1])
    stiff_in = pltpu.make_async_copy(stiff_hbm, stiff_ref, in_sem.at[2])
    wave_row_in.start()
    grid_in = [
        pltpu.make_async_copy(
            grid_ref.at[r // grid_ref.shape[1], r % grid_ref.shape[1]],
            rows.at[pl.ds(r, 1), pl.ds(0, lon_slots)],
            in_sem.at[3 + r],
        )
        for r in range(8)
    ]
    for copy in grid_in:
        copy.start()
    own_in = pltpu.make_async_copy(
        legendre_ref.at[h], weights.at[:, pl.ds(0, LANES)], own_sem.at[0]
    )
    own_in.start()
    wave_in.start()
    stiff_in.start()
    rows[:, pl.ds(lon_slots, rows.shape[1] - lon_slots)] = jnp.zeros(
        (8, rows.shape[1] - lon_slots), F32
    )
    build_tables(lon_ref, rows, table_ref, low_table, None, lon_slots)
    swap = [
        pltpu.make_async_remote_copy(
            src_ref=legendre_ref.at[1 - h, g],
            dst_ref=weights.at[g, pl.ds(LANES, LANES)],
            send_sem=swap_send_sem.at[g],
            recv_sem=swap_recv_sem.at[g],
            device_id=(w, 1 - h, f),
            device_id_type=MESH,
        )
        for g in range(groups)
    ]

    @pl.when(f == 1)
    def _():
        pl.semaphore_wait(barrier, hemis * sides - 1)
        pl.semaphore_signal(near_sem, inc=1, device_id=(w, h, 0), device_id_type=MESH)

    @pl.when(f == 0)
    def _():
        pl.semaphore_wait(near_sem, 1)

    for copy in swap[:1]:
        copy.start()
    late = w // 2 + lax.rem(w, 2) + h >= 4

    @pl.when(jnp.logical_not(late))
    def _():
        for copy in swap[1:2]:
            copy.start()

    wave_row_in.wait()
    waves = slot_waves(wave_row_ref[...].reshape(1, -1), devices)
    for copy in grid_in:
        copy.wait()
    forward_stage(lon_ref, rows, table_ref, low_table, waves, flip, send_ref, lon_slots)

    def slice_of(ref, place, count):
        return ref.at[pl.ds(pl.multiple_of(place * SUB, SUB), count)]

    def everything(ref, count):
        return ref.at[pl.ds(0, (devices - 1) * count)]

    def copies(source, target, source_place, target_place, sent, got, count):
        return [
            pltpu.make_async_remote_copy(
                src_ref=slice_of(source, source_place(*partner(i)), count),
                dst_ref=slice_of(target, target_place(*partner(i)), count),
                send_sem=sent,
                recv_sem=got,
                device_id=partner(i)[:3],
                device_id_type=MESH,
            )
            for i in far_first
        ]

    def whole(source, target, sent, got, count):
        return pltpu.make_async_remote_copy(
            src_ref=everything(source, count),
            dst_ref=everything(target, count),
            send_sem=sent,
            recv_sem=got,
            device_id=partner(1)[:3],
            device_id_type=MESH,
        )

    out_copies = copies(
        send_ref,
        recv,
        lambda pw, ph, pf, ih: (pw * sides + pf) * hemis + ph,
        lambda pw, ph, pf, ih: ih * 2 * bands + f * bands + w,
        send_sem.at[0],
        recv_sem.at[0],
        groups,
    )
    out_whole = whole(send_ref, recv, send_sem.at[0], recv_sem.at[0], groups)
    @pl.when(f == 0)
    def _():
        pl.semaphore_wait(barrier, devices - 1)
        pl.semaphore_signal(all_sem, inc=1, device_id=(w, h, 1), device_id_type=MESH)

    @pl.when(f == 1)
    def _():
        pl.semaphore_wait(all_sem, 1)

    for copy in out_copies:
        copy.start()

    @pl.when(late)
    def _():
        for copy in swap[1:2]:
            copy.start()

    for copy in swap[2:]:
        copy.start()
    slice_of(recv, f * bands + w, groups)[...] = slice_of(send_ref, owner, groups)[...]
    wave_in.wait()
    stiff_in.wait()
    damping_table(wave_count, stiff_ref, wave_ref, first, damp)
    find_places(waves, places)
    own_in.wait()
    out_whole.wait_recv()

    home_rows = (groups - 1, 1)
    home_whole = [
        whole(source, target, back_send_sem.at[at], back_recv_sem.at[at], home_rows[at])
        for at, (source, target) in enumerate(((back_send, back_recv), (last_send, last_recv)))
    ]

    def send_home(at):
        source, target = ((back_send, back_recv), (last_send, last_recv))[at]
        for copy in copies(
            source,
            target,
            lambda pw, ph, pf, ih: ih * 2 * bands + pf * bands + pw,
            lambda pw, ph, pf, ih: owner,
            back_send_sem.at[at],
            back_recv_sem.at[at],
            home_rows[at],
        ):
            copy.start()
        slice_of(target, owner, home_rows[at])[...] = slice_of(
            source, f * bands + w, home_rows[at]
        )[...]

    lane_slot = iota((SUB, LANES), 1) // 16
    zero = jnp.zeros((SUB, LANES), F32)
    for g in range(groups):
        blocks = []
        for rel in range(hemis):
            base = rel * 2 * bands * SUB + g
            north = recv[pl.ds(base, bands, stride=SUB), :]
            south = recv[pl.ds(base + bands * SUB, bands, stride=SUB), :]
            even, odd = north + south, north - south
            for s in range(SUB):
                blocks.append(
                    jnp.concatenate([jnp.where(lane_slot == s, even, 0.0), zero], axis=1)
                )
                blocks.append(
                    jnp.concatenate([zero, jnp.where(lane_slot == s, odd, 0.0)], axis=1)
                )
        spaced = jnp.concatenate(blocks, axis=0).astype(BF16)
        swap[g].wait_recv()
        spectral = mxu(weights[g], spaced, TN)
        damped = (spectral * damp[g]).astype(BF16)
        full = mxu(weights[g], damped)
        for rel in range(hemis):
            sums = []
            for q in range(2):
                total = None
                for s in range(SUB):
                    at = rel * LANES + s * 16 + q * SUB
                    piece = full[at : at + SUB, q * LANES : (q + 1) * LANES]
                    total = piece if total is None else jnp.where(lane_slot == s, piece, total)
                sums.append(total)
            target, base = back_send, rel * 2 * bands * SUB + g
            if g == groups - 1:
                target, base = last_send, rel * 2 * bands * SUB
            target[pl.ds(base, bands, stride=SUB), :] = sums[0] + sums[1]
            target[pl.ds(base + bands * SUB, bands, stride=SUB), :] = sums[0] - sums[1]
        if g >= groups - 2:
            send_home(g - groups + 2)

    halves = []
    for at in range(2):
        home_whole[at].wait_recv()
        halves.append(
            home_part(
                (back_recv, last_recv)[at], (flip, other_flip)[at], places, home_rows[at],
                2 * (groups - 1) * at,
            )
        )
    left_lines(lon_ref[0], wave_count, halves, 2 * (groups - 1), places, left_ref)
    for copy in swap:
        copy.wait_send()
    out_whole.wait_send()
    for copy in home_whole:
        copy.wait_send()


def inverse_kernel(wave_count, lon_ref, left_ref, table_ref, smooth_ref, bracket_ref, acc):
    fields, levels, _, lon_slots = smooth_ref.shape
    quarter = table_ref.shape[1]
    count, fourth, n_float = length_of(lon_ref)
    acc[...] = jnp.zeros_like(acc)
    fold_cos, fold_sin = fold_tables(n_float, quarter)
    sums = mxu(left_ref[...], table_ref[...])
    re = [sums[16 * r : 16 * r + 16] for r in range(4)]
    im = [None] + [sums[48 + 16 * r : 64 + 16 * r] for r in range(1, 4)]
    cos = [fold_cos[r : r + 1] for r in range(4)]
    sin = [fold_sin[r : r + 1] for r in range(4)]
    h0 = re[0]
    h1r, h1i = re[1] * cos[1] - im[1] * sin[1], re[1] * sin[1] + im[1] * cos[1]
    h2 = re[2] * cos[2] - im[2] * sin[2]
    h3r, h3i = re[3] * cos[3] - im[3] * sin[3], re[3] * sin[3] + im[3] * cos[3]
    even, odd, cross, turn = h0 + h2, h0 - h2, h1r + h3r, h3i - h1i
    live = iota((16, quarter), 1) < fourth
    scale = 1.0 / jnp.sqrt(n_float)
    width = quarter + LANES
    for a, value in enumerate((even + cross, odd + turn, even - cross, odd - turn)):
        value = jnp.where(live, value * scale, 0.0)
        smooth, slope = value[0:8], value[8:16]
        flipped = jnp.concatenate([slope[4:8], slope[0:4]], axis=0)
        product = smooth * flipped
        bracket = product - jnp.concatenate([product[4:8], product[0:4]], axis=0)
        segment = jnp.concatenate([smooth, bracket], axis=0)
        segment = jnp.concatenate([segment, jnp.zeros((16, LANES), F32)], axis=1)
        start = fourth * a
        segment = pltpu.roll(segment, lax.rem(start, LANES), 1)
        aligned = pl.multiple_of((start // LANES) * LANES, LANES)
        acc[:, pl.ds(aligned, width)] += segment
    for f in range(fields):
        for l in range(levels):
            smooth_ref[f, l] = acc[pl.ds(f * levels + l, 1), pl.ds(0, lon_slots)]
    for l in range(levels):
        bracket_ref[l] = acc[pl.ds(8 + l, 1), pl.ds(0, lon_slots)]


def in_hbm(x):
    return pltpu.with_memory_space_constraint(x, pltpu.HBM)


def fast_device(axes, grid, lon_count, wave_order, legendre, stiffness):
    bands, hemis, sides = axes
    owners = bands * hemis * sides
    wave_count = wave_order.shape[0]
    fields, levels, _, lon_slots = grid.shape
    groups = wave_count // owners // SUB
    k_count = legendre.shape[4]
    quarter = round_up(lon_slots // 4, LANES)
    waves4 = wave_count // 4
    long_rows = lon_slots + 2 * LANES
    smem = pl.BlockSpec(memory_space=pltpu.SMEM)
    vmem = pl.BlockSpec(memory_space=pltpu.VMEM)
    hbm = pl.BlockSpec(memory_space=pltpu.HBM)
    weights = legendre.reshape(hemis, groups, LANES, k_count)
    message = pltpu.VMEM((owners * SUB, LANES), F32)
    left, table = pl.pallas_call(
        functools.partial(middle_kernel, axes, wave_count),
        out_shape=(
            pltpu.VMEM((7 * 16, 2 * waves4), BF16),
            pltpu.VMEM((2 * waves4, quarter), BF16),
        ),
        in_specs=[smem, hbm, hbm, hbm, hbm],
        out_specs=(vmem, vmem),
        scratch_shapes=[
            pltpu.SMEM(stiffness.shape, F32),
            pltpu.SMEM(wave_order.shape, jnp.int32),
            pltpu.VMEM(wave_order.shape, jnp.int32),
            pltpu.VMEM((8, long_rows), F32),
            pltpu.VMEM((2 * waves4, quarter), BF16),
            pltpu.VMEM((LANES, LANES), F32),
            message,
            message,
            message,
            message,
            pltpu.VMEM((groups, 2 * LANES, k_count), BF16),
            pltpu.VMEM((groups, k_count, 2 * LANES), F32),
            pltpu.VMEM((6 * SUB, LANES), jnp.int32),
            pltpu.VMEM((LANES, LANES), F32),
            message,
            message,
            pltpu.SemaphoreType.DMA((1,)),
            pltpu.SemaphoreType.DMA((1,)),
            pltpu.SemaphoreType.DMA((2,)),
            pltpu.SemaphoreType.DMA((2,)),
            pltpu.SemaphoreType.DMA((1,)),
            pltpu.SemaphoreType.DMA((groups,)),
            pltpu.SemaphoreType.DMA((groups,)),
            pltpu.SemaphoreType.DMA((11,)),
            pltpu.SemaphoreType.REGULAR,
            pltpu.SemaphoreType.REGULAR,
        ],
        compiler_params=pltpu.CompilerParams(
            collective_id=0, has_side_effects=True, vmem_limit_bytes=24 << 20
        ),
        name="middle",
    )(lon_count, *[in_hbm(x) for x in (stiffness, wave_order, grid, weights)])
    return pl.pallas_call(
        functools.partial(inverse_kernel, wave_count),
        out_shape=(
            jax.ShapeDtypeStruct(grid.shape, F32),
            jax.ShapeDtypeStruct((levels, 1, lon_slots), F32),
        ),
        in_specs=[smem, vmem, vmem],
        out_specs=(vmem, vmem),
        scratch_shapes=[pltpu.VMEM((16, long_rows), F32)],
        compiler_params=pltpu.CompilerParams(vmem_limit_bytes=24 << 20),
        name="inverse",
    )(lon_count, left, table)


M = 768
FIELDS = 2
LEVELS = 4
K = 384


exact_mode = lax.Precision.HIGHEST


def general_device(grid, lon_count, wave_order, legendre, stiffness):
    lon_slots = grid.shape[3]
    rows_per = FIELDS * LEVELS
    channels = 2 * rows_per
    inner_width = 64
    wave_blocks = M // inner_width
    band_count = lax.axis_size("wave")
    slot_dev = M // (2 * band_count)
    cycle_length = lon_count[0]
    longitudes = jnp.arange(lon_slots, dtype=jnp.int32)
    wavenumbers = jnp.arange(M, dtype=jnp.int32)
    angle_step = 2.0 * jnp.pi / cycle_length.astype(jnp.float32)
    block_starts = jnp.arange(wave_blocks, dtype=jnp.int32) * inner_width
    inner_waves = jnp.arange(inner_width, dtype=jnp.int32)
    outer_angle = angle_step * (block_starts[:, None] * longitudes[None, :] % cycle_length).astype(
        jnp.float32
    )
    outer_cos = jnp.cos(outer_angle)
    outer_sin = jnp.sin(outer_angle)
    inner_angle = angle_step * (longitudes[:, None] * inner_waves[None, :] % cycle_length).astype(
        jnp.float32
    )
    inner_table = jnp.concatenate([jnp.cos(inner_angle), jnp.sin(inner_angle)], axis=1)
    cycle_scale = 1.0 / jnp.sqrt(cycle_length.astype(jnp.float32))
    live_points = longitudes < cycle_length
    wave_live = 2 * wavenumbers < cycle_length
    cycle_rows = jnp.where(live_points[None, :], grid[:, :, 0, :].reshape(rows_per, lon_slots), 0.0)
    modulated = jnp.stack(
        [cycle_rows[:, None, :] * outer_cos[None], -(cycle_rows[:, None, :] * outer_sin[None])]
    )
    product = jnp.dot(
        modulated.reshape(2 * rows_per * wave_blocks, lon_slots), inner_table, precision=exact_mode
    )
    product = product.reshape(2, rows_per, wave_blocks, 2 * inner_width)
    real_part = product[0, :, :, :inner_width] + product[1, :, :, inner_width:]
    imag_part = product[1, :, :, :inner_width] - product[0, :, :, inner_width:]
    fourier = jnp.stack([real_part, imag_part]).reshape(channels, M) * cycle_scale
    fourier = jnp.where(wave_live[None, :], fourier, 0.0)
    slotted = fourier[:, wave_order].reshape(channels, band_count, 2, slot_dev)
    side_index = lax.axis_index("fld")
    arrived = lax.all_to_all(
        lax.all_to_all(slotted[None, :, None], "wave", split_axis=3, concat_axis=2, tiled=True),
        "fld",
        split_axis=4,
        concat_axis=0,
        tiled=True,
    )
    stacked = arrived.reshape(2, channels, band_count, slot_dev)
    even_part = (stacked[0] + stacked[1]).astype(jnp.bfloat16)
    odd_part = (stacked[0] - stacked[1]).astype(jnp.bfloat16)
    parities = jnp.stack([even_part, odd_part])
    weights = legendre[:, 0]
    owner_index = lax.axis_index("wave") * 2 + side_index
    my_waves = lax.dynamic_slice_in_dim(wave_order, owner_index * slot_dev, slot_dev)
    degrees = (
        my_waves[:, None, None]
        + 2 * jnp.arange(K, dtype=jnp.int32)[None, None, :]
        + jnp.arange(2, dtype=jnp.int32)[None, :, None]
    )
    valid_degree = degrees < M
    spectral = jnp.einsum("aqwk,qcwa->aqck", weights, parities, preferred_element_type=jnp.float32)
    spectral = jnp.where(valid_degree[:, :, None, :], spectral, 0.0)
    chan_stiff = jnp.tile(jnp.repeat(stiffness, LEVELS), 2)
    degree_float = degrees.astype(jnp.float32)
    degree_ratio = degree_float * (degree_float + 1.0) / (M * (M - 1))
    summed = lax.psum(spectral, "hemi")
    damped = (
        summed / (1.0 + chan_stiff[None, None, :, None] * degree_ratio[:, :, None, :])
    ).astype(jnp.bfloat16)
    returned = jnp.einsum("aqwk,aqck->qcwa", weights, damped, preferred_element_type=jnp.float32)
    north_vals = returned[0] + returned[1]
    south_vals = returned[0] - returned[1]
    homebound = lax.all_to_all(
        lax.all_to_all(
            jnp.stack([north_vals, south_vals])[:, None, None],
            "wave",
            split_axis=4,
            concat_axis=2,
            tiled=True,
        ),
        "fld",
        split_axis=0,
        concat_axis=1,
        tiled=True,
    )
    homebound = homebound.reshape(2, band_count, channels, slot_dev)
    slot_values = jnp.transpose(homebound, (2, 1, 0, 3)).reshape(channels, M)
    spectra = jnp.zeros((channels, M), jnp.float32).at[:, wave_order].set(slot_values)
    weight_wave = jnp.where(wavenumbers == 0, 1.0, 2.0) * jnp.where(wave_live, cycle_scale, 0.0)
    real_coef = spectra[:rows_per] * weight_wave
    imag_coef = spectra[rows_per:] * weight_wave
    wave_ratio = wavenumbers.astype(jnp.float32) / M
    cos_coef = jnp.stack([real_coef, -(imag_coef * wave_ratio)]).reshape(
        2 * rows_per, wave_blocks, inner_width
    )
    sin_coef = jnp.stack([imag_coef, real_coef * wave_ratio]).reshape(
        2 * rows_per, wave_blocks, inner_width
    )
    left_rows = jnp.stack(
        [
            jnp.concatenate([cos_coef, -sin_coef], axis=2),
            jnp.concatenate([sin_coef, cos_coef], axis=2),
        ]
    )
    cycle_sums = lax.dot_general(
        left_rows.reshape(4 * rows_per * wave_blocks, 2 * inner_width),
        inner_table,
        (((1,), (1,)), ((), ())),
        precision=exact_mode,
    )
    cycle_sums = cycle_sums.reshape(2, 2 * rows_per, wave_blocks, lon_slots)
    values = jnp.sum(cycle_sums[0] * outer_cos[None] - cycle_sums[1] * outer_sin[None], axis=1)
    values = jnp.where(live_points[None, :], values, 0.0)
    smooth_rows = values[:rows_per].reshape(FIELDS, LEVELS, lon_slots)
    slope_rows = values[rows_per:].reshape(FIELDS, LEVELS, lon_slots)
    bracket = smooth_rows[0] * slope_rows[1] - smooth_rows[1] * slope_rows[0]
    return (smooth_rows[:, :, None, :], bracket[:, None, :])


def solution(mesh):
    axes = (mesh.shape["wave"], mesh.shape["hemi"], mesh.shape["fld"])
    bands, hemis, sides = axes
    placed = (
        P(None, None, ("wave", "hemi", "fld"), None),
        P(("wave", "hemi", "fld")),
        P(),
        P(("wave", "fld"), "hemi", None, None, None),
        P(),
    )
    fits = bands == 8 and hemis == 2 and sides == 2 and M == 24 * bands * hemis * sides
    step = functools.partial(fast_device, axes) if fits else general_device
    return jax.shard_map(
        step,
        mesh=mesh,
        in_specs=placed,
        out_specs=(
            P(None, None, ("wave", "hemi", "fld"), None),
            P(None, ("wave", "hemi", "fld"), None),
        ),
        check_vma=False,
    )
```

```python
import functools
import math

import jax
import jax.numpy as jnp
from jax import lax
from jax.experimental import pallas as pl
from jax.experimental.pallas import tpu as pltpu
from jax.sharding import PartitionSpec as P

LANES = 128
SUB = 8
HALF = LANES // 2
F32 = jnp.float32
BF16 = jnp.bfloat16
NN = (((1,), (0,)), ((), ()))
NT = (((1,), (1,)), ((), ()))
TN = (((0,), (0,)), ((), ()))
MESH = pl.DeviceIdType.MESH


def round_up(value, step):
    return -(-value // step) * step


def mxu(a, b, dims=NN):
    return lax.dot_general(a, b, dims, preferred_element_type=F32)


def split(x):
    high = x.astype(BF16)
    return high, (x - high.astype(F32)).astype(BF16)


def iota(shape, axis):
    return lax.broadcasted_iota(jnp.int32, shape, axis)


def sine_turn(x):
    y = x * x
    total = jnp.full_like(y, 0.0)
    for power in (13, 11, 9, 7, 5, 3, 1):
        sign = 1.0 if power % 4 == 1 else -1.0
        total = total * y + sign * (2.0 * math.pi) ** power / math.factorial(power)
    return total * x


def turn_tables(steps, period):
    inverse = 1.0 / period
    rest = steps - jnp.floor(steps * inverse) * period
    turn = rest * inverse
    turn = turn - jnp.floor(turn + 0.5)
    shifted = turn - 0.25
    shifted = jnp.where(shifted < -0.5, shifted + 1.0, shifted)
    return sine_turn(0.25 - jnp.abs(turn)), sine_turn(0.25 - jnp.abs(shifted))


def length_of(lon_ref):
    count = lon_ref[0]
    return count, lax.shift_right_logical(count, 2), jnp.full((1, 1), count.astype(F32), F32)


def fold_tables(n_float, quarter):
    steps = iota((8, quarter), 0) * iota((8, quarter), 1)
    return turn_tables(steps.astype(F32), n_float)


def roll_lanes(x, amount):
    amount = amount % x.shape[1]
    return x if amount == 0 else pltpu.roll(x, amount, 1)


def lane_gather(tile, index):
    return jnp.take_along_axis(tile, index, axis=1, mode="promise_in_bounds")


def window_at(tiles, start, most, count):
    whole = lax.shift_right_logical(start, 7)
    bits = (most // LANES).bit_length()
    for bit in reversed(range(bits)):
        step = 1 << bit
        keep = count + step
        hit = jnp.full(tiles[0].shape, whole, jnp.int32) & step != 0
        tiles = [
            jnp.where(hit, tiles[i + step], tiles[i]) if i + step < len(tiles) else tiles[i]
            for i in range(min(keep, len(tiles)))
        ]
    lane = iota(tiles[0].shape, 1) + jnp.full(tiles[0].shape, start & (LANES - 1), jnp.int32)
    index = lane & (LANES - 1)
    turned = [lane_gather(tile, index) for tile in tiles[: count + 1]]
    inside = lane < LANES
    return jnp.concatenate(
        [jnp.where(inside, turned[i], turned[i + 1]) for i in range(count)], axis=1
    )


def half_low(shape):
    return iota(shape, 1) < HALF


def wave_of(tile, shape):
    lane = iota(shape, 1)
    if tile < 4:
        return 4 * lane + tile
    step = jnp.where(lane < HALF, lane, lane - HALF)
    return 4 * (LANES + step) + 2 * (tile - 4) + jnp.where(lane < HALF, 0, 1)


def pick(tiles, tile_id, lane_id):
    out = None
    for i, tile in enumerate(tiles):
        moved = lane_gather(tile, lane_id)
        out = moved if out is None else jnp.where(tile_id == i, moved, out)
    return out


def slot_waves(wave_row, owners):
    row = jnp.broadcast_to(wave_row.astype(F32), (SUB, wave_row.shape[1]))
    tiles = [row[:, i * LANES : (i + 1) * LANES] for i in range(row.shape[1] // LANES)]
    slots = row.shape[1] // owners
    lane = iota((SUB, LANES), 1)
    out = []
    for group in range(slots // SUB):
        for part in range(owners // 16):
            slot = (part * 16 + lane // SUB) * slots + group * SUB + lane % SUB
            first = part * 16 * slots // LANES
            last = ((part * 16 + 15) * slots + group * SUB + SUB - 1) // LANES
            out.append(pick(tiles[first : last + 1], slot // LANES - first, slot % LANES))
    return out


def build_tables(lon_ref, rows, table_ref, low_table, pieces, lon_slots):
    quarter = table_ref.shape[1]
    waves4 = table_ref.shape[0] // 2
    _, fourth, _ = length_of(lon_ref)
    fourth_float = jnp.full((1, 1), fourth.astype(F32), F32)
    c_steps = iota((waves4, LANES), 0)
    lane_steps = iota((waves4, LANES), 1)
    near_cos, near_sin = turn_tables((c_steps * lane_steps).astype(F32), fourth_float)
    far_cos, far_sin = turn_tables((c_steps * lane_steps * LANES).astype(F32), fourth_float)
    rest = waves4 - LANES
    for block in range(quarter // LANES):
        fc, fs = far_cos[:, block : block + 1], far_sin[:, block : block + 1]
        cols = pl.ds(block * LANES, LANES)
        for part, value in enumerate(
            (near_cos * fc - near_sin * fs, near_cos * fs + near_sin * fc)
        ):
            high, low = split(value)
            for ref, half in ((table_ref, high), (low_table, low)):
                ref[pl.ds(part * LANES, LANES), cols] = half[:LANES]
                ref[pl.ds(2 * LANES + part * rest, rest), cols] = half[LANES:]


def forward_stage(lon_ref, rows, table_ref, low_table, waves, flip, send_ref, lon_slots):
    quarter = table_ref.shape[1]
    count, fourth, n_float = length_of(lon_ref)
    live = iota((8, quarter), 1) < fourth
    tiles = [rows[:, i * LANES : (i + 1) * LANES] for i in range(rows.shape[1] // LANES)]
    parts = [rows[:, :quarter]]
    for a in range(1, 4):
        parts.append(window_at(tiles, fourth * a, a * (lon_slots // 4), quarter // LANES))
    x0, x1, x2, x3 = [jnp.where(live, part, 0.0) for part in parts]
    fold_cos, fold_sin = fold_tables(n_float, quarter)
    c1, s1, c2, s2 = fold_cos[1:2], fold_sin[1:2], fold_cos[2:3], fold_sin[2:3]
    c3, s3 = fold_cos[3:4], fold_sin[3:4]
    a02, d02, a13, d13 = x0 + x2, x0 - x2, x1 + x3, x1 - x3
    even = a02 - a13
    z = jnp.concatenate(
        [
            a02 + a13,
            d02 * c1 - d13 * s1,
            even * c2,
            d02 * c3 + d13 * s3,
            jnp.zeros_like(x0),
            -d13 * c1 - d02 * s1,
            -even * s2,
            d13 * c3 - d02 * s3,
        ],
        axis=0,
    )
    z_high, z_low = split(z)
    both = mxu(jnp.concatenate([z_high, z_low], axis=0), table_ref[...], NT)
    total = both[:64] + both[64:] + mxu(z_high, low_table[...], NT)
    t0, t1, t2 = (total[:, i * LANES : (i + 1) * LANES] for i in range(3))
    near = [t0[:32] + t1[32:], t0[32:] - t1[:32]]
    turned = roll_lanes(t2, HALF)
    low = half_low((32, LANES))
    far = [
        jnp.where(low, t2[:32], turned[:32]) + jnp.where(low, turned[32:], t2[32:]),
        jnp.where(low, t2[32:], turned[32:]) - jnp.where(low, turned[:32], t2[:32]),
    ]
    scale = 1.0 / jnp.sqrt(n_float)
    low = half_low((8, LANES))
    sources = []
    for tile in range(6):
        if tile < 4:
            halves = [part[8 * tile : 8 * tile + 8] for part in near]
        else:
            r = 2 * (tile - 4)
            halves = [
                jnp.where(low, part[8 * r : 8 * r + 8], part[8 * r + 8 : 8 * r + 16])
                for part in far
            ]
        keep = 2 * wave_of(tile, (8, LANES)) < count
        sources.append([jnp.where(keep, half * scale, 0.0) for half in halves])
    moved = []
    for wave in waves:
        m = wave.astype(jnp.int32)
        r, c = m % 4, m // 4
        tile_id = jnp.where(c < LANES, r, 4 + r // 2)
        lane_id = jnp.where(c < LANES, c, c - LANES + HALF * (r % 2))
        for part in range(2):
            moved.append(pick([source[part] for source in sources], tile_id, lane_id))
    moved.append(jnp.zeros((LANES - 8 * len(moved), LANES), F32))
    flip[...] = jnp.concatenate(moved, axis=0).T
    lane_block = iota((16, LANES), 1) // 16
    lines = [flip[pl.ds(s, 16, stride=SUB), :] for s in range(SUB)]
    for t in range(len(waves)):
        out = None
        for s in range(SUB):
            line = roll_lanes(lines[s], 16 * (s - t))
            out = line if out is None else jnp.where(lane_block == s, line, out)
        send_ref[pl.ds(16 * SUB * (t % 2) + t // 2, 16, stride=SUB), :] = out


def home_part(back_recv, flip, places, groups, first):
    lane_block = iota((16, LANES), 1) // 16
    tiles = [(g, part) for g in range(groups) for part in range(2)]
    lines = [
        back_recv[pl.ds(16 * SUB * part + g, 16, stride=SUB), :] for g, part in tiles
    ]
    for s in range(SUB):
        out = None
        for t in range(len(tiles)):
            line = roll_lanes(lines[t], 16 * (t - s))
            out = line if out is None else jnp.where(lane_block == t, line, out)
        flip[pl.ds(s, 16, stride=SUB), :] = out
    turned = flip[...].T
    picked = []
    for tile in range(6):
        code = places[pl.ds(tile * SUB, SUB), :]
        tile_id, lane_id = code // LANES - first, code % LANES
        picked.append(
            [
                pick(
                    [turned[16 * t + at : 16 * t + at + 8] for t in range(len(tiles))],
                    tile_id,
                    lane_id,
                )
                for at in (0, 8)
            ]
        )
    return picked


def find_places(waves, places):
    stacked = jnp.concatenate(
        [wave[0:1] for wave in waves] + [jnp.zeros((LANES - len(waves), LANES), F32)], axis=0
    ).T
    place = iota((LANES, LANES), 0).astype(F32)
    for tile in range(6):
        want = wave_of(tile, (LANES, LANES)).astype(F32)
        total = jnp.zeros((LANES, LANES), F32)
        for t in range(len(waves)):
            total = jnp.where(stacked[:, t : t + 1] == want, place + float(LANES * t), total)
        places[pl.ds(tile * SUB, SUB), :] = jnp.broadcast_to(
            jnp.sum(total, axis=0, keepdims=True), (SUB, LANES)
        ).astype(jnp.int32)


def damping_table(wave_count, stiff_ref, wave_ref, first, damp):
    groups, k_count, width = damp.shape
    lane = iota((SUB, width), 1)
    field = lane // 4 % 2
    stiff = jnp.where(field == 0, stiff_ref[0], stiff_ref[1])
    for g in range(groups):
        wave = lane // LANES
        for s in range(SUB):
            wave = wave + jnp.where(lane // 16 % SUB == s, wave_ref[first + g * SUB + s], 0)
        degrees = wave[0:1] + 2 * iota((k_count, width), 0)
        degree_float = degrees.astype(F32)
        ratio = degree_float * (degree_float + 1.0) / (wave_count * (wave_count - 1))
        damp[g] = jnp.where(degrees < wave_count, 1.0 / (1.0 + stiff[0:1] * ratio), 0.0)


def left_lines(count, wave_count, halves, last, places, left_ref):
    low = half_low((16, LANES))
    near_re, near_im, far_re, far_im = [], [], [], []
    for tile in range(6):
        first = places[pl.ds(tile * SUB, SUB), :] < last * LANES
        m = wave_of(tile, (8, LANES))
        weight = jnp.where(2 * m < count, jnp.where(m == 0, 1.0, 2.0), 0.0)
        steep = m.astype(F32) / wave_count
        real, imag = (
            jnp.where(first, early, late) * weight
            for early, late in zip(halves[0][tile], halves[1][tile])
        )
        cre = jnp.concatenate([real, -imag * steep], axis=0)
        cim = jnp.concatenate([imag, real * steep], axis=0)
        if tile < 4:
            near_re.append(cre)
            near_im.append(cim)
        else:
            cre_turned, cim_turned = roll_lanes(cre, HALF), roll_lanes(cim, HALF)
            far_re += [jnp.where(low, cre, -cim_turned), jnp.where(low, cre_turned, -cim)]
            far_im += [jnp.where(low, cim, cre_turned), jnp.where(low, cim_turned, cre)]
    lines = [
        jnp.concatenate([near_re[r], -near_im[r], far_re[r]], axis=1) for r in range(4)
    ] + [jnp.concatenate([near_im[r], near_re[r], far_im[r]], axis=1) for r in range(1, 4)]
    for at, line in enumerate(lines):
        left_ref[pl.ds(16 * at, 16), :] = line.astype(BF16)


def middle_kernel(
    axes, wave_count, lon_ref, stiff_hbm, wave_hbm, grid_ref, legendre_ref,
    left_ref, table_ref,
    stiff_ref, wave_ref, wave_row_ref, rows, low_table, flip, send_ref, recv, back_send, back_recv,
    weights, damp, places, other_flip, last_send, last_recv,
    send_sem, recv_sem, back_send_sem, back_recv_sem, own_sem, swap_send_sem, swap_recv_sem, in_sem, near_sem, all_sem,
):
    bands, hemis, sides = axes
    devices = bands * hemis * sides
    w, h, f = lax.axis_index("wave"), lax.axis_index("hemi"), lax.axis_index("fld")
    owner = (w * sides + f) * hemis + h
    groups = weights.shape[0]
    lon_slots = grid_ref.shape[3]
    first = owner * groups * SUB

    def partner(i):
        iz, ix, ih, side = i // 8, i // 4 % 2, i // 2 % 2, i % 2
        z, x = w // 2, lax.rem(w, 2)
        pz = (z, z + 1 - 2 * lax.rem(z, 2), lax.rem(z + 2, 4), 3 - z)[iz]
        px = 1 - x if ix else x
        return pz * 2 + px, (1 - h if ih else h), (1 - f if side else f), ih

    far_first = sorted(
        range(1, devices), key=lambda i: -(i // 8 + i // 4 % 2 + i // 2 % 2 + 0.1 * (i % 2))
    )
    barrier = pltpu.get_barrier_semaphore()
    greeted = [partner(i)[:2] + (0,) for i in far_first if i > 1 and i % 2 == 0]
    for device in greeted + [(w, h, 1 - f), (w, 1 - h, 1)]:
        pl.semaphore_signal(barrier, inc=1, device_id=device, device_id_type=MESH)

    wave_row_in = pltpu.make_async_copy(wave_hbm, wave_row_ref, in_sem.at[0])
    wave_in = pltpu.make_async_copy(wave_hbm, wave_ref, in_sem.at[1])
    stiff_in = pltpu.make_async_copy(stiff_hbm, stiff_ref, in_sem.at[2])
    wave_row_in.start()
    grid_in = [
        pltpu.make_async_copy(
            grid_ref.at[r // grid_ref.shape[1], r % grid_ref.shape[1]],
            rows.at[pl.ds(r, 1), pl.ds(0, lon_slots)],
            in_sem.at[3 + r],
        )
        for r in range(8)
    ]
    for copy in grid_in:
        copy.start()
    own_in = pltpu.make_async_copy(
        legendre_ref.at[h], weights.at[:, pl.ds(0, LANES)], own_sem.at[0]
    )
    own_in.start()
    wave_in.start()
    stiff_in.start()
    rows[:, pl.ds(lon_slots, rows.shape[1] - lon_slots)] = jnp.zeros(
        (8, rows.shape[1] - lon_slots), F32
    )
    build_tables(lon_ref, rows, table_ref, low_table, None, lon_slots)
    swap = [
        pltpu.make_async_remote_copy(
            src_ref=legendre_ref.at[1 - h, g],
            dst_ref=weights.at[g, pl.ds(LANES, LANES)],
            send_sem=swap_send_sem.at[g],
            recv_sem=swap_recv_sem.at[g],
            device_id=(w, 1 - h, f),
            device_id_type=MESH,
        )
        for g in range(groups)
    ]

    @pl.when(f == 1)
    def _():
        pl.semaphore_wait(barrier, hemis * sides - 1)
        pl.semaphore_signal(near_sem, inc=1, device_id=(w, h, 0), device_id_type=MESH)

    @pl.when(f == 0)
    def _():
        pl.semaphore_wait(near_sem, 1)

    for copy in swap[:2]:
        copy.start()
    wave_row_in.wait()
    waves = slot_waves(wave_row_ref[...].reshape(1, -1), devices)
    for copy in grid_in:
        copy.wait()
    forward_stage(lon_ref, rows, table_ref, low_table, waves, flip, send_ref, lon_slots)

    def slice_of(ref, place, count):
        return ref.at[pl.ds(pl.multiple_of(place * SUB, SUB), count)]

    def everything(ref, count):
        return ref.at[pl.ds(0, (devices - 1) * count)]

    def copies(source, target, source_place, target_place, sent, got, count):
        return [
            pltpu.make_async_remote_copy(
                src_ref=slice_of(source, source_place(*partner(i)), count),
                dst_ref=slice_of(target, target_place(*partner(i)), count),
                send_sem=sent,
                recv_sem=got,
                device_id=partner(i)[:3],
                device_id_type=MESH,
            )
            for i in far_first
        ]

    def whole(source, target, sent, got, count):
        return pltpu.make_async_remote_copy(
            src_ref=everything(source, count),
            dst_ref=everything(target, count),
            send_sem=sent,
            recv_sem=got,
            device_id=partner(1)[:3],
            device_id_type=MESH,
        )

    out_copies = copies(
        send_ref,
        recv,
        lambda pw, ph, pf, ih: (pw * sides + pf) * hemis + ph,
        lambda pw, ph, pf, ih: ih * 2 * bands + f * bands + w,
        send_sem.at[0],
        recv_sem.at[0],
        groups,
    )
    out_whole = whole(send_ref, recv, send_sem.at[0], recv_sem.at[0], groups)
    @pl.when(f == 0)
    def _():
        pl.semaphore_wait(barrier, devices - 1)
        pl.semaphore_signal(all_sem, inc=1, device_id=(w, h, 1), device_id_type=MESH)

    @pl.when(f == 1)
    def _():
        pl.semaphore_wait(all_sem, 1)

    for copy in out_copies:
        copy.start()
    for copy in swap[2:]:
        copy.start()
    slice_of(recv, f * bands + w, groups)[...] = slice_of(send_ref, owner, groups)[...]
    wave_in.wait()
    stiff_in.wait()
    damping_table(wave_count, stiff_ref, wave_ref, first, damp)
    find_places(waves, places)
    own_in.wait()
    out_whole.wait_recv()

    home_rows = (groups - 1, 1)
    home_whole = [
        whole(source, target, back_send_sem.at[at], back_recv_sem.at[at], home_rows[at])
        for at, (source, target) in enumerate(((back_send, back_recv), (last_send, last_recv)))
    ]

    def send_home(at):
        source, target = ((back_send, back_recv), (last_send, last_recv))[at]
        for copy in copies(
            source,
            target,
            lambda pw, ph, pf, ih: ih * 2 * bands + pf * bands + pw,
            lambda pw, ph, pf, ih: owner,
            back_send_sem.at[at],
            back_recv_sem.at[at],
            home_rows[at],
        ):
            copy.start()
        slice_of(target, owner, home_rows[at])[...] = slice_of(
            source, f * bands + w, home_rows[at]
        )[...]

    lane_slot = iota((SUB, LANES), 1) // 16
    zero = jnp.zeros((SUB, LANES), F32)
    for g in range(groups):
        blocks = []
        for rel in range(hemis):
            base = rel * 2 * bands * SUB + g
            north = recv[pl.ds(base, bands, stride=SUB), :]
            south = recv[pl.ds(base + bands * SUB, bands, stride=SUB), :]
            even, odd = north + south, north - south
            for s in range(SUB):
                blocks.append(
                    jnp.concatenate([jnp.where(lane_slot == s, even, 0.0), zero], axis=1)
                )
                blocks.append(
                    jnp.concatenate([zero, jnp.where(lane_slot == s, odd, 0.0)], axis=1)
                )
        spaced = jnp.concatenate(blocks, axis=0).astype(BF16)
        swap[g].wait_recv()
        spectral = mxu(weights[g], spaced, TN)
        damped = (spectral * damp[g]).astype(BF16)
        full = mxu(weights[g], damped)
        for rel in range(hemis):
            sums = []
            for q in range(2):
                total = None
                for s in range(SUB):
                    at = rel * LANES + s * 16 + q * SUB
                    piece = full[at : at + SUB, q * LANES : (q + 1) * LANES]
                    total = piece if total is None else jnp.where(lane_slot == s, piece, total)
                sums.append(total)
            target, base = back_send, rel * 2 * bands * SUB + g
            if g == groups - 1:
                target, base = last_send, rel * 2 * bands * SUB
            target[pl.ds(base, bands, stride=SUB), :] = sums[0] + sums[1]
            target[pl.ds(base + bands * SUB, bands, stride=SUB), :] = sums[0] - sums[1]
        if g >= groups - 2:
            send_home(g - groups + 2)

    halves = []
    for at in range(2):
        home_whole[at].wait_recv()
        halves.append(
            home_part(
                (back_recv, last_recv)[at], (flip, other_flip)[at], places, home_rows[at],
                2 * (groups - 1) * at,
            )
        )
    left_lines(lon_ref[0], wave_count, halves, 2 * (groups - 1), places, left_ref)
    for copy in swap:
        copy.wait_send()
    out_whole.wait_send()
    for copy in home_whole:
        copy.wait_send()


def inverse_kernel(
    wave_count, lon_ref, left_ref, table_ref, smooth_ref, bracket_ref, acc, smooth_rows,
    bracket_rows, sem,
):
    fields, levels, _, lon_slots = smooth_ref.shape
    quarter = table_ref.shape[1]
    count, fourth, n_float = length_of(lon_ref)
    acc[...] = jnp.zeros_like(acc)
    fold_cos, fold_sin = fold_tables(n_float, quarter)
    sums = mxu(left_ref[...], table_ref[...])
    re = [sums[16 * r : 16 * r + 16] for r in range(4)]
    im = [None] + [sums[48 + 16 * r : 64 + 16 * r] for r in range(1, 4)]
    cos = [fold_cos[r : r + 1] for r in range(4)]
    sin = [fold_sin[r : r + 1] for r in range(4)]
    h0 = re[0]
    h1r, h1i = re[1] * cos[1] - im[1] * sin[1], re[1] * sin[1] + im[1] * cos[1]
    h2 = re[2] * cos[2] - im[2] * sin[2]
    h3r, h3i = re[3] * cos[3] - im[3] * sin[3], re[3] * sin[3] + im[3] * cos[3]
    even, odd, cross, turn = h0 + h2, h0 - h2, h1r + h3r, h3i - h1i
    live = iota((16, quarter), 1) < fourth
    scale = 1.0 / jnp.sqrt(n_float)
    width = quarter + LANES
    for a, value in enumerate((even + cross, odd + turn, even - cross, odd - turn)):
        value = jnp.where(live, value * scale, 0.0)
        smooth, slope = value[0:8], value[8:16]
        flipped = jnp.concatenate([slope[4:8], slope[0:4]], axis=0)
        product = smooth * flipped
        bracket = product - jnp.concatenate([product[4:8], product[0:4]], axis=0)
        segment = jnp.concatenate([smooth, bracket], axis=0)
        segment = jnp.concatenate([segment, jnp.zeros((16, LANES), F32)], axis=1)
        start = fourth * a
        segment = pltpu.roll(segment, lax.rem(start, LANES), 1)
        aligned = pl.multiple_of((start // LANES) * LANES, LANES)
        acc[:, pl.ds(aligned, width)] += segment
    for f in range(fields):
        for l in range(levels):
            smooth_rows[f, l] = acc[pl.ds(f * levels + l, 1), pl.ds(0, lon_slots)]
    smooth_out = pltpu.make_async_copy(smooth_rows, smooth_ref, sem.at[0])
    smooth_out.start()
    for l in range(levels):
        bracket_rows[l] = acc[pl.ds(8 + l, 1), pl.ds(0, lon_slots)]
    bracket_out = pltpu.make_async_copy(bracket_rows, bracket_ref, sem.at[1])
    bracket_out.start()
    smooth_out.wait()
    bracket_out.wait()


def in_hbm(x):
    return pltpu.with_memory_space_constraint(x, pltpu.HBM)


def fast_device(axes, grid, lon_count, wave_order, legendre, stiffness):
    bands, hemis, sides = axes
    owners = bands * hemis * sides
    wave_count = wave_order.shape[0]
    fields, levels, _, lon_slots = grid.shape
    groups = wave_count // owners // SUB
    k_count = legendre.shape[4]
    quarter = round_up(lon_slots // 4, LANES)
    waves4 = wave_count // 4
    long_rows = lon_slots + 2 * LANES
    smem = pl.BlockSpec(memory_space=pltpu.SMEM)
    vmem = pl.BlockSpec(memory_space=pltpu.VMEM)
    hbm = pl.BlockSpec(memory_space=pltpu.HBM)
    weights = legendre.reshape(hemis, groups, LANES, k_count)
    message = pltpu.VMEM((owners * SUB, LANES), F32)
    left, table = pl.pallas_call(
        functools.partial(middle_kernel, axes, wave_count),
        out_shape=(
            pltpu.VMEM((7 * 16, 2 * waves4), BF16),
            pltpu.VMEM((2 * waves4, quarter), BF16),
        ),
        in_specs=[smem, hbm, hbm, hbm, hbm],
        out_specs=(vmem, vmem),
        scratch_shapes=[
            pltpu.SMEM(stiffness.shape, F32),
            pltpu.SMEM(wave_order.shape, jnp.int32),
            pltpu.VMEM(wave_order.shape, jnp.int32),
            pltpu.VMEM((8, long_rows), F32),
            pltpu.VMEM((2 * waves4, quarter), BF16),
            pltpu.VMEM((LANES, LANES), F32),
            message,
            message,
            message,
            message,
            pltpu.VMEM((groups, 2 * LANES, k_count), BF16),
            pltpu.VMEM((groups, k_count, 2 * LANES), F32),
            pltpu.VMEM((6 * SUB, LANES), jnp.int32),
            pltpu.VMEM((LANES, LANES), F32),
            message,
            message,
            pltpu.SemaphoreType.DMA((1,)),
            pltpu.SemaphoreType.DMA((1,)),
            pltpu.SemaphoreType.DMA((2,)),
            pltpu.SemaphoreType.DMA((2,)),
            pltpu.SemaphoreType.DMA((1,)),
            pltpu.SemaphoreType.DMA((groups,)),
            pltpu.SemaphoreType.DMA((groups,)),
            pltpu.SemaphoreType.DMA((11,)),
            pltpu.SemaphoreType.REGULAR,
            pltpu.SemaphoreType.REGULAR,
        ],
        compiler_params=pltpu.CompilerParams(
            collective_id=0, has_side_effects=True, vmem_limit_bytes=24 << 20
        ),
        name="middle",
    )(lon_count, *[in_hbm(x) for x in (stiffness, wave_order, grid, weights)])
    return pl.pallas_call(
        functools.partial(inverse_kernel, wave_count),
        out_shape=(
            jax.ShapeDtypeStruct(grid.shape, F32),
            jax.ShapeDtypeStruct((levels, 1, lon_slots), F32),
        ),
        in_specs=[smem, vmem, vmem],
        out_specs=(hbm, hbm),
        scratch_shapes=[
            pltpu.VMEM((16, long_rows), F32),
            pltpu.VMEM(grid.shape, F32),
            pltpu.VMEM((levels, 1, lon_slots), F32),
            pltpu.SemaphoreType.DMA((2,)),
        ],
        compiler_params=pltpu.CompilerParams(vmem_limit_bytes=24 << 20),
        name="inverse",
    )(lon_count, left, table)


M = 768
FIELDS = 2
LEVELS = 4
K = 384


exact_mode = lax.Precision.HIGHEST


def general_device(grid, lon_count, wave_order, legendre, stiffness):
    lon_slots = grid.shape[3]
    rows_per = FIELDS * LEVELS
    channels = 2 * rows_per
    inner_width = 64
    wave_blocks = M // inner_width
    band_count = lax.axis_size("wave")
    slot_dev = M // (2 * band_count)
    cycle_length = lon_count[0]
    longitudes = jnp.arange(lon_slots, dtype=jnp.int32)
    wavenumbers = jnp.arange(M, dtype=jnp.int32)
    angle_step = 2.0 * jnp.pi / cycle_length.astype(jnp.float32)
    block_starts = jnp.arange(wave_blocks, dtype=jnp.int32) * inner_width
    inner_waves = jnp.arange(inner_width, dtype=jnp.int32)
    outer_angle = angle_step * (block_starts[:, None] * longitudes[None, :] % cycle_length).astype(
        jnp.float32
    )
    outer_cos = jnp.cos(outer_angle)
    outer_sin = jnp.sin(outer_angle)
    inner_angle = angle_step * (longitudes[:, None] * inner_waves[None, :] % cycle_length).astype(
        jnp.float32
    )
    inner_table = jnp.concatenate([jnp.cos(inner_angle), jnp.sin(inner_angle)], axis=1)
    cycle_scale = 1.0 / jnp.sqrt(cycle_length.astype(jnp.float32))
    live_points = longitudes < cycle_length
    wave_live = 2 * wavenumbers < cycle_length
    cycle_rows = jnp.where(live_points[None, :], grid[:, :, 0, :].reshape(rows_per, lon_slots), 0.0)
    modulated = jnp.stack(
        [cycle_rows[:, None, :] * outer_cos[None], -(cycle_rows[:, None, :] * outer_sin[None])]
    )
    product = jnp.dot(
        modulated.reshape(2 * rows_per * wave_blocks, lon_slots), inner_table, precision=exact_mode
    )
    product = product.reshape(2, rows_per, wave_blocks, 2 * inner_width)
    real_part = product[0, :, :, :inner_width] + product[1, :, :, inner_width:]
    imag_part = product[1, :, :, :inner_width] - product[0, :, :, inner_width:]
    fourier = jnp.stack([real_part, imag_part]).reshape(channels, M) * cycle_scale
    fourier = jnp.where(wave_live[None, :], fourier, 0.0)
    slotted = fourier[:, wave_order].reshape(channels, band_count, 2, slot_dev)
    side_index = lax.axis_index("fld")
    arrived = lax.all_to_all(
        lax.all_to_all(slotted[None, :, None], "wave", split_axis=3, concat_axis=2, tiled=True),
        "fld",
        split_axis=4,
        concat_axis=0,
        tiled=True,
    )
    stacked = arrived.reshape(2, channels, band_count, slot_dev)
    even_part = (stacked[0] + stacked[1]).astype(jnp.bfloat16)
    odd_part = (stacked[0] - stacked[1]).astype(jnp.bfloat16)
    parities = jnp.stack([even_part, odd_part])
    weights = legendre[:, 0]
    owner_index = lax.axis_index("wave") * 2 + side_index
    my_waves = lax.dynamic_slice_in_dim(wave_order, owner_index * slot_dev, slot_dev)
    degrees = (
        my_waves[:, None, None]
        + 2 * jnp.arange(K, dtype=jnp.int32)[None, None, :]
        + jnp.arange(2, dtype=jnp.int32)[None, :, None]
    )
    valid_degree = degrees < M
    spectral = jnp.einsum("aqwk,qcwa->aqck", weights, parities, preferred_element_type=jnp.float32)
    spectral = jnp.where(valid_degree[:, :, None, :], spectral, 0.0)
    chan_stiff = jnp.tile(jnp.repeat(stiffness, LEVELS), 2)
    degree_float = degrees.astype(jnp.float32)
    degree_ratio = degree_float * (degree_float + 1.0) / (M * (M - 1))
    summed = lax.psum(spectral, "hemi")
    damped = (
        summed / (1.0 + chan_stiff[None, None, :, None] * degree_ratio[:, :, None, :])
    ).astype(jnp.bfloat16)
    returned = jnp.einsum("aqwk,aqck->qcwa", weights, damped, preferred_element_type=jnp.float32)
    north_vals = returned[0] + returned[1]
    south_vals = returned[0] - returned[1]
    homebound = lax.all_to_all(
        lax.all_to_all(
            jnp.stack([north_vals, south_vals])[:, None, None],
            "wave",
            split_axis=4,
            concat_axis=2,
            tiled=True,
        ),
        "fld",
        split_axis=0,
        concat_axis=1,
        tiled=True,
    )
    homebound = homebound.reshape(2, band_count, channels, slot_dev)
    slot_values = jnp.transpose(homebound, (2, 1, 0, 3)).reshape(channels, M)
    spectra = jnp.zeros((channels, M), jnp.float32).at[:, wave_order].set(slot_values)
    weight_wave = jnp.where(wavenumbers == 0, 1.0, 2.0) * jnp.where(wave_live, cycle_scale, 0.0)
    real_coef = spectra[:rows_per] * weight_wave
    imag_coef = spectra[rows_per:] * weight_wave
    wave_ratio = wavenumbers.astype(jnp.float32) / M
    cos_coef = jnp.stack([real_coef, -(imag_coef * wave_ratio)]).reshape(
        2 * rows_per, wave_blocks, inner_width
    )
    sin_coef = jnp.stack([imag_coef, real_coef * wave_ratio]).reshape(
        2 * rows_per, wave_blocks, inner_width
    )
    left_rows = jnp.stack(
        [
            jnp.concatenate([cos_coef, -sin_coef], axis=2),
            jnp.concatenate([sin_coef, cos_coef], axis=2),
        ]
    )
    cycle_sums = lax.dot_general(
        left_rows.reshape(4 * rows_per * wave_blocks, 2 * inner_width),
        inner_table,
        (((1,), (1,)), ((), ())),
        precision=exact_mode,
    )
    cycle_sums = cycle_sums.reshape(2, 2 * rows_per, wave_blocks, lon_slots)
    values = jnp.sum(cycle_sums[0] * outer_cos[None] - cycle_sums[1] * outer_sin[None], axis=1)
    values = jnp.where(live_points[None, :], values, 0.0)
    smooth_rows = values[:rows_per].reshape(FIELDS, LEVELS, lon_slots)
    slope_rows = values[rows_per:].reshape(FIELDS, LEVELS, lon_slots)
    bracket = smooth_rows[0] * slope_rows[1] - smooth_rows[1] * slope_rows[0]
    return (smooth_rows[:, :, None, :], bracket[:, None, :])


def solution(mesh):
    axes = (mesh.shape["wave"], mesh.shape["hemi"], mesh.shape["fld"])
    bands, hemis, sides = axes
    placed = (
        P(None, None, ("wave", "hemi", "fld"), None),
        P(("wave", "hemi", "fld")),
        P(),
        P(("wave", "fld"), "hemi", None, None, None),
        P(),
    )
    fits = bands == 8 and hemis == 2 and sides == 2 and M == 24 * bands * hemis * sides
    step = functools.partial(fast_device, axes) if fits else general_device
    return jax.shard_map(
        step,
        mesh=mesh,
        in_specs=placed,
        out_specs=(
            P(None, None, ("wave", "hemi", "fld"), None),
            P(None, ("wave", "hemi", "fld"), None),
        ),
        check_vma=False,
    )
```
